512 devices in a mesh: rows: 64 (over y, x, core), vars: 8 (over z).
Axes of the slice: x: 4, y: 8, z: 8, core: 2. Of those that a mesh axis runs over, the one named last changes fastest.
Arguments:
- fields: bfloat16 [64, 262144], P('vars', 'rows'), may hold values from -6 to 6
- stencil: int32 [131072, 4], P('rows'), may hold values from 0 to 1023
- stencil_weight: float32 [131072, 4], P('rows'), may hold values from 0.1 to 1
- owner_map: int32 [8192, 1], P('rows'), may hold values from 0 to 63; in each aligned block of 128 rows (0 to 127, 128 to 255, ...) at most 4 rows name the same one
- embed_weight: bfloat16 [64, 16, 1024], P('vars'), may hold values from -1.5 to 1.5
- embed_bias: bfloat16 [64, 1024], P('vars'), may hold values from -3 to 3
- agg_query: float32 [16, 64], replicated, may hold values from -40 to 40
- out_grad: bfloat16 [16384, 1024], P('rows'), may hold values from -6 to 6
Outputs:
- tokens: bfloat16 [16384, 1024], P('rows', 'vars')
- field_grad: float32 [64, 262144], P('vars', 'rows')
- weight_grad: float32 [64, 16, 1024], P('vars')
- bias_grad: float32 [64, 1024], P('vars')
- query_grad: float32 [16, 64], replicated
The draws below stay inside these ranges and needn't reach their ends.
Inputs may be any that keep to these rules, and one draw needn't show every extreme that they name: `stencil`: the index of a point within the pixel's own block. `owner_map`: among the 128 patches of one device along rows, no owner is named more than 4 times, a bound that some block reaches.
All inputs are finite; a program needn't handle non-finite values.
Results may differ from the reference program's by a relative error of at most 0.0055.
The reference program's roundings to bfloat16 on the way (of `matrix`, `pixels`, `embedded`, `grad_low` and `grad_pixels`) count: a program that leaves them out, or rounds other values in their place, can miss the bound.
Values may be sent and summed in bfloat16 or wider, within the bound.
No kernel may reach another device: no remote copies, remote signals or barrier semaphores. Data moves between devices by JAX's collectives and lax.ppermute only.
A program may use at most 128 MiB of HBM per device.

```python
import math
import jax
import jax.numpy as jnp
import numpy as np
from jax import lax

D = 1024
H = 16
DH = 64
P_SIZE = 16
K = 4
NVAR = 64
PTS_BLK = 1024
PB = 32
BLOCKS = 4
PIX_BLK = 512
SRC = 128
MOST = 4
CAPR = 256
PATCHES = 8192
SLOTS = 16384
PIXELS = 131072
POINTS = 262144
N_ROWS = 64


def draw_agg_query(key, part):
    base = jax.random.normal(jax.random.fold_in(key, 11), (H, DH), jnp.float32)
    return jnp.clip(base, -4.5, 4.5)


def touch_ends(values, key, smallest, high):
    longest = values.shape.index(max(values.shape))
    spots = []
    for shift in (0, 1):
        where = [jax.random.randint(jax.random.fold_in(key, axis), (), 0, length) for axis, length in enumerate(values.shape)]
        where[longest] = (where[longest] + shift) % values.shape[longest]
        spots.append(tuple(where))
    return values.at[spots[0]].set(smallest).at[spots[1]].set(high)


def block_levels(stream_key, dims, split, low, top_value):
    loudness = 1.0
    for axis_at, blocks in split:
        heights = jax.random.uniform(jax.random.fold_in(jax.random.fold_in(stream_key, 6), axis_at), (blocks,), jnp.float32, low / len(split), top_value / len(split))
        loudness = loudness * jnp.repeat(jnp.exp(heights), dims[axis_at] // blocks).reshape((-1,) + (1,) * (len(dims) - 1 - axis_at))
    return loudness


def shared_out(rng, own, number, rows, count, top, limit, lean):
    ranking = jax.random.permutation(rng, count)
    packed, usual = portions_of(count, rows * top, limit, lean, True), portions_of(count, rows * top, limit, lean, False)
    places = jnp.arange(count)

    def named(sizes, turn):
        used = int((sizes > 0).sum())
        fixed = max(1, used // 4)
        shifted = fixed + (places - fixed + turn * (used - fixed)) % max(1, count - fixed)
        return jnp.zeros((count,), jnp.int32).at[ranking[jnp.where(places < fixed, places, shifted)]].set(jnp.asarray(sizes, jnp.int32))

    sizes = jnp.where(number % 4 == 0, named(packed, number // 4), named(usual, number - number // 4 - 1))
    mixed = jax.random.permutation(jax.random.fold_in(own, 3), count)
    donor, sink = mixed[0:count // 2 * 2:2], mixed[1:count // 2 * 2:2]
    slack = jnp.minimum(sizes[donor] - 1, limit - sizes[sink]) // 2
    slack = jnp.where((donor == ranking[0]) | (sink == ranking[0]) | (sizes[sink] == 0), 0, jnp.maximum(slack, 0))
    shifted = jax.random.randint(jax.random.fold_in(own, 4), (count // 2,), 0, 1 << 20) % (slack + 1)
    sizes = sizes.at[donor].add(-shifted).at[sink].add(shifted)
    labels = jnp.searchsorted(jnp.cumsum(sizes), jnp.arange(rows * top), side="right").astype(jnp.int32)
    listing = labels.reshape(top, rows).T
    listing = listing[jax.random.permutation(jax.random.fold_in(own, 1), rows)]
    turn = jax.random.randint(jax.random.fold_in(own, 2), (rows, 1), 0, top)
    return jnp.take_along_axis(listing, (jnp.arange(top)[None, :] + turn) % top, axis=1)


def portions_of(count, total, reach, skew, full):
    loads = [(1 << 20) // math.isqrt(grade ** skew) + 1 for grade in range(1, count + 1)]
    largest = reach if full else min(reach, max(-(-total // count), total * loads[0] // sum(loads)))
    least = 1 if total - largest >= count - 1 else 0
    given, surplus = [largest] + [least] * (count - 1), total - largest - least * (count - 1)
    while surplus > 0:
        free = [i for i in range(1, count) if given[i] < largest] or [i for i in range(1, count) if given[i] < reach]
        mass, left = sum([loads[i] for i in free]), surplus
        for i in free:
            addition = min(reach - given[i], max(1, left * loads[i] // mass), surplus)
            given[i] = given[i] + addition
            surplus = surplus - addition
    return np.array(given)


def noise(rng, extent, deviation, reach, shards=(), kind=jnp.bfloat16):
    level = block_levels(rng, extent, shards, -0.22, 0.18) if shards else 1.0
    values = jax.random.normal(rng, extent, jnp.float32) * deviation * level
    return jnp.minimum(jnp.maximum(values, -reach), reach).astype(kind)


def setup_inputs(seed: int = 0) -> dict:
    arg_keys = jax.random.split(jax.random.key(seed), 9)
    fields = noise(arg_keys[0], (NVAR, POINTS), 1.0, 6.0, ((0, 8), (1, 64)))
    stencil = touch_ends(jax.random.randint(arg_keys[1], (PIXELS, K), 0, PTS_BLK), jax.random.fold_in(arg_keys[1], 1), 0, PTS_BLK - 1).astype(jnp.int32)
    stencil_weight = jnp.clip(0.1 + 0.9 * jax.random.uniform(arg_keys[2], (PIXELS, K), jnp.float32) ** block_levels(arg_keys[2], (PIXELS, K), ((0, 64),), -0.2, 0.2), 0.1, 1.0)
    owner_map_keys = jax.random.split(jax.random.fold_in(arg_keys[3], 1), PATCHES // SRC)
    owner_map_turns = jax.random.permutation(jax.random.fold_in(arg_keys[3], 3), PATCHES // SRC)
    owner_map = jax.vmap(lambda own, number: shared_out(jax.random.fold_in(arg_keys[3], 2), own, number, SRC, N_ROWS, 1, MOST, 2))(owner_map_keys, owner_map_turns).reshape((PATCHES, 1))
    embed_weight = noise(arg_keys[4], (NVAR, P_SIZE, D), P_SIZE ** -0.5, 1.5, ((0, 8),))
    embed_bias = noise(arg_keys[5], (NVAR, D), 0.5, 3.0, ((0, 8),))
    agg_query = draw_agg_query(jax.random.fold_in(arg_keys[8], 71), 0)
    out_grad = noise(arg_keys[7], (SLOTS, D), 1.0, 6.0, ((0, 64),))
    return dict(fields=fields, stencil=stencil, stencil_weight=stencil_weight, owner_map=owner_map, embed_weight=embed_weight, embed_bias=embed_bias, agg_query=agg_query, out_grad=out_grad)


def interp_matrix(index_rows, weight_rows):
    columns = jnp.arange(PTS_BLK, dtype=jnp.int32)
    summed = jnp.zeros((index_rows.shape[0], PTS_BLK), jnp.float32)
    for entry in range(K):
        summed = summed + jnp.where(index_rows[:, entry:entry + 1] == columns[None, :], weight_rows[:, entry:entry + 1], 0.0)
    return summed.astype(jnp.bfloat16)

def reference(fields, stencil, stencil_weight, owner_map, embed_weight, embed_bias, agg_query, out_grad):
    high = lax.Precision.HIGHEST
    block_total = BLOCKS * N_ROWS
    field_blocks = fields.reshape(NVAR, block_total, PTS_BLK).transpose(1, 0, 2)
    index_blocks = stencil.reshape(block_total, PIX_BLK, K)
    weight_blocks = stencil_weight.reshape(block_total, PIX_BLK, K)

    def forward_block(pieces):
        field_block, index_rows, weight_rows = pieces
        matrix = interp_matrix(index_rows, weight_rows)
        return jnp.dot(field_block, matrix.T, preferred_element_type=jnp.float32).astype(jnp.bfloat16)
    pixels = lax.map(forward_block, (field_blocks, index_blocks, weight_blocks))
    pixels = pixels.reshape(N_ROWS, BLOCKS, NVAR, PB, P_SIZE).transpose(0, 1, 3, 2, 4).reshape(N_ROWS, SRC, NVAR, P_SIZE)
    routes = owner_map.reshape(N_ROWS, SRC)
    onehot = (routes[:, :, None] == jnp.arange(N_ROWS, dtype=jnp.int32)[None, None, :]).astype(jnp.int32)
    order_rank = lax.optimization_barrier(jnp.sum(onehot * (jnp.cumsum(onehot, axis=1) - 1), axis=2))
    slots = routes * CAPR + jnp.arange(N_ROWS, dtype=jnp.int32)[:, None] * MOST + order_rank
    slots = slots.astype(jnp.int32)
    upstream_all = out_grad[slots.reshape(-1)].reshape(N_ROWS, SRC, D)
    score_scale = 1.0 / math.sqrt(DH)
    query_f = agg_query.astype(jnp.float32)
    weight_f = embed_weight.astype(jnp.float32)
    bias_f = embed_bias.astype(jnp.float32)

    def owner_step(running, pieces):
        weight_acc, bias_acc, query_acc = running
        pix_rows, grad_rows = pieces
        embedded = (jnp.einsum('svp,vpd->svd', pix_rows.astype(jnp.float32), weight_f, precision=high) + bias_f[None]).astype(jnp.bfloat16)
        head_view = embedded.astype(jnp.float32).reshape(SRC, NVAR, H, DH)
        scores = jnp.einsum('svhe,he->shv', head_view, query_f, precision=high) * score_scale
        attention = jax.nn.softmax(scores, axis=2)
        mixture = jnp.einsum('shv,svhe->she', attention, head_view, precision=high)
        token_rows = mixture.reshape(SRC, D).astype(jnp.bfloat16)
        upstream = grad_rows.astype(jnp.float32).reshape(SRC, H, DH)
        inner_out = lax.optimization_barrier(jnp.sum(upstream * mixture, axis=2))
        grad_attn = jnp.einsum('she,svhe->shv', upstream, head_view, precision=high)
        grad_score = attention * (grad_attn - inner_out[:, :, None])
        grad_embed = jnp.einsum('shv,she->svhe', attention, upstream, precision=high) + jnp.einsum('shv,he->svhe', grad_score, query_f, precision=high) * score_scale
        grad_embed = grad_embed.reshape(SRC, NVAR, D)
        grad_low = grad_embed.astype(jnp.bfloat16)
        weight_acc = weight_acc + jnp.einsum('svp,svd->vpd', pix_rows.astype(jnp.float32), grad_low.astype(jnp.float32), precision=high)
        bias_acc = bias_acc + lax.optimization_barrier(jnp.sum(grad_embed, axis=0))
        query_acc = query_acc + jnp.einsum('shv,svhe->he', grad_score, head_view, precision=high) * score_scale
        grad_pixels = jnp.einsum('svd,vpd->svp', grad_low.astype(jnp.float32), weight_f, precision=high).astype(jnp.bfloat16)
        return ((weight_acc, bias_acc, query_acc), (token_rows, grad_pixels))
    start_sums = (jnp.zeros((NVAR, P_SIZE, D), jnp.float32), jnp.zeros((NVAR, D), jnp.float32), jnp.zeros((H, DH), jnp.float32))
    sums_final, outputs = lax.scan(owner_step, start_sums, (pixels, upstream_all))
    weight_grad, bias_grad, query_grad = sums_final
    token_rows, grad_pixels = outputs
    tokens = jnp.zeros((SLOTS, D), jnp.bfloat16).at[slots.reshape(-1)].set(token_rows.reshape(PATCHES, D))
    grad_blocks = grad_pixels.reshape(N_ROWS, BLOCKS, PB, NVAR, P_SIZE).transpose(0, 1, 3, 2, 4).reshape(block_total, NVAR, PIX_BLK)

    def backward_block(pieces):
        grad_block, index_rows, weight_rows = pieces
        matrix = interp_matrix(index_rows, weight_rows)
        return jnp.dot(grad_block, matrix, preferred_element_type=jnp.float32)
    field_blocks_grad = lax.map(backward_block, (grad_blocks, index_blocks, weight_blocks))
    field_grad = field_blocks_grad.transpose(1, 0, 2).reshape(NVAR, POINTS)
    return (tokens, field_grad, weight_grad, bias_grad, query_grad)
```

```python
import math

import jax
import jax.numpy as jnp
from jax import lax
from jax.experimental import pallas as pl
from jax.experimental.pallas import tpu as pltpu
from jax.sharding import Mesh
from jax.sharding import PartitionSpec as P

D = 1024
H = 16
DH = 64
P_SIZE = 16
K = 4
PTS_BLK = 1024
PB = 32
PIX_BLK = PB * P_SIZE
LANES = 128
TILES = D // LANES
CHUNK = 24
INTERPRET = False

f32 = jnp.float32
bf16 = jnp.bfloat16


def iota(shape, axis):
    return lax.broadcasted_iota(jnp.int32, shape, axis)


def dot(first, second):
    return lax.dot_general(first, second, (((1,), (0,)), ((), ())), preferred_element_type=f32)


def dot_t(first, second):
    return lax.dot_general(first, second, (((1,), (1,)), ((), ())), preferred_element_type=f32)


def split(value, parts):
    pieces = []
    for _ in range(parts):
        piece = value.astype(bf16)
        pieces.append(piece)
        value = value - piece.astype(f32)
    return pieces


def kernel_call(body, out_shape, scratch=(), in_specs=None, out_specs=None, aliases=None):
    extra = {}
    if in_specs is not None:
        extra["in_specs"] = in_specs
    if out_specs is not None:
        extra["out_specs"] = out_specs
    return pl.pallas_call(
        body,
        out_shape=out_shape,
        scratch_shapes=list(scratch),
        input_output_aliases=aliases or {},
        interpret=INTERPRET,
        compiler_params=pltpu.CompilerParams(vmem_limit_bytes=50 << 20),
        **extra,
    )


def interp_transposed(index_ref, weight_ref, block):
    where = pl.ds(block * PIX_BLK, PIX_BLK)
    index = [index_ref[k : k + 1, where] for k in range(K)]
    weight = [weight_ref[k : k + 1, where] for k in range(K)]
    points = iota((PTS_BLK, PIX_BLK), 0)
    matrix = jnp.zeros((PTS_BLK, PIX_BLK), f32)
    for k in range(K):
        total = jnp.zeros((1, PIX_BLK), f32)
        for j in range(K):
            total = total + jnp.where(index[j] == index[k], weight[j], 0.0)
        matrix = jnp.where(points == index[k], total, matrix)
    return matrix.astype(bf16)


def spread(rows, cols, test):
    return jnp.where(test(iota((rows, cols), 0), iota((rows, cols), 1)), 1.0, 0.0).astype(bf16)


def pixel_masks(var_local):
    wide = var_local * P_SIZE
    copy_rows = spread(wide, var_local, lambda r, c: r // P_SIZE == c)
    own_pixel = iota((wide, PIX_BLK), 0) % P_SIZE == iota((wide, PIX_BLK), 1) % P_SIZE
    return copy_rows, own_pixel


def head_expand(copies):
    return spread(copies * H, D, lambda r, c: r % H == c // DH)


def forward_kernel(
    index_ref, weight_ref, fields_ref, embed_ref, bias_ref, query_ref, x_ref, e_ref, s_ref, exch_ref, sum_ref
):
    var_local = fields_ref.shape[0]
    blocks = fields_ref.shape[1] // PTS_BLK
    wide = var_local * P_SIZE
    copy_rows, own_pixel = pixel_masks(var_local)
    gather = spread(PB, PIX_BLK, lambda r, c: r == c // P_SIZE)
    for block in range(blocks):
        matrix = interp_transposed(index_ref, weight_ref, block)
        pixels = dot(fields_ref[:, pl.ds(block * PTS_BLK, PTS_BLK)], matrix).astype(bf16)
        widened = jnp.where(own_pixel, dot(copy_rows, pixels), 0.0).astype(bf16)
        x_ref[pl.ds(block * PB, PB), :] = dot_t(gather, widened).astype(bf16)
    x_all = x_ref[...]
    patches = x_all.shape[0]
    var_of = iota((patches, wide), 1) // P_SIZE
    head_rows = iota((3 * H, D), 0) % H == iota((3 * H, D), 1) // DH
    parts = split(query_ref[...], 3)
    query_rows = jnp.concatenate(
        [jnp.broadcast_to(part.astype(f32), (H, D)) for part in parts], axis=0
    )
    query_rows = jnp.where(head_rows, query_rows, 0.0).astype(bf16)
    peak = None
    scores = []
    for v in range(var_local):
        own = jnp.where(var_of == v, x_all, jnp.zeros_like(x_all))
        embedded = (dot(own, embed_ref[...]) + bias_ref[v : v + 1, :].astype(f32)).astype(bf16)
        e_ref[v] = embedded
        three = dot_t(embedded, query_rows)
        score = (three[:, :H] + three[:, H : 2 * H] + three[:, 2 * H :]) * (1.0 / math.sqrt(DH))
        s_ref[v] = score
        scores.append(score)
        peak = score if peak is None else jnp.maximum(peak, score)
    expand = head_expand(2)
    total = None
    for v in range(var_local):
        weights = jnp.exp(scores[v] - peak)
        total = weights if total is None else total + weights
        both = jnp.concatenate(split(weights, 2), axis=1)
        term = dot(both, expand) * e_ref[v].astype(f32)
        if v == 0:
            sum_ref[...] = term
        else:
            sum_ref[...] += term
    groups = exch_ref.shape[0]
    width = D // groups
    for g in range(groups):
        exch_ref[g] = sum_ref[:, g * width : (g + 1) * width]


def target_of(column_ref, row_ref, depth, as_row):
    column = column_ref[...]
    row = row_ref[...]
    count = column.shape[0]
    same = column == row
    first, second = iota((count, count), 0), iota((count, count), 1)
    if as_row:
        rank = jnp.sum(jnp.where(same & (first < second), 1.0, 0.0), axis=0, keepdims=True)
        return row * depth + rank.astype(jnp.int32)
    rank = jnp.sum(jnp.where(same & (second < first), 1.0, 0.0), axis=1, keepdims=True)
    return column * depth + rank.astype(jnp.int32)


def stats_kernel(depth, column_ref, row_ref, inbox_ref, e_ref, s_ref, up_ref, ga_ref, stats_ref):
    patches = column_ref.shape[0]
    slots = inbox_ref.shape[0]
    target = target_of(column_ref, row_ref, depth, False)
    pick = jnp.where(iota((patches, slots), 1) == target, 1.0, 0.0).astype(bf16)
    upstream = dot(pick, inbox_ref[...])
    up_ref[...] = upstream.astype(bf16)
    reduce_heads = spread(D, H, lambda r, c: r // DH == c)
    var_local = e_ref.shape[0]
    peak = s_ref[0]
    for v in range(1, var_local):
        peak = jnp.maximum(peak, s_ref[v])
    total = jnp.zeros_like(peak)
    inner = jnp.zeros_like(peak)
    for v in range(var_local):
        high, low = split(upstream * e_ref[v].astype(f32), 2)
        grad_attn = dot(high, reduce_heads) + dot(low, reduce_heads)
        ga_ref[v] = grad_attn
        weights = jnp.exp(s_ref[v] - peak)
        total = total + weights
        inner = inner + weights * grad_attn
    packed = jnp.concatenate([peak, total, inner, jnp.zeros((patches, LANES - 3 * H), f32)], axis=1)
    if patches < LANES:
        packed = jnp.concatenate([packed, jnp.zeros((LANES - patches, LANES), f32)], axis=0)
    stats_ref[...] = packed.T[: 3 * H, :]


def combine_stats(stats_ref, patches):
    groups = stats_ref.shape[0]
    peaks, totals, inners = [], [], []
    for g in range(groups):
        rows = jnp.concatenate([stats_ref[g], jnp.zeros((LANES - 3 * H, LANES), f32)], axis=0).T
        rows = rows[:patches]
        peaks.append(rows[:, :H])
        totals.append(rows[:, H : 2 * H])
        inners.append(rows[:, 2 * H : 3 * H])
    peak = peaks[0]
    for other in peaks[1:]:
        peak = jnp.maximum(peak, other)
    factors = [jnp.exp(one - peak) for one in peaks]
    total = sum(f * t for f, t in zip(factors, totals))
    inner = sum(f * t for f, t in zip(factors, inners)) / total
    return peak, total, inner, factors


def tokens_kernel(depth, slots, place_ref, column_ref, row_ref, stats_ref, sums_ref, out_ref):
    patches = column_ref.shape[0]
    groups, _, width = sums_ref.shape
    _, total, _, factors = combine_stats(stats_ref, patches)
    heads = width // DH
    first = place_ref[0] * heads
    pick = jnp.where(
        iota((3 * H, width), 0) % H == first + iota((3 * H, width), 1) // DH, 1.0, 0.0
    ).astype(bf16)
    mixture = jnp.zeros((patches, width), f32)
    for g in range(groups):
        scale = jnp.concatenate(split(factors[g] / total, 3), axis=1)
        mixture = mixture + dot(scale, pick) * sums_ref[g]
    target = target_of(column_ref, row_ref, depth, True)
    place = jnp.where(iota((slots, patches), 0) == target, 1.0, 0.0).astype(bf16)
    out_ref[...] = dot(place, mixture.astype(bf16)).astype(bf16)


def backward_kernel(
    stats_ref, s_ref, ga_ref, up_ref, e_ref, x_ref, embed_ref, query_ref, wide_ref, gx_ref
):
    var_local, patches = e_ref.shape[0], e_ref.shape[1]
    wide = var_local * P_SIZE
    peak, total, inner, _ = combine_stats(stats_ref, patches)
    inverse = 1.0 / total
    expand = head_expand(2)
    query = query_ref[...]
    q_parts = split(query, 3)
    rows = [q_parts[0], q_parts[1], q_parts[2], q_parts[0], q_parts[1], q_parts[2]]
    query_rows = jnp.concatenate([jnp.broadcast_to(r.astype(f32), (H, D)) for r in rows], axis=0)
    on_head = iota((6 * H, D), 0) % H == iota((6 * H, D), 1) // DH
    query_rows = jnp.where(on_head, query_rows, 0.0).astype(bf16)
    upstream = up_ref[...].astype(f32)
    x_t = x_ref[...].astype(f32).T.astype(bf16)
    embed_t = embed_ref[...].astype(f32).T.astype(bf16)
    lane_var = iota((patches, wide), 1) // P_SIZE
    grad_x = jnp.zeros((patches, wide), f32)
    query_sum = jnp.zeros((2 * H, D), f32)
    for v in range(var_local):
        attention = jnp.exp(s_ref[v] - peak) * inverse
        grad_score = attention * (ga_ref[v] - inner) * (1.0 / math.sqrt(DH))
        attn = jnp.concatenate(split(attention, 2), axis=1)
        high, low = split(grad_score, 2)
        scored = jnp.concatenate([high, high, high, low, low, low], axis=1)
        grad = dot(attn, expand) * upstream + dot(scored, query_rows)
        low_grad = grad.astype(bf16)
        bias_row = jnp.sum(grad, axis=0, keepdims=True)
        weight_rows = dot(x_t[v * P_SIZE : (v + 1) * P_SIZE, :], low_grad)
        for t in range(TILES):
            cut = slice(t * LANES, (t + 1) * LANES)
            wide_ref[v * TILES + t, :P_SIZE, :] = weight_rows[:, cut]
            wide_ref[v * TILES + t, P_SIZE : P_SIZE + 1, :] = bias_row[:, cut]
        grad_x = jnp.where(lane_var == v, dot(low_grad, embed_t), grad_x)
        pair = jnp.concatenate([high.astype(f32), low.astype(f32)], axis=1)
        pair = jnp.concatenate([pair, jnp.zeros((patches, LANES - 2 * H), f32)], axis=1)
        query_sum = query_sum + dot(pair.T[: 2 * H, :].astype(bf16), e_ref[v])
    gx_ref[...] = grad_x.astype(bf16)
    diagonal = iota((2 * H, D), 0) % H == iota((2 * H, D), 1) // DH
    query_row = jnp.sum(jnp.where(diagonal, query_sum, 0.0), axis=0, keepdims=True)
    chunks = wide_ref.shape[0]
    share = D // chunks
    for j in range(chunks):
        t, at = (j * share) // LANES, (j * share) % LANES
        row = query_row[:, t * LANES : (t + 1) * LANES]
        wide_ref[j, P_SIZE + 1 : P_SIZE + 2, :] = row
        wide_ref[j, P_SIZE + 2 :, :] = jnp.zeros((CHUNK - P_SIZE - 2, LANES), f32)


def field_kernel(index_ref, weight_ref, gx_ref, out_ref):
    wide = gx_ref.shape[1]
    var_local = wide // P_SIZE
    blocks = gx_ref.shape[0] // PB
    gx_t = gx_ref[...].astype(f32).T.astype(bf16)
    fold = spread(var_local, wide, lambda r, c: c // P_SIZE == r)
    own_pixel = iota((wide, PIX_BLK), 0) % P_SIZE == iota((wide, PIX_BLK), 1) % P_SIZE
    copy = spread(PB, PIX_BLK, lambda r, c: r == c // P_SIZE)
    for block in range(blocks):
        wide_grad = dot(gx_t[:, block * PB : (block + 1) * PB], copy)
        wide_grad = jnp.where(own_pixel, wide_grad, 0.0).astype(bf16)
        grad = dot(fold, wide_grad).astype(bf16)
        matrix = interp_transposed(index_ref, weight_ref, block)
        out_ref[:, pl.ds(block * PTS_BLK, PTS_BLK)] = dot_t(grad, matrix)


def local(
    fields, stencil, stencil_weight, owner_map, embed_weight, embed_bias, agg_query, out_grad
):
    rows = ("r", "c")
    ring = lax.axis_size("r")
    groups = lax.axis_size("z")
    row_devices = ring * 2
    var_local = fields.shape[0]
    patches = owner_map.shape[0]
    capacity = out_grad.shape[0]
    depth = capacity // row_devices
    width = D // groups
    wide = var_local * P_SIZE
    shape = jax.ShapeDtypeStruct

    inbox = lax.all_to_all(
        out_grad.reshape(row_devices, depth, D), rows, split_axis=0, concat_axis=0, tiled=True
    ).reshape(capacity, D)

    index_t = stencil.T
    weight_t = stencil_weight.T
    embed_flat = embed_weight.reshape(wide, D)
    query = agg_query.reshape(1, D)
    row_map = owner_map.reshape(1, patches)
    x_all, embedded, scores, sums = kernel_call(
        forward_kernel,
        (
            shape((patches, wide), bf16),
            shape((var_local, patches, D), bf16),
            shape((var_local, patches, H), f32),
            shape((groups, patches, width), f32),
        ),
        scratch=[pltpu.VMEM((patches, D), f32)],
    )(index_t, weight_t, fields, embed_flat, embed_bias, query)

    upstream, grad_attn, stats = kernel_call(
        lambda *refs: stats_kernel(depth, *refs),
        (
            shape((patches, D), bf16),
            shape((var_local, patches, H), f32),
            shape((3 * H, LANES), f32),
        ),
    )(owner_map, row_map, inbox, embedded, scores)

    all_stats = lax.all_to_all(
        jnp.broadcast_to(stats[None], (groups, 3 * H, LANES)), "z", 0, 0, tiled=True
    )
    all_sums = lax.all_to_all(sums, "z", 0, 0, tiled=True)

    place = lax.axis_index("z").astype(jnp.int32).reshape(1)
    outbox = kernel_call(
        lambda *refs: tokens_kernel(depth, capacity, *refs),
        shape((capacity, width), bf16),
        in_specs=[pl.BlockSpec(memory_space=pltpu.SMEM)] + [pl.BlockSpec(memory_space=pltpu.VMEM)] * 4,
    )(place, owner_map, row_map, all_stats, all_sums)
    tokens = lax.all_to_all(
        outbox.reshape(row_devices, depth, width), rows, 0, 0, tiled=True
    ).reshape(capacity, width)

    chunks = row_devices if row_devices == var_local * TILES else var_local * TILES
    partial, grad_x = kernel_call(
        backward_kernel,
        (
            shape((chunks, CHUNK, LANES), f32),
            shape((patches, wide), bf16),
        ),
    )(all_stats, scores, grad_attn, upstream, embedded, x_all, embed_flat, query)

    field_grad = kernel_call(field_kernel, shape((var_local, blocks_of(fields)), f32))(
        index_t, weight_t, grad_x
    )

    halves = lax.all_to_all(
        partial.reshape(2, chunks // 2, CHUNK, LANES), "c", 0, 0, tiled=True
    )
    mine = lax.all_to_all(halves[0] + halves[1], "r", 0, 0, tiled=True)
    own = jnp.sum(mine.reshape(ring, chunks // (2 * ring), CHUNK, LANES), axis=0)
    spread_out = jnp.broadcast_to(own[None], (ring,) + own.shape).reshape(mine.shape)
    half = lax.all_to_all(spread_out, "r", 0, 0, tiled=True)
    other = lax.ppermute(half, "c", [(0, 1), (1, 0)])
    core = lax.axis_index("c")
    whole = jnp.where(
        core == 0, jnp.stack([half, other]), jnp.stack([other, half])
    ).reshape(var_local, TILES, CHUNK, LANES)
    weight_grad = whole[:, :, :P_SIZE, :].transpose(0, 2, 1, 3).reshape(var_local, P_SIZE, D)
    bias_grad = whole[:, :, P_SIZE, :].reshape(var_local, D)
    share = D // chunks
    per_tile = LANES // share
    query_rows = whole.reshape(TILES, per_tile, CHUNK, LANES)[:, :, P_SIZE + 1, :]
    query_sum = query_rows[:, 0, :]
    query_all = lax.all_to_all(
        jnp.broadcast_to(query_sum[None], (groups, TILES, LANES)), "z", 0, 0, tiled=True
    )
    query_grad = jnp.sum(query_all, axis=0).reshape(H, DH)
    return (tokens, field_grad, weight_grad, bias_grad, query_grad)


def blocks_of(fields):
    return fields.shape[1]


def solution(mesh):
    rows, groups = mesh.shape["rows"], mesh.shape["vars"]
    inner = Mesh(mesh.devices.reshape(rows // 2, 2, groups), ("r", "c", "z"))
    by_rows = ("r", "c")
    return jax.shard_map(
        local,
        mesh=inner,
        in_specs=(
            P("z", by_rows),
            P(by_rows, None),
            P(by_rows, None),
            P(by_rows, None),
            P("z", None, None),
            P("z", None),
            P(),
            P(by_rows, None),
        ),
        out_specs=(
            P(by_rows, "z"),
            P("z", by_rows),
            P("z", None, None),
            P("z", None),
            P(),
        ),
        check_vma=False,
    )
```

```python
import math

import jax
import jax.numpy as jnp
from jax import lax
from jax.experimental import pallas as pl
from jax.experimental.pallas import tpu as pltpu
from jax.sharding import Mesh
from jax.sharding import PartitionSpec as P

D = 1024
H = 16
DH = 64
P_SIZE = 16
K = 4
PTS_BLK = 1024
PB = 32
PIX_BLK = PB * P_SIZE
LANES = 128
TILES = D // LANES
CHUNK = 24
INTERPRET = False

f32 = jnp.float32
bf16 = jnp.bfloat16


def iota(shape, axis):
    return lax.broadcasted_iota(jnp.int32, shape, axis)


def dot(first, second):
    return lax.dot_general(first, second, (((1,), (0,)), ((), ())), preferred_element_type=f32)


def dot_t(first, second):
    return lax.dot_general(first, second, (((1,), (1,)), ((), ())), preferred_element_type=f32)


def split(value, parts):
    pieces = []
    for _ in range(parts):
        piece = value.astype(bf16)
        pieces.append(piece)
        value = value - piece.astype(f32)
    return pieces


def kernel_call(body, out_shape, scratch=(), in_specs=None, out_specs=None, aliases=None):
    extra = {}
    if in_specs is not None:
        extra["in_specs"] = in_specs
    if out_specs is not None:
        extra["out_specs"] = out_specs
    return pl.pallas_call(
        body,
        out_shape=out_shape,
        scratch_shapes=list(scratch),
        input_output_aliases=aliases or {},
        interpret=INTERPRET,
        compiler_params=pltpu.CompilerParams(vmem_limit_bytes=50 << 20),
        **extra,
    )


def interp_transposed(index_ref, weight_ref, block):
    where = pl.ds(block * PIX_BLK, PIX_BLK)
    index = [index_ref[k : k + 1, where] for k in range(K)]
    weight = [weight_ref[k : k + 1, where] for k in range(K)]
    points = iota((PTS_BLK, PIX_BLK), 0)
    matrix = jnp.zeros((PTS_BLK, PIX_BLK), f32)
    for k in range(K):
        total = jnp.zeros((1, PIX_BLK), f32)
        for j in range(K):
            total = total + jnp.where(index[j] == index[k], weight[j], 0.0)
        matrix = jnp.where(points == index[k], total, matrix)
    return matrix.astype(bf16)


def spread(rows, cols, test):
    return jnp.where(test(iota((rows, cols), 0), iota((rows, cols), 1)), 1.0, 0.0).astype(bf16)


def pixel_masks(var_local):
    wide = var_local * P_SIZE
    copy_rows = spread(wide, var_local, lambda r, c: r // P_SIZE == c)
    own_pixel = iota((wide, PIX_BLK), 0) % P_SIZE == iota((wide, PIX_BLK), 1) % P_SIZE
    return copy_rows, own_pixel


def head_expand(copies):
    return spread(copies * H, D, lambda r, c: r % H == c // DH)


def forward_kernel(
    index_ref, weight_ref, fields_ref, embed_ref, bias_ref, query_ref, x_ref, e_ref, s_ref, exch_ref, sum_ref
):
    var_local = fields_ref.shape[0]
    blocks = fields_ref.shape[1] // PTS_BLK
    wide = var_local * P_SIZE
    copy_rows, own_pixel = pixel_masks(var_local)
    gather = spread(PB, PIX_BLK, lambda r, c: r == c // P_SIZE)
    for block in range(blocks):
        matrix = interp_transposed(index_ref, weight_ref, block)
        pixels = dot(fields_ref[:, pl.ds(block * PTS_BLK, PTS_BLK)], matrix).astype(bf16)
        widened = jnp.where(own_pixel, dot(copy_rows, pixels), 0.0).astype(bf16)
        x_ref[pl.ds(block * PB, PB), :] = dot_t(gather, widened).astype(bf16)
    x_all = x_ref[...]
    patches = x_all.shape[0]
    var_of = iota((patches, wide), 1) // P_SIZE
    head_rows = iota((3 * H, D), 0) % H == iota((3 * H, D), 1) // DH
    parts = split(query_ref[...], 3)
    query_rows = jnp.concatenate(
        [jnp.broadcast_to(part.astype(f32), (H, D)) for part in parts], axis=0
    )
    query_rows = jnp.where(head_rows, query_rows, 0.0).astype(bf16)
    peak = None
    scores = []
    for v in range(var_local):
        own = jnp.where(var_of == v, x_all, jnp.zeros_like(x_all))
        embedded = (dot(own, embed_ref[...]) + bias_ref[v : v + 1, :].astype(f32)).astype(bf16)
        e_ref[v] = embedded
        three = dot_t(embedded, query_rows)
        score = (three[:, :H] + three[:, H : 2 * H] + three[:, 2 * H :]) * (1.0 / math.sqrt(DH))
        s_ref[v] = score
        scores.append(score)
        peak = score if peak is None else jnp.maximum(peak, score)
    expand = head_expand(2)
    total = None
    for v in range(var_local):
        weights = jnp.exp(scores[v] - peak)
        total = weights if total is None else total + weights
        both = jnp.concatenate(split(weights, 2), axis=1)
        term = dot(both, expand) * e_ref[v].astype(f32)
        if v == 0:
            sum_ref[...] = term
        else:
            sum_ref[...] += term
    groups = exch_ref.shape[0]
    width = D // groups
    for g in range(groups):
        exch_ref[g, :patches, :] = sum_ref[:, g * width : (g + 1) * width]


def target_of(column_ref, row_ref, depth, as_row):
    column = column_ref[...]
    row = row_ref[...]
    count = column.shape[0]
    same = column == row
    first, second = iota((count, count), 0), iota((count, count), 1)
    if as_row:
        rank = jnp.sum(jnp.where(same & (first < second), 1.0, 0.0), axis=0, keepdims=True)
        return row * depth + rank.astype(jnp.int32)
    rank = jnp.sum(jnp.where(same & (second < first), 1.0, 0.0), axis=1, keepdims=True)
    return column * depth + rank.astype(jnp.int32)


def stats_kernel(
    depth, column_ref, row_ref, inbox_ref, e_ref, s_ref, old_ref, up_ref, ga_ref, exch_ref, stats_ref, sems
):
    patches = column_ref.shape[0]
    slots = inbox_ref.shape[0]
    target = target_of(column_ref, row_ref, depth, False)
    pick = jnp.where(iota((patches, slots), 1) == target, 1.0, 0.0).astype(bf16)
    upstream = dot(pick, inbox_ref[...])
    up_ref[...] = upstream.astype(bf16)
    reduce_heads = spread(D, H, lambda r, c: r // DH == c)
    var_local = e_ref.shape[0]
    peak = s_ref[0]
    for v in range(1, var_local):
        peak = jnp.maximum(peak, s_ref[v])
    total = jnp.zeros_like(peak)
    inner = jnp.zeros_like(peak)
    for v in range(var_local):
        high, low = split(upstream * e_ref[v].astype(f32), 2)
        grad_attn = dot(high, reduce_heads) + dot(low, reduce_heads)
        ga_ref[v] = grad_attn
        weights = jnp.exp(s_ref[v] - peak)
        total = total + weights
        inner = inner + weights * grad_attn
    packed = jnp.concatenate([peak, total, inner, jnp.zeros((patches, LANES - 3 * H), f32)], axis=1)
    if patches < LANES:
        packed = jnp.concatenate([packed, jnp.zeros((LANES - patches, LANES), f32)], axis=0)
    stats_ref[...] = packed.T[: 3 * H, :]
    copies = [
        pltpu.make_async_copy(stats_ref, exch_ref.at[g, pl.ds(patches, 3 * H)], sems.at[g])
        for g in range(exch_ref.shape[0])
    ]
    for copy in copies:
        copy.start()
    for copy in copies:
        copy.wait()


def combine_stats(exch_ref, patches):
    groups = exch_ref.shape[0]
    peaks, totals, inners = [], [], []
    for g in range(groups):
        stats = exch_ref[g, patches : patches + 3 * H, :]
        rows = jnp.concatenate([stats, jnp.zeros((LANES - 3 * H, LANES), f32)], axis=0).T
        rows = rows[:patches]
        peaks.append(rows[:, :H])
        totals.append(rows[:, H : 2 * H])
        inners.append(rows[:, 2 * H : 3 * H])
    peak = peaks[0]
    for other in peaks[1:]:
        peak = jnp.maximum(peak, other)
    factors = [jnp.exp(one - peak) for one in peaks]
    total = sum(f * t for f, t in zip(factors, totals))
    inner = sum(f * t for f, t in zip(factors, inners)) / total
    return peak, total, inner, factors


def tokens_kernel(depth, slots, place_ref, column_ref, row_ref, exch_ref, out_ref):
    patches = column_ref.shape[0]
    groups, _, width = exch_ref.shape
    _, total, _, factors = combine_stats(exch_ref, patches)
    heads = width // DH
    first = place_ref[0] * heads
    pick = jnp.where(
        iota((3 * H, width), 0) % H == first + iota((3 * H, width), 1) // DH, 1.0, 0.0
    ).astype(bf16)
    mixture = jnp.zeros((patches, width), f32)
    for g in range(groups):
        scale = jnp.concatenate(split(factors[g] / total, 3), axis=1)
        mixture = mixture + dot(scale, pick) * exch_ref[g, :patches, :]
    target = target_of(column_ref, row_ref, depth, True)
    place = jnp.where(iota((slots, patches), 0) == target, 1.0, 0.0).astype(bf16)
    out_ref[...] = dot(place, mixture.astype(bf16))


def backward_kernel(
    exch_ref, s_ref, ga_ref, up_ref, e_ref, x_ref, embed_ref, query_ref, wide_ref, gx_ref
):
    var_local, patches = e_ref.shape[0], e_ref.shape[1]
    wide = var_local * P_SIZE
    peak, total, inner, _ = combine_stats(exch_ref, patches)
    inverse = 1.0 / total
    expand = head_expand(2)
    query = query_ref[...]
    q_parts = split(query, 3)
    rows = [q_parts[0], q_parts[1], q_parts[2], q_parts[0], q_parts[1], q_parts[2]]
    query_rows = jnp.concatenate([jnp.broadcast_to(r.astype(f32), (H, D)) for r in rows], axis=0)
    on_head = iota((6 * H, D), 0) % H == iota((6 * H, D), 1) // DH
    query_rows = jnp.where(on_head, query_rows, 0.0).astype(bf16)
    upstream = up_ref[...].astype(f32)
    x_t = x_ref[...].astype(f32).T.astype(bf16)
    embed_t = embed_ref[...].astype(f32).T.astype(bf16)
    lane_var = iota((patches, wide), 1) // P_SIZE
    grad_x = jnp.zeros((patches, wide), f32)
    query_sum = jnp.zeros((2 * H, D), f32)
    for v in range(var_local):
        attention = jnp.exp(s_ref[v] - peak) * inverse
        grad_score = attention * (ga_ref[v] - inner) * (1.0 / math.sqrt(DH))
        attn = jnp.concatenate(split(attention, 2), axis=1)
        high, low = split(grad_score, 2)
        scored = jnp.concatenate([high, high, high, low, low, low], axis=1)
        grad = dot(attn, expand) * upstream + dot(scored, query_rows)
        low_grad = grad.astype(bf16)
        bias_row = jnp.sum(grad, axis=0, keepdims=True)
        weight_rows = dot(x_t[v * P_SIZE : (v + 1) * P_SIZE, :], low_grad)
        for t in range(TILES):
            cut = slice(t * LANES, (t + 1) * LANES)
            wide_ref[v * TILES + t, :P_SIZE, :] = weight_rows[:, cut]
            wide_ref[v * TILES + t, P_SIZE : P_SIZE + 1, :] = bias_row[:, cut]
        grad_x = jnp.where(lane_var == v, dot(low_grad, embed_t), grad_x)
        pair = jnp.concatenate([high.astype(f32), low.astype(f32)], axis=1)
        pair = jnp.concatenate([pair, jnp.zeros((patches, LANES - 2 * H), f32)], axis=1)
        query_sum = query_sum + dot(pair.T[: 2 * H, :].astype(bf16), e_ref[v])
    gx_ref[...] = grad_x.astype(bf16)
    diagonal = iota((2 * H, D), 0) % H == iota((2 * H, D), 1) // DH
    query_row = jnp.sum(jnp.where(diagonal, query_sum, 0.0), axis=0, keepdims=True)
    half = wide_ref.shape[0] // 2
    for t in range(TILES):
        at = (t // (TILES // 2)) * half + t % (TILES // 2)
        wide_ref[at, P_SIZE + 1 : P_SIZE + 2, :] = query_row[:, t * LANES : (t + 1) * LANES]


def field_kernel(index_ref, weight_ref, gx_ref, out_ref):
    wide = gx_ref.shape[1]
    var_local = wide // P_SIZE
    blocks = gx_ref.shape[0] // PB
    gx_t = gx_ref[...].astype(f32).T.astype(bf16)
    fold = spread(var_local, wide, lambda r, c: c // P_SIZE == r)
    own_pixel = iota((wide, PIX_BLK), 0) % P_SIZE == iota((wide, PIX_BLK), 1) % P_SIZE
    copy = spread(PB, PIX_BLK, lambda r, c: r == c // P_SIZE)
    for block in range(blocks):
        wide_grad = dot(gx_t[:, block * PB : (block + 1) * PB], copy)
        wide_grad = jnp.where(own_pixel, wide_grad, 0.0).astype(bf16)
        grad = dot(fold, wide_grad).astype(bf16)
        matrix = interp_transposed(index_ref, weight_ref, block)
        out_ref[:, pl.ds(block * PTS_BLK, PTS_BLK)] = dot_t(grad, matrix)


def local(
    fields, stencil, stencil_weight, owner_map, embed_weight, embed_bias, agg_query, out_grad
):
    rows = ("r", "c")
    ring = lax.axis_size("r")
    groups = lax.axis_size("z")
    row_devices = ring * 2
    var_local = fields.shape[0]
    patches = owner_map.shape[0]
    capacity = out_grad.shape[0]
    depth = capacity // row_devices
    width = D // groups
    wide = var_local * P_SIZE
    shape = jax.ShapeDtypeStruct

    inbox = lax.all_to_all(
        out_grad.reshape(row_devices, depth, D), rows, split_axis=0, concat_axis=0, tiled=True
    ).reshape(capacity, D)

    index_t = stencil.T
    weight_t = stencil_weight.T
    embed_flat = embed_weight.reshape(wide, D)
    query = agg_query.reshape(1, D)
    row_map = owner_map.reshape(1, patches)
    x_all, embedded, scores, sums = kernel_call(
        forward_kernel,
        (
            shape((patches, wide), bf16),
            shape((var_local, patches, D), bf16),
            shape((var_local, patches, H), f32),
            shape((groups, patches + 3 * H, width), f32),
        ),
        scratch=[pltpu.VMEM((patches, D), f32)],
    )(index_t, weight_t, fields, embed_flat, embed_bias, query)

    vmem = pl.BlockSpec(memory_space=pltpu.VMEM)
    anywhere = pl.BlockSpec(memory_space=pl.ANY)
    upstream, grad_attn, exchange = kernel_call(
        lambda *refs: stats_kernel(depth, *refs),
        (
            shape((patches, D), bf16),
            shape((var_local, patches, H), f32),
            shape(sums.shape, f32),
        ),
        scratch=[pltpu.VMEM((3 * H, LANES), f32), pltpu.SemaphoreType.DMA((groups,))],
        in_specs=[vmem] * 5 + [anywhere],
        out_specs=(vmem, vmem, anywhere),
        aliases={5: 2},
    )(owner_map, row_map, inbox, embedded, scores, sums)
    exchange = lax.all_to_all(exchange, "z", 0, 0, tiled=True)

    chunks = var_local * TILES
    partial, grad_x = kernel_call(
        backward_kernel,
        (
            shape((chunks, CHUNK, LANES), f32),
            shape((patches, wide), bf16),
        ),
    )(exchange, scores, grad_attn, upstream, embedded, x_all, embed_flat, query)

    place = lax.axis_index("z").astype(jnp.int32).reshape(1)
    outbox = kernel_call(
        lambda *refs: tokens_kernel(depth, capacity, *refs),
        shape((capacity, width), f32),
        in_specs=[pl.BlockSpec(memory_space=pltpu.SMEM)] + [vmem] * 3,
    )(place, owner_map, row_map, exchange)

    field_grad = kernel_call(field_kernel, shape((var_local, blocks_of(fields)), f32))(
        index_t, weight_t, grad_x
    )

    core = lax.axis_index("c")
    share = chunks // (2 * ring)
    both = 2 * depth
    halves = lax.all_to_all(
        partial.reshape(2, chunks // 2, CHUNK, LANES), "c", 0, 0, tiled=True
    )
    halves = halves[0] + halves[1]
    going = jnp.concatenate(
        [halves.reshape(ring, share * CHUNK, LANES), outbox.reshape(ring, both, width)], axis=1
    )
    coming = lax.all_to_all(going, "r", 0, 0, tiled=True)
    query_half = lax.psum(halves[: TILES // 2, P_SIZE + 1, :], "z")
    own = jnp.sum(coming[:, : share * CHUNK], axis=0).reshape(share, CHUNK, LANES)
    spare = jnp.zeros((share, CHUNK - P_SIZE - 1, LANES), f32)
    spare = spare.at[0, : TILES // 2].set(query_half)
    own = jnp.concatenate([own[:, : P_SIZE + 1], spare], axis=1)
    half = lax.all_to_all(
        jnp.broadcast_to(own[None], (ring,) + own.shape), "r", 0, 0, tiled=True
    )

    arrived = coming[:, share * CHUNK :].astype(bf16).reshape(ring, 2, depth, width)
    swap = [(0, 1), (1, 0)]
    crossed = lax.ppermute(jnp.where(core == 0, arrived[:, 1], arrived[:, 0]), "c", swap)
    kept = jnp.where(core == 0, arrived[:, 0], arrived[:, 1])
    tokens = jnp.where(
        core == 0, jnp.stack([kept, crossed], axis=1), jnp.stack([crossed, kept], axis=1)
    ).reshape(capacity, width)

    other = lax.ppermute(half, "c", swap)
    whole = jnp.where(core == 0, jnp.stack([half, other]), jnp.stack([other, half]))
    query_rows = whole[:, :, 0, P_SIZE + 1 : P_SIZE + 1 + TILES // 2, :]
    query_grad = jnp.sum(query_rows, axis=1).reshape(H, DH)
    whole = whole.reshape(var_local, TILES, CHUNK, LANES)
    weight_grad = whole[:, :, :P_SIZE, :].transpose(0, 2, 1, 3).reshape(var_local, P_SIZE, D)
    bias_grad = whole[:, :, P_SIZE, :].reshape(var_local, D)
    return (tokens, field_grad, weight_grad, bias_grad, query_grad)


def blocks_of(fields):
    return fields.shape[1]


def solution(mesh):
    rows, groups = mesh.shape["rows"], mesh.shape["vars"]
    inner = Mesh(mesh.devices.reshape(rows // 2, 2, groups), ("r", "c", "z"))
    by_rows = ("r", "c")
    return jax.shard_map(
        local,
        mesh=inner,
        in_specs=(
            P("z", by_rows),
            P(by_rows, None),
            P(by_rows, None),
            P(by_rows, None),
            P("z", None, None),
            P("z", None),
            P(),
            P(by_rows, None),
        ),
        out_specs=(
            P(by_rows, "z"),
            P("z", by_rows),
            P("z", None, None),
            P("z", None),
            P(),
        ),
        check_vma=False,
    )
```

```python
import math

import jax
import jax.numpy as jnp
from jax import lax
from jax.experimental import pallas as pl
from jax.experimental.pallas import tpu as pltpu
from jax.sharding import Mesh
from jax.sharding import PartitionSpec as P

D = 1024
H = 16
DH = 64
P_SIZE = 16
K = 4
PTS_BLK = 1024
PB = 32
PIX_BLK = PB * P_SIZE
LANES = 128
TILES = D // LANES
CHUNK = 24
INTERPRET = False

f32 = jnp.float32
bf16 = jnp.bfloat16


def iota(shape, axis):
    return lax.broadcasted_iota(jnp.int32, shape, axis)


def dot(first, second):
    return lax.dot_general(first, second, (((1,), (0,)), ((), ())), preferred_element_type=f32)


def dot_t(first, second):
    return lax.dot_general(first, second, (((1,), (1,)), ((), ())), preferred_element_type=f32)


def split(value, parts):
    pieces = []
    for _ in range(parts):
        piece = value.astype(bf16)
        pieces.append(piece)
        value = value - piece.astype(f32)
    return pieces


def kernel_call(body, out_shape, mib, scratch=(), in_specs=None, out_specs=None, aliases=None):
    extra = {}
    if in_specs is not None:
        extra["in_specs"] = in_specs
    if out_specs is not None:
        extra["out_specs"] = out_specs
    return pl.pallas_call(
        body,
        out_shape=out_shape,
        scratch_shapes=list(scratch),
        input_output_aliases=aliases or {},
        interpret=INTERPRET,
        compiler_params=pltpu.CompilerParams(vmem_limit_bytes=mib << 20),
        **extra,
    )


def interp_transposed(index_ref, weight_ref, block):
    where = pl.ds(block * PIX_BLK, PIX_BLK)
    index = [index_ref[k : k + 1, where] for k in range(K)]
    weight = [weight_ref[k : k + 1, where] for k in range(K)]
    points = iota((PTS_BLK, PIX_BLK), 0)
    matrix = jnp.zeros((PTS_BLK, PIX_BLK), f32)
    for k in range(K):
        total = jnp.zeros((1, PIX_BLK), f32)
        for j in range(K):
            total = total + jnp.where(index[j] == index[k], weight[j], 0.0)
        matrix = jnp.where(points == index[k], total, matrix)
    return matrix.astype(bf16)


def spread(rows, cols, test):
    return jnp.where(test(iota((rows, cols), 0), iota((rows, cols), 1)), 1.0, 0.0).astype(bf16)


def pixel_masks(var_local):
    wide = var_local * P_SIZE
    copy_rows = spread(wide, var_local, lambda r, c: r // P_SIZE == c)
    own_pixel = iota((wide, PIX_BLK), 0) % P_SIZE == iota((wide, PIX_BLK), 1) % P_SIZE
    return copy_rows, own_pixel


def head_expand(copies):
    return spread(copies * H, D, lambda r, c: r % H == c // DH)


def forward_kernel(
    index_ref, weight_ref, fields_ref, embed_ref, bias_ref, query_ref, x_ref, e_ref, s_ref, exch_ref, sum_ref
):
    var_local = fields_ref.shape[0]
    blocks = fields_ref.shape[1] // PTS_BLK
    wide = var_local * P_SIZE
    copy_rows, own_pixel = pixel_masks(var_local)
    gather = spread(PB, PIX_BLK, lambda r, c: r == c // P_SIZE)
    for block in range(blocks):
        matrix = interp_transposed(index_ref, weight_ref, block)
        pixels = dot(fields_ref[:, pl.ds(block * PTS_BLK, PTS_BLK)], matrix).astype(bf16)
        widened = jnp.where(own_pixel, dot(copy_rows, pixels), 0.0).astype(bf16)
        x_ref[pl.ds(block * PB, PB), :] = dot_t(gather, widened).astype(bf16)
    x_all = x_ref[...]
    patches = x_all.shape[0]
    var_of = iota((patches, wide), 1) // P_SIZE
    head_rows = iota((3 * H, D), 0) % H == iota((3 * H, D), 1) // DH
    parts = split(query_ref[...], 3)
    query_rows = jnp.concatenate(
        [jnp.broadcast_to(part.astype(f32), (H, D)) for part in parts], axis=0
    )
    query_rows = jnp.where(head_rows, query_rows, 0.0).astype(bf16)
    peak = None
    scores = []
    for v in range(var_local):
        own = jnp.where(var_of == v, x_all, jnp.zeros_like(x_all))
        embedded = (dot(own, embed_ref[...]) + bias_ref[v : v + 1, :].astype(f32)).astype(bf16)
        e_ref[v] = embedded
        three = dot_t(embedded, query_rows)
        score = (three[:, :H] + three[:, H : 2 * H] + three[:, 2 * H :]) * (1.0 / math.sqrt(DH))
        s_ref[v] = score
        scores.append(score)
        peak = score if peak is None else jnp.maximum(peak, score)
    expand = head_expand(2)
    total = None
    for v in range(var_local):
        weights = jnp.exp(scores[v] - peak)
        total = weights if total is None else total + weights
        both = jnp.concatenate(split(weights, 2), axis=1)
        term = dot(both, expand) * e_ref[v].astype(f32)
        if v == 0:
            sum_ref[...] = term
        else:
            sum_ref[...] += term
    groups = exch_ref.shape[0]
    width = D // groups
    for g in range(groups):
        exch_ref[g, :patches, :] = sum_ref[:, g * width : (g + 1) * width]


def target_of(column_ref, row_ref, depth, as_row):
    column = column_ref[...]
    row = row_ref[...]
    count = column.shape[0]
    same = column == row
    first, second = iota((count, count), 0), iota((count, count), 1)
    if as_row:
        rank = jnp.sum(jnp.where(same & (first < second), 1.0, 0.0), axis=0, keepdims=True)
        return row * depth + rank.astype(jnp.int32)
    rank = jnp.sum(jnp.where(same & (second < first), 1.0, 0.0), axis=1, keepdims=True)
    return column * depth + rank.astype(jnp.int32)


def stats_kernel(
    depth, column_ref, row_ref, inbox_ref, e_ref, s_ref, old_ref, up_ref, ga_ref, exch_ref, stats_ref, sems
):
    patches = column_ref.shape[0]
    slots = inbox_ref.shape[0]
    target = target_of(column_ref, row_ref, depth, False)
    pick = jnp.where(iota((patches, slots), 1) == target, 1.0, 0.0).astype(bf16)
    upstream = dot(pick, inbox_ref[...])
    up_ref[...] = upstream.astype(bf16)
    reduce_heads = spread(D, H, lambda r, c: r // DH == c)
    var_local = e_ref.shape[0]
    peak = s_ref[0]
    for v in range(1, var_local):
        peak = jnp.maximum(peak, s_ref[v])
    total = jnp.zeros_like(peak)
    inner = jnp.zeros_like(peak)
    for v in range(var_local):
        high, low = split(upstream * e_ref[v].astype(f32), 2)
        grad_attn = dot(high, reduce_heads) + dot(low, reduce_heads)
        ga_ref[v] = grad_attn
        weights = jnp.exp(s_ref[v] - peak)
        total = total + weights
        inner = inner + weights * grad_attn
    packed = jnp.concatenate([peak, total, inner, jnp.zeros((patches, LANES - 3 * H), f32)], axis=1)
    if patches < LANES:
        packed = jnp.concatenate([packed, jnp.zeros((LANES - patches, LANES), f32)], axis=0)
    stats_ref[...] = packed.T[: 3 * H, :]
    copies = [
        pltpu.make_async_copy(stats_ref, exch_ref.at[g, pl.ds(patches, 3 * H)], sems.at[g])
        for g in range(exch_ref.shape[0])
    ]
    for copy in copies:
        copy.start()
    for copy in copies:
        copy.wait()


def combine_stats(exch_ref, patches):
    groups = exch_ref.shape[0]
    peaks, totals, inners = [], [], []
    for g in range(groups):
        stats = exch_ref[g, patches : patches + 3 * H, :]
        rows = jnp.concatenate([stats, jnp.zeros((LANES - 3 * H, LANES), f32)], axis=0).T
        rows = rows[:patches]
        peaks.append(rows[:, :H])
        totals.append(rows[:, H : 2 * H])
        inners.append(rows[:, 2 * H : 3 * H])
    peak = peaks[0]
    for other in peaks[1:]:
        peak = jnp.maximum(peak, other)
    factors = [jnp.exp(one - peak) for one in peaks]
    total = sum(f * t for f, t in zip(factors, totals))
    inner = sum(f * t for f, t in zip(factors, inners)) / total
    return peak, total, inner, factors


def merge_kernel(depth, slots, place_ref, column_ref, row_ref, exch_ref, halves_ref, going_ref, query_ref):
    patches = column_ref.shape[0]
    groups, _, width = exch_ref.shape
    ring, rows = halves_ref.shape[1], halves_ref.shape[2]
    _, total, _, factors = combine_stats(exch_ref, patches)
    heads = width // DH
    first = place_ref[0] * heads
    pick = jnp.where(
        iota((3 * H, width), 0) % H == first + iota((3 * H, width), 1) // DH, 1.0, 0.0
    ).astype(bf16)
    mixture = jnp.zeros((patches, width), f32)
    for g in range(groups):
        scale = jnp.concatenate(split(factors[g] / total, 3), axis=1)
        mixture = mixture + dot(scale, pick) * exch_ref[g, :patches, :]
    target = target_of(column_ref, row_ref, depth, True)
    place = jnp.where(iota((slots, patches), 0) == target, 1.0, 0.0).astype(bf16)
    tokens = dot(place, mixture.astype(bf16))
    going_ref[:, rows:, :] = tokens.reshape(ring, slots // ring, width)
    going_ref[:, :rows, :] = halves_ref[0] + halves_ref[1]
    share = rows // CHUNK
    for t in range(TILES // 2):
        at = (t % share) * CHUNK + P_SIZE + 1
        query_ref[t : t + 1, :] = going_ref[t // share, at : at + 1, :]


def own_kernel(coming_ref, query_ref, out_ref):
    ring, rows = out_ref.shape[0], out_ref.shape[1]
    own = coming_ref[0, :rows, :]
    for r in range(1, ring):
        own = own + coming_ref[r, :rows, :]
    spare = jnp.concatenate(
        [query_ref[...], jnp.zeros((CHUNK - P_SIZE - 1 - TILES // 2, LANES), f32)], axis=0
    )
    rest = [own[CHUNK:]] if rows > CHUNK else []
    own = jnp.concatenate([own[: P_SIZE + 1], spare] + rest, axis=0)
    for r in range(ring):
        out_ref[r] = own


def final_kernel(core_ref, half_ref, other_ref, weight_ref, bias_ref, query_ref):
    ring, rows = half_ref.shape[0], half_ref.shape[1]
    share = rows // CHUNK
    low = core_ref[0] == 0
    for c in range(2):
        query = jnp.zeros((TILES // 2, LANES), f32)
        for r in range(ring):
            half, other = half_ref[r], other_ref[r]
            block = jnp.where(low, half, other) if c == 0 else jnp.where(low, other, half)
            for k in range(share):
                v, t = divmod((c * ring + r) * share + k, TILES)
                cut = slice(t * LANES, (t + 1) * LANES)
                weight_ref[v * P_SIZE : (v + 1) * P_SIZE, cut] = block[k * CHUNK : k * CHUNK + P_SIZE]
                bias_ref[v : v + 1, cut] = block[k * CHUNK + P_SIZE : k * CHUNK + P_SIZE + 1]
            query = query + block[P_SIZE + 1 : P_SIZE + 1 + TILES // 2]
        for t in range(TILES // 2):
            at = (c * (TILES // 2) + t) * 2
            query_ref[at : at + 1, :] = query[t : t + 1, :DH]
            query_ref[at + 1 : at + 2, :] = query[t : t + 1, DH:]


def backward_kernel(
    exch_ref, s_ref, ga_ref, up_ref, e_ref, x_ref, embed_ref, query_ref, wide_ref, gx_ref
):
    var_local, patches = e_ref.shape[0], e_ref.shape[1]
    wide = var_local * P_SIZE
    peak, total, inner, _ = combine_stats(exch_ref, patches)
    inverse = 1.0 / total
    expand = head_expand(2)
    query = query_ref[...]
    q_parts = split(query, 3)
    rows = [q_parts[0], q_parts[1], q_parts[2], q_parts[0], q_parts[1], q_parts[2]]
    query_rows = jnp.concatenate([jnp.broadcast_to(r.astype(f32), (H, D)) for r in rows], axis=0)
    on_head = iota((6 * H, D), 0) % H == iota((6 * H, D), 1) // DH
    query_rows = jnp.where(on_head, query_rows, 0.0).astype(bf16)
    upstream = up_ref[...].astype(f32)
    x_t = x_ref[...].astype(f32).T.astype(bf16)
    embed_t = embed_ref[...].astype(f32).T.astype(bf16)
    lane_var = iota((patches, wide), 1) // P_SIZE
    grad_x = jnp.zeros((patches, wide), f32)
    query_sum = jnp.zeros((2 * H, D), f32)
    for v in range(var_local):
        attention = jnp.exp(s_ref[v] - peak) * inverse
        grad_score = attention * (ga_ref[v] - inner) * (1.0 / math.sqrt(DH))
        attn = jnp.concatenate(split(attention, 2), axis=1)
        high, low = split(grad_score, 2)
        scored = jnp.concatenate([high, high, high, low, low, low], axis=1)
        grad = dot(attn, expand) * upstream + dot(scored, query_rows)
        low_grad = grad.astype(bf16)
        bias_row = jnp.sum(grad, axis=0, keepdims=True)
        weight_rows = dot(x_t[v * P_SIZE : (v + 1) * P_SIZE, :], low_grad)
        for t in range(TILES):
            cut = slice(t * LANES, (t + 1) * LANES)
            wide_ref[v * TILES + t, :P_SIZE, :] = weight_rows[:, cut]
            wide_ref[v * TILES + t, P_SIZE : P_SIZE + 1, :] = bias_row[:, cut]
        grad_x = jnp.where(lane_var == v, dot(low_grad, embed_t), grad_x)
        pair = jnp.concatenate([high.astype(f32), low.astype(f32)], axis=1)
        pair = jnp.concatenate([pair, jnp.zeros((patches, LANES - 2 * H), f32)], axis=1)
        query_sum = query_sum + dot(pair.T[: 2 * H, :].astype(bf16), e_ref[v])
    gx_ref[...] = grad_x.astype(bf16)
    diagonal = iota((2 * H, D), 0) % H == iota((2 * H, D), 1) // DH
    query_row = jnp.sum(jnp.where(diagonal, query_sum, 0.0), axis=0, keepdims=True)
    half = wide_ref.shape[0] // 2
    for t in range(TILES):
        at = (t // (TILES // 2)) * half + t % (TILES // 2)
        wide_ref[at, P_SIZE + 1 : P_SIZE + 2, :] = query_row[:, t * LANES : (t + 1) * LANES]


def field_kernel(index_ref, weight_ref, gx_ref, out_ref):
    wide = gx_ref.shape[1]
    var_local = wide // P_SIZE
    blocks = gx_ref.shape[0] // PB
    gx_t = gx_ref[...].astype(f32).T.astype(bf16)
    fold = spread(var_local, wide, lambda r, c: c // P_SIZE == r)
    own_pixel = iota((wide, PIX_BLK), 0) % P_SIZE == iota((wide, PIX_BLK), 1) % P_SIZE
    copy = spread(PB, PIX_BLK, lambda r, c: r == c // P_SIZE)
    for block in range(blocks):
        wide_grad = dot(gx_t[:, block * PB : (block + 1) * PB], copy)
        wide_grad = jnp.where(own_pixel, wide_grad, 0.0).astype(bf16)
        grad = dot(fold, wide_grad).astype(bf16)
        matrix = interp_transposed(index_ref, weight_ref, block)
        out_ref[:, pl.ds(block * PTS_BLK, PTS_BLK)] = dot_t(grad, matrix)


def local(
    fields, stencil, stencil_weight, owner_map, embed_weight, embed_bias, agg_query, out_grad
):
    by_rows = ("r", "c")
    ring = lax.axis_size("r")
    groups = lax.axis_size("z")
    row_devices = ring * 2
    var_local = fields.shape[0]
    patches = owner_map.shape[0]
    capacity = out_grad.shape[0]
    depth = capacity // row_devices
    width = D // groups
    wide = var_local * P_SIZE
    shape = jax.ShapeDtypeStruct

    inbox = lax.all_to_all(
        out_grad.reshape(row_devices, depth, D), by_rows, split_axis=0, concat_axis=0, tiled=True
    ).reshape(capacity, D)

    index_t = stencil.T
    weight_t = stencil_weight.T
    embed_flat = embed_weight.reshape(wide, D)
    query = agg_query.reshape(1, D)
    row_map = owner_map.reshape(1, patches)
    x_all, embedded, scores, sums = kernel_call(
        forward_kernel,
        (
            shape((patches, wide), bf16),
            shape((var_local, patches, D), bf16),
            shape((var_local, patches, H), f32),
            shape((groups, patches + 3 * H, width), f32),
        ),
        mib=20,
        scratch=[pltpu.VMEM((patches, D), f32)],
    )(index_t, weight_t, fields, embed_flat, embed_bias, query)

    vmem = pl.BlockSpec(memory_space=pltpu.VMEM)
    anywhere = pl.BlockSpec(memory_space=pl.ANY)
    upstream, grad_attn, exchange = kernel_call(
        lambda *refs: stats_kernel(depth, *refs),
        (
            shape((patches, D), bf16),
            shape((var_local, patches, H), f32),
            shape(sums.shape, f32),
        ),
        mib=12,
        scratch=[pltpu.VMEM((3 * H, LANES), f32), pltpu.SemaphoreType.DMA((groups,))],
        in_specs=[vmem] * 5 + [anywhere],
        out_specs=(vmem, vmem, anywhere),
        aliases={5: 2},
    )(owner_map, row_map, inbox, embedded, scores, sums)
    exchange = lax.all_to_all(exchange, "z", 0, 0, tiled=True)

    chunks = var_local * TILES
    partial, grad_x = kernel_call(
        backward_kernel,
        (
            shape((chunks, CHUNK, LANES), f32),
            shape((patches, wide), bf16),
        ),
        mib=16,
    )(exchange, scores, grad_attn, upstream, embedded, x_all, embed_flat, query)

    field_grad = kernel_call(field_kernel, shape((var_local, fields.shape[1]), f32), mib=16)(
        index_t, weight_t, grad_x
    )

    core = lax.axis_index("c").astype(jnp.int32)
    place = lax.axis_index("z").astype(jnp.int32)
    smem = pl.BlockSpec(memory_space=pltpu.SMEM)
    rows = chunks // (2 * ring) * CHUNK
    both = 2 * depth
    halves = lax.all_to_all(partial.reshape(2, ring, rows, LANES), "c", 0, 0, tiled=True)
    going, query_half = kernel_call(
        lambda *refs: merge_kernel(depth, capacity, *refs),
        (shape((ring, rows + both, LANES), f32), shape((TILES // 2, LANES), f32)),
        mib=8,
        in_specs=[smem] + [vmem] * 4,
    )(place.reshape(1), owner_map, row_map, exchange, halves)
    coming = lax.all_to_all(going, "r", 0, 0, tiled=True)
    query_half = lax.psum(query_half, "z")
    own = kernel_call(own_kernel, shape((ring, rows, LANES), f32), mib=8)(coming, query_half)
    half = lax.all_to_all(own, "r", 0, 0, tiled=True)

    arrived = coming[:, rows:].astype(bf16).reshape(ring, 2, depth, width)
    swap = [(0, 1), (1, 0)]
    crossed = lax.ppermute(jnp.where(core == 0, arrived[:, 1], arrived[:, 0]), "c", swap)
    kept = jnp.where(core == 0, arrived[:, 0], arrived[:, 1])
    tokens = jnp.where(
        core == 0, jnp.stack([kept, crossed], axis=1), jnp.stack([crossed, kept], axis=1)
    ).reshape(capacity, width)

    half, tokens = lax.optimization_barrier((half, tokens))
    other = lax.ppermute(half, "c", swap)
    weight_grad, bias_grad, query_grad = kernel_call(
        final_kernel,
        (shape((wide, D), f32), shape((var_local, D), f32), shape((H, DH), f32)),
        mib=8,
        in_specs=[smem, vmem, vmem],
    )(core.reshape(1), half, other)
    weight_grad = weight_grad.reshape(var_local, P_SIZE, D)
    return (tokens, field_grad, weight_grad, bias_grad, query_grad)


def solution(mesh):
    rows, groups = mesh.shape["rows"], mesh.shape["vars"]
    inner = Mesh(mesh.devices.reshape(rows // 2, 2, groups), ("r", "c", "z"))
    by_rows = ("r", "c")
    return jax.shard_map(
        local,
        mesh=inner,
        in_specs=(
            P("z", by_rows),
            P(by_rows, None),
            P(by_rows, None),
            P(by_rows, None),
            P("z", None, None),
            P("z", None),
            P(),
            P(by_rows, None),
        ),
        out_specs=(
            P(by_rows, "z"),
            P("z", by_rows),
            P("z", None, None),
            P("z", None),
            P(),
        ),
        check_vma=False,
    )
```

```python
import math

import jax
import jax.numpy as jnp
from jax import lax
from jax.experimental import pallas as pl
from jax.experimental.pallas import tpu as pltpu
from jax.sharding import Mesh
from jax.sharding import PartitionSpec as P

D = 1024
H = 16
DH = 64
P_SIZE = 16
K = 4
PTS_BLK = 1024
PB = 32
PIX_BLK = PB * P_SIZE
LANES = 128
TILES = D // LANES
CHUNK = 24
INTERPRET = False

f32 = jnp.float32
bf16 = jnp.bfloat16


def iota(shape, axis):
    return lax.broadcasted_iota(jnp.int32, shape, axis)


def dot(first, second):
    return lax.dot_general(first, second, (((1,), (0,)), ((), ())), preferred_element_type=f32)


def dot_t(first, second):
    return lax.dot_general(first, second, (((1,), (1,)), ((), ())), preferred_element_type=f32)


def split(value, parts):
    pieces = []
    for _ in range(parts):
        piece = value.astype(bf16)
        pieces.append(piece)
        value = value - piece.astype(f32)
    return pieces


def over_vars(value, join):
    shift = value.shape[1] // 2
    while shift >= H:
        value = join(value, pltpu.roll(value, shift, axis=1))
        shift //= 2
    return value


def group(value, v):
    return value[:, v * H : (v + 1) * H]


def kernel_call(body, out_shape, mib, scratch=(), in_specs=None, out_specs=None, aliases=None):
    extra = {}
    if in_specs is not None:
        extra["in_specs"] = in_specs
    if out_specs is not None:
        extra["out_specs"] = out_specs
    return pl.pallas_call(
        body,
        out_shape=out_shape,
        scratch_shapes=list(scratch),
        input_output_aliases=aliases or {},
        interpret=INTERPRET,
        compiler_params=pltpu.CompilerParams(vmem_limit_bytes=mib << 20),
        **extra,
    )


def interp_transposed(index_ref, weight_ref, block):
    where = pl.ds(block * PIX_BLK, PIX_BLK)
    index = [index_ref[k : k + 1, where] for k in range(K)]
    weight = [weight_ref[k : k + 1, where] for k in range(K)]
    points = iota((PTS_BLK, PIX_BLK), 0)
    matrix = jnp.zeros((PTS_BLK, PIX_BLK), f32)
    for k in range(K):
        total = jnp.zeros((1, PIX_BLK), f32)
        for j in range(K):
            total = total + jnp.where(index[j] == index[k], weight[j], 0.0)
        matrix = jnp.where(points == index[k], total, matrix)
    return matrix.astype(bf16)


def spread(rows, cols, test):
    return jnp.where(test(iota((rows, cols), 0), iota((rows, cols), 1)), 1.0, 0.0).astype(bf16)


def pixel_masks(var_local):
    wide = var_local * P_SIZE
    copy_rows = spread(wide, var_local, lambda r, c: r // P_SIZE == c)
    own_pixel = iota((wide, PIX_BLK), 0) % P_SIZE == iota((wide, PIX_BLK), 1) % P_SIZE
    return copy_rows, own_pixel


def head_expand(copies):
    return spread(copies * H, D, lambda r, c: r % H == c // DH)


def forward_kernel(
    index_ref, weight_ref, fields_ref, embed_ref, bias_ref, query_ref, x_ref, e_ref, s_ref, exch_ref, sum_ref
):
    var_local = fields_ref.shape[0]
    blocks = fields_ref.shape[1] // PTS_BLK
    wide = var_local * P_SIZE
    copy_rows, own_pixel = pixel_masks(var_local)
    gather = spread(PB, PIX_BLK, lambda r, c: r == c // P_SIZE)
    for block in range(blocks):
        matrix = interp_transposed(index_ref, weight_ref, block)
        pixels = dot(fields_ref[:, pl.ds(block * PTS_BLK, PTS_BLK)], matrix).astype(bf16)
        widened = jnp.where(own_pixel, dot(copy_rows, pixels), 0.0).astype(bf16)
        x_ref[pl.ds(block * PB, PB), :] = dot_t(gather, widened).astype(bf16)
    x_all = x_ref[...]
    patches = x_all.shape[0]
    var_of = iota((patches, wide), 1) // P_SIZE
    head_rows = iota((3 * H, D), 0) % H == iota((3 * H, D), 1) // DH
    parts = split(query_ref[...], 3)
    query_rows = jnp.concatenate(
        [jnp.broadcast_to(part.astype(f32), (H, D)) for part in parts], axis=0
    )
    query_rows = jnp.where(head_rows, query_rows, 0.0).astype(bf16)
    scores = []
    for v in range(var_local):
        own = jnp.where(var_of == v, x_all, jnp.zeros_like(x_all))
        embedded = (dot(own, embed_ref[...]) + bias_ref[v : v + 1, :].astype(f32)).astype(bf16)
        e_ref[v] = embedded
        three = dot_t(embedded, query_rows)
        scores.append(three[:, :H] + three[:, H : 2 * H] + three[:, 2 * H :])
    scores = jnp.concatenate(scores, axis=1) * (1.0 / math.sqrt(DH))
    s_ref[...] = scores
    weights = split(jnp.exp(scores - over_vars(scores, jnp.maximum)), 2)
    expand = head_expand(2)
    for v in range(var_local):
        both = jnp.concatenate([group(part, v) for part in weights], axis=1)
        term = dot(both, expand) * e_ref[v].astype(f32)
        if v == 0:
            sum_ref[...] = term
        else:
            sum_ref[...] += term
    groups = exch_ref.shape[0]
    width = D // groups
    for g in range(groups):
        exch_ref[g, :patches, :] = sum_ref[:, g * width : (g + 1) * width]


def target_of(column_ref, row_ref, depth, as_row):
    column = column_ref[...]
    row = row_ref[...]
    count = column.shape[0]
    same = column == row
    first, second = iota((count, count), 0), iota((count, count), 1)
    if as_row:
        rank = jnp.sum(jnp.where(same & (first < second), 1.0, 0.0), axis=0, keepdims=True)
        return row * depth + rank.astype(jnp.int32)
    rank = jnp.sum(jnp.where(same & (second < first), 1.0, 0.0), axis=1, keepdims=True)
    return column * depth + rank.astype(jnp.int32)


def outbox_kernel(grad_ref, out_ref):
    out_ref[...] = grad_ref[...].reshape(out_ref.shape)


def stats_kernel(
    depth,
    column_ref,
    row_ref,
    inbox_ref,
    e_ref,
    s_ref,
    x_ref,
    old_ref,
    up_ref,
    both_ref,
    xt_ref,
    exch_ref,
    stats_ref,
    sems,
):
    patches = column_ref.shape[0]
    slots = inbox_ref.shape[0] * inbox_ref.shape[1]
    target = target_of(column_ref, row_ref, depth, False)
    pick = jnp.where(iota((patches, slots), 1) == target, 1.0, 0.0).astype(bf16)
    upstream = dot(pick, inbox_ref[...].reshape(slots, D))
    up_ref[...] = upstream.astype(bf16)
    reduce_heads = spread(D, H, lambda r, c: r // DH == c)
    var_local = e_ref.shape[0]
    grad_attn = []
    for v in range(var_local):
        high, low = split(upstream * e_ref[v].astype(f32), 2)
        grad_attn.append(dot(high, reduce_heads) + dot(low, reduce_heads))
    grad_attn = jnp.concatenate(grad_attn, axis=1)
    scores = s_ref[...]
    both_ref[0] = scores
    both_ref[1] = grad_attn
    xt_ref[...] = x_ref[...].astype(f32).T.astype(bf16)
    peak = over_vars(scores, jnp.maximum)
    weights = jnp.exp(scores - peak)
    total = over_vars(weights, jnp.add)
    inner = over_vars(weights * grad_attn, jnp.add)
    packed = [group(peak, 0), group(total, 0), group(inner, 0)]
    packed = jnp.concatenate(packed + [jnp.zeros((patches, LANES - 3 * H), f32)], axis=1)
    if patches < LANES:
        packed = jnp.concatenate([packed, jnp.zeros((LANES - patches, LANES), f32)], axis=0)
    stats_ref[...] = packed.T[: 3 * H, :]
    copies = [
        pltpu.make_async_copy(stats_ref, exch_ref.at[g, pl.ds(patches, 3 * H)], sems.at[g])
        for g in range(exch_ref.shape[0])
    ]
    for copy in copies:
        copy.start()
    for copy in copies:
        copy.wait()


def combine_stats(exch_ref, patches):
    groups = exch_ref.shape[0]
    peaks, totals, inners = [], [], []
    for g in range(groups):
        stats = exch_ref[g, patches : patches + 3 * H, :]
        rows = jnp.concatenate([stats, jnp.zeros((LANES - 3 * H, LANES), f32)], axis=0).T
        rows = rows[:patches]
        peaks.append(rows[:, :H])
        totals.append(rows[:, H : 2 * H])
        inners.append(rows[:, 2 * H : 3 * H])
    peak = peaks[0]
    for other in peaks[1:]:
        peak = jnp.maximum(peak, other)
    factors = [jnp.exp(one - peak) for one in peaks]
    total = sum(f * t for f, t in zip(factors, totals))
    inner = sum(f * t for f, t in zip(factors, inners)) / total
    return peak, total, inner, factors


def merge_kernel(depth, slots, place_ref, column_ref, row_ref, exch_ref, halves_ref, going_ref, query_ref):
    patches = column_ref.shape[0]
    groups, _, width = exch_ref.shape
    ring, rows = halves_ref.shape[1], halves_ref.shape[2]
    _, total, _, factors = combine_stats(exch_ref, patches)
    heads = width // DH
    first = place_ref[0] * heads
    pick = jnp.where(
        iota((3 * H, width), 0) % H == first + iota((3 * H, width), 1) // DH, 1.0, 0.0
    ).astype(bf16)
    mixture = jnp.zeros((patches, width), f32)
    for g in range(groups):
        scale = jnp.concatenate(split(factors[g] / total, 3), axis=1)
        mixture = mixture + dot(scale, pick) * exch_ref[g, :patches, :]
    target = target_of(column_ref, row_ref, depth, True)
    place = jnp.where(iota((slots, patches), 0) == target, 1.0, 0.0).astype(bf16)
    tokens = dot(place, mixture.astype(bf16))
    going_ref[:, rows:, :] = tokens.reshape(ring, slots // ring, width)
    going_ref[:, :rows, :] = halves_ref[0] + halves_ref[1]
    share = rows // CHUNK
    for t in range(TILES // 2):
        at = (t % share) * CHUNK + P_SIZE + 1
        query_ref[t : t + 1, :] = going_ref[t // share, at : at + 1, :]


def own_kernel(coming_ref, query_ref, out_ref):
    ring, rows = out_ref.shape[0], out_ref.shape[1]
    own = coming_ref[0, :rows, :]
    for r in range(1, ring):
        own = own + coming_ref[r, :rows, :]
    spare = jnp.concatenate(
        [query_ref[...], jnp.zeros((CHUNK - P_SIZE - 1 - TILES // 2, LANES), f32)], axis=0
    )
    rest = [own[CHUNK:]] if rows > CHUNK else []
    own = jnp.concatenate([own[: P_SIZE + 1], spare] + rest, axis=0)
    for r in range(ring):
        out_ref[r] = own


def final_kernel(core_ref, half_ref, other_ref, weight_ref, bias_ref, query_ref):
    ring, rows = half_ref.shape[0], half_ref.shape[1]
    share = rows // CHUNK
    low = core_ref[0] == 0
    for c in range(2):
        query = jnp.zeros((TILES // 2, LANES), f32)
        for r in range(ring):
            half, other = half_ref[r], other_ref[r]
            block = jnp.where(low, half, other) if c == 0 else jnp.where(low, other, half)
            for k in range(share):
                v, t = divmod((c * ring + r) * share + k, TILES)
                cut = slice(t * LANES, (t + 1) * LANES)
                weight_ref[v * P_SIZE : (v + 1) * P_SIZE, cut] = block[k * CHUNK : k * CHUNK + P_SIZE]
                bias_ref[v : v + 1, cut] = block[k * CHUNK + P_SIZE : k * CHUNK + P_SIZE + 1]
            query = query + block[P_SIZE + 1 : P_SIZE + 1 + TILES // 2]
        for t in range(TILES // 2):
            at = (c * (TILES // 2) + t) * 2
            query_ref[at : at + 1, :] = query[t : t + 1, :DH]
            query_ref[at + 1 : at + 2, :] = query[t : t + 1, DH:]


def backward_kernel(
    exch_ref, both_ref, up_ref, e_ref, xt_ref, embed_ref, query_ref, wide_ref, gx_ref
):
    var_local, patches = e_ref.shape[0], e_ref.shape[1]
    wide = var_local * P_SIZE
    peak, total, inner, _ = combine_stats(exch_ref, patches)
    peak, inner, inverse = (
        jnp.concatenate([one] * var_local, axis=1) for one in (peak, inner, 1.0 / total)
    )
    attention = jnp.exp(both_ref[0] - peak) * inverse
    grad_score = attention * (both_ref[1] - inner) * (1.0 / math.sqrt(DH))
    attention = split(attention, 2)
    high, low = split(grad_score, 2)
    turned = [part.astype(f32).T.astype(bf16) for part in (high, low)]
    expand = head_expand(2)
    query = query_ref[...]
    q_parts = split(query, 3)
    rows = [q_parts[0], q_parts[1], q_parts[2], q_parts[0], q_parts[1], q_parts[2]]
    query_rows = jnp.concatenate([jnp.broadcast_to(r.astype(f32), (H, D)) for r in rows], axis=0)
    on_head = iota((6 * H, D), 0) % H == iota((6 * H, D), 1) // DH
    query_rows = jnp.where(on_head, query_rows, 0.0).astype(bf16)
    upstream = up_ref[...].astype(f32)
    x_t = xt_ref[...]
    embed_t = embed_ref[...].astype(f32).T.astype(bf16)
    lane_var = iota((patches, wide), 1) // P_SIZE
    grad_x = jnp.zeros((patches, wide), f32)
    query_sum = jnp.zeros((2 * H, D), f32)
    for v in range(var_local):
        attn = jnp.concatenate([group(part, v) for part in attention], axis=1)
        first, second = group(high, v), group(low, v)
        scored = jnp.concatenate([first, first, first, second, second, second], axis=1)
        grad = dot(attn, expand) * upstream + dot(scored, query_rows)
        low_grad = grad.astype(bf16)
        bias_row = jnp.sum(grad, axis=0, keepdims=True)
        weight_rows = dot(x_t[v * P_SIZE : (v + 1) * P_SIZE, :], low_grad)
        for t in range(TILES):
            cut = slice(t * LANES, (t + 1) * LANES)
            wide_ref[v * TILES + t, :P_SIZE, :] = weight_rows[:, cut]
            wide_ref[v * TILES + t, P_SIZE : P_SIZE + 1, :] = bias_row[:, cut]
        grad_x = jnp.where(lane_var == v, dot(low_grad, embed_t), grad_x)
        pair = jnp.concatenate([part[v * H : (v + 1) * H] for part in turned], axis=0)
        query_sum = query_sum + dot(pair, e_ref[v])
    gx_ref[...] = grad_x.astype(bf16)
    diagonal = iota((2 * H, D), 0) % H == iota((2 * H, D), 1) // DH
    query_row = jnp.sum(jnp.where(diagonal, query_sum, 0.0), axis=0, keepdims=True)
    half = wide_ref.shape[0] // 2
    for t in range(TILES):
        at = (t // (TILES // 2)) * half + t % (TILES // 2)
        wide_ref[at, P_SIZE + 1 : P_SIZE + 2, :] = query_row[:, t * LANES : (t + 1) * LANES]


def field_kernel(index_ref, weight_ref, gx_ref, out_ref):
    wide = gx_ref.shape[1]
    var_local = wide // P_SIZE
    blocks = gx_ref.shape[0] // PB
    gx_t = gx_ref[...].astype(f32).T.astype(bf16)
    fold = spread(var_local, wide, lambda r, c: c // P_SIZE == r)
    own_pixel = iota((wide, PIX_BLK), 0) % P_SIZE == iota((wide, PIX_BLK), 1) % P_SIZE
    copy = spread(PB, PIX_BLK, lambda r, c: r == c // P_SIZE)
    for block in range(blocks):
        wide_grad = dot(gx_t[:, block * PB : (block + 1) * PB], copy)
        wide_grad = jnp.where(own_pixel, wide_grad, 0.0).astype(bf16)
        grad = dot(fold, wide_grad).astype(bf16)
        matrix = interp_transposed(index_ref, weight_ref, block)
        out_ref[:, pl.ds(block * PTS_BLK, PTS_BLK)] = dot_t(grad, matrix)


def local(
    fields, stencil, stencil_weight, owner_map, embed_weight, embed_bias, agg_query, out_grad
):
    by_rows = ("r", "c")
    ring = lax.axis_size("r")
    groups = lax.axis_size("z")
    row_devices = ring * 2
    var_local = fields.shape[0]
    patches = owner_map.shape[0]
    capacity = out_grad.shape[0]
    depth = capacity // row_devices
    width = D // groups
    wide = var_local * P_SIZE
    shape = jax.ShapeDtypeStruct

    inbox = lax.all_to_all(
        kernel_call(outbox_kernel, shape((row_devices, depth, D), bf16), mib=8)(out_grad),
        by_rows,
        split_axis=0,
        concat_axis=0,
        tiled=True,
    )

    index_t = stencil.T
    weight_t = stencil_weight.T
    embed_flat = embed_weight.reshape(wide, D)
    query = agg_query.reshape(1, D)
    row_map = owner_map.reshape(1, patches)
    x_all, embedded, scores, sums = kernel_call(
        forward_kernel,
        (
            shape((patches, wide), bf16),
            shape((var_local, patches, D), bf16),
            shape((patches, var_local * H), f32),
            shape((groups, patches + 3 * H, width), f32),
        ),
        mib=20,
        scratch=[pltpu.VMEM((patches, D), f32)],
    )(index_t, weight_t, fields, embed_flat, embed_bias, query)

    vmem = pl.BlockSpec(memory_space=pltpu.VMEM)
    anywhere = pl.BlockSpec(memory_space=pl.ANY)
    upstream, both, x_turned, exchange = kernel_call(
        lambda *refs: stats_kernel(depth, *refs),
        (
            shape((patches, D), bf16),
            shape((2, patches, var_local * H), f32),
            shape((wide, patches), bf16),
            shape(sums.shape, f32),
        ),
        mib=12,
        scratch=[pltpu.VMEM((3 * H, LANES), f32), pltpu.SemaphoreType.DMA((groups,))],
        in_specs=[vmem] * 6 + [anywhere],
        out_specs=(vmem, vmem, vmem, anywhere),
        aliases={6: 3},
    )(owner_map, row_map, inbox, embedded, scores, x_all, sums)
    exchange = lax.all_to_all(exchange, "z", 0, 0, tiled=True)

    chunks = var_local * TILES
    partial, grad_x = kernel_call(
        backward_kernel,
        (
            shape((chunks, CHUNK, LANES), f32),
            shape((patches, wide), bf16),
        ),
        mib=16,
    )(exchange, both, upstream, embedded, x_turned, embed_flat, query)

    field_grad = kernel_call(field_kernel, shape((var_local, fields.shape[1]), f32), mib=16)(
        index_t, weight_t, grad_x
    )

    core = lax.axis_index("c").astype(jnp.int32)
    place = lax.axis_index("z").astype(jnp.int32)
    smem = pl.BlockSpec(memory_space=pltpu.SMEM)
    rows = chunks // (2 * ring) * CHUNK
    pair = 2 * depth
    halves = lax.all_to_all(partial.reshape(2, ring, rows, LANES), "c", 0, 0, tiled=True)
    going, query_half = kernel_call(
        lambda *refs: merge_kernel(depth, capacity, *refs),
        (shape((ring, rows + pair, LANES), f32), shape((TILES // 2, LANES), f32)),
        mib=8,
        in_specs=[smem] + [vmem] * 4,
    )(place.reshape(1), owner_map, row_map, exchange, halves)
    coming = lax.all_to_all(going, "r", 0, 0, tiled=True)
    query_half = lax.psum(query_half, "z")
    own = kernel_call(own_kernel, shape((ring, rows, LANES), f32), mib=8)(coming, query_half)
    half = lax.all_to_all(own, "r", 0, 0, tiled=True)

    arrived = coming[:, rows:].astype(bf16).reshape(ring, 2, depth, width)
    swap = [(0, 1), (1, 0)]
    crossed = lax.ppermute(jnp.where(core == 0, arrived[:, 1], arrived[:, 0]), "c", swap)
    kept = jnp.where(core == 0, arrived[:, 0], arrived[:, 1])
    tokens = jnp.where(
        core == 0, jnp.stack([kept, crossed], axis=1), jnp.stack([crossed, kept], axis=1)
    ).reshape(capacity, width)

    half, tokens, field_grad = lax.optimization_barrier((half, tokens, field_grad))
    other = lax.ppermute(half, "c", swap)
    weight_grad, bias_grad, query_grad = kernel_call(
        final_kernel,
        (shape((wide, D), f32), shape((var_local, D), f32), shape((H, DH), f32)),
        mib=8,
        in_specs=[smem, vmem, vmem],
    )(core.reshape(1), half, other)
    weight_grad = weight_grad.reshape(var_local, P_SIZE, D)
    return (tokens, field_grad, weight_grad, bias_grad, query_grad)


def solution(mesh):
    rows, groups = mesh.shape["rows"], mesh.shape["vars"]
    inner = Mesh(mesh.devices.reshape(rows // 2, 2, groups), ("r", "c", "z"))
    by_rows = ("r", "c")
    return jax.shard_map(
        local,
        mesh=inner,
        in_specs=(
            P("z", by_rows),
            P(by_rows, None),
            P(by_rows, None),
            P(by_rows, None),
            P("z", None, None),
            P("z", None),
            P(),
            P(by_rows, None),
        ),
        out_specs=(
            P(by_rows, "z"),
            P("z", by_rows),
            P("z", None, None),
            P("z", None),
            P(),
        ),
        check_vma=False,
    )
```

```python
import math

import jax
import jax.numpy as jnp
from jax import lax
from jax.experimental import pallas as pl
from jax.experimental.pallas import tpu as pltpu
from jax.sharding import Mesh
from jax.sharding import PartitionSpec as P

D = 1024
H = 16
DH = 64
P_SIZE = 16
K = 4
PTS_BLK = 1024
PB = 32
PIX_BLK = PB * P_SIZE
LANES = 128
TILES = D // LANES
CHUNK = 24
INTERPRET = False

f32 = jnp.float32
bf16 = jnp.bfloat16


def iota(shape, axis):
    return lax.broadcasted_iota(jnp.int32, shape, axis)


def dot(first, second):
    return lax.dot_general(first, second, (((1,), (0,)), ((), ())), preferred_element_type=f32)


def dot_t(first, second):
    return lax.dot_general(first, second, (((1,), (1,)), ((), ())), preferred_element_type=f32)


def split(value, parts):
    pieces = []
    for _ in range(parts):
        piece = value.astype(bf16)
        pieces.append(piece)
        value = value - piece.astype(f32)
    return pieces


def over_vars(value, join):
    shift = value.shape[1] // 2
    while shift >= H:
        value = join(value, pltpu.roll(value, shift, axis=1))
        shift //= 2
    return value


def group(value, v):
    return value[:, v * H : (v + 1) * H]


def kernel_call(body, out_shape, mib, scratch=(), in_specs=None, out_specs=None, aliases=None):
    extra = {}
    if in_specs is not None:
        extra["in_specs"] = in_specs
    if out_specs is not None:
        extra["out_specs"] = out_specs
    return pl.pallas_call(
        body,
        out_shape=out_shape,
        scratch_shapes=list(scratch),
        input_output_aliases=aliases or {},
        interpret=INTERPRET,
        compiler_params=pltpu.CompilerParams(vmem_limit_bytes=mib << 20),
        **extra,
    )


def interp_transposed(index_ref, weight_ref, block):
    where = pl.ds(block * PIX_BLK, PIX_BLK)
    index = [index_ref[k : k + 1, where] for k in range(K)]
    weight = [weight_ref[k : k + 1, where] for k in range(K)]
    points = iota((PTS_BLK, PIX_BLK), 0)
    matrix = jnp.zeros((PTS_BLK, PIX_BLK), f32)
    for k in range(K):
        total = jnp.zeros((1, PIX_BLK), f32)
        for j in range(K):
            total = total + jnp.where(index[j] == index[k], weight[j], 0.0)
        matrix = jnp.where(points == index[k], total, matrix)
    return matrix.astype(bf16)


def spread(rows, cols, test):
    return jnp.where(test(iota((rows, cols), 0), iota((rows, cols), 1)), 1.0, 0.0).astype(bf16)


def pixel_masks(var_local):
    wide = var_local * P_SIZE
    copy_rows = spread(wide, var_local, lambda r, c: r // P_SIZE == c)
    own_pixel = iota((wide, PIX_BLK), 0) % P_SIZE == iota((wide, PIX_BLK), 1) % P_SIZE
    return copy_rows, own_pixel


def head_expand(copies):
    return spread(copies * H, D, lambda r, c: r % H == c // DH)


def forward_kernel(
    index_ref, weight_ref, fields_ref, embed_ref, bias_ref, query_ref, x_ref, e_ref, s_ref, exch_ref, matrix_ref, sum_ref
):
    var_local = fields_ref.shape[0]
    blocks = fields_ref.shape[1] // PTS_BLK
    wide = var_local * P_SIZE
    copy_rows, own_pixel = pixel_masks(var_local)
    gather = spread(PB, PIX_BLK, lambda r, c: r == c // P_SIZE)
    for block in range(blocks):
        matrix = interp_transposed(index_ref, weight_ref, block)
        matrix_ref[block] = matrix
        pixels = dot(fields_ref[:, pl.ds(block * PTS_BLK, PTS_BLK)], matrix).astype(bf16)
        widened = jnp.where(own_pixel, dot(copy_rows, pixels), 0.0).astype(bf16)
        x_ref[pl.ds(block * PB, PB), :] = dot_t(gather, widened).astype(bf16)
    x_all = x_ref[...]
    patches = x_all.shape[0]
    var_of = iota((patches, wide), 1) // P_SIZE
    head_rows = iota((3 * H, D), 0) % H == iota((3 * H, D), 1) // DH
    parts = split(query_ref[...], 3)
    query_rows = jnp.concatenate(
        [jnp.broadcast_to(part.astype(f32), (H, D)) for part in parts], axis=0
    )
    query_rows = jnp.where(head_rows, query_rows, 0.0).astype(bf16)
    scores = []
    for v in range(var_local):
        own = jnp.where(var_of == v, x_all, jnp.zeros_like(x_all))
        embedded = (dot(own, embed_ref[...]) + bias_ref[v : v + 1, :].astype(f32)).astype(bf16)
        e_ref[v] = embedded
        three = dot_t(embedded, query_rows)
        scores.append(three[:, :H] + three[:, H : 2 * H] + three[:, 2 * H :])
    scores = jnp.concatenate(scores, axis=1) * (1.0 / math.sqrt(DH))
    s_ref[...] = scores
    weights = jnp.exp(scores - over_vars(scores, jnp.maximum))
    weights = split(weights / over_vars(weights, jnp.add), 2)
    expand = head_expand(2)
    for v in range(var_local):
        both = jnp.concatenate([group(part, v) for part in weights], axis=1)
        term = dot(both, expand) * e_ref[v].astype(f32)
        if v == 0:
            sum_ref[...] = term
        else:
            sum_ref[...] += term
    groups = exch_ref.shape[0]
    width = D // groups
    for g in range(groups):
        exch_ref[g, :patches, :] = sum_ref[:, g * width : (g + 1) * width]


def target_of(column_ref, row_ref, depth, as_row):
    column = column_ref[...]
    row = row_ref[...]
    count = column.shape[0]
    same = column == row
    first, second = iota((count, count), 0), iota((count, count), 1)
    if as_row:
        rank = jnp.sum(jnp.where(same & (first < second), 1.0, 0.0), axis=0, keepdims=True)
        return row * depth + rank.astype(jnp.int32)
    rank = jnp.sum(jnp.where(same & (second < first), 1.0, 0.0), axis=1, keepdims=True)
    return column * depth + rank.astype(jnp.int32)


def outbox_kernel(grad_ref, out_ref):
    out_ref[...] = grad_ref[...].reshape(out_ref.shape)


def stats_kernel(
    depth,
    column_ref,
    row_ref,
    inbox_ref,
    e_ref,
    s_ref,
    x_ref,
    old_ref,
    up_ref,
    both_ref,
    xt_ref,
    exch_ref,
    stats_ref,
    sems,
):
    patches = column_ref.shape[0]
    slots = inbox_ref.shape[0] * inbox_ref.shape[1]
    target = target_of(column_ref, row_ref, depth, False)
    pick = jnp.where(iota((patches, slots), 1) == target, 1.0, 0.0).astype(bf16)
    upstream = dot(pick, inbox_ref[...].reshape(slots, D))
    up_ref[...] = upstream.astype(bf16)
    reduce_heads = spread(D, H, lambda r, c: r // DH == c)
    var_local = e_ref.shape[0]
    grad_attn = []
    for v in range(var_local):
        high, low = split(upstream * e_ref[v].astype(f32), 2)
        grad_attn.append(dot(high, reduce_heads) + dot(low, reduce_heads))
    grad_attn = jnp.concatenate(grad_attn, axis=1)
    scores = s_ref[...]
    both_ref[0] = scores
    both_ref[1] = grad_attn
    xt_ref[...] = x_ref[...].astype(f32).T.astype(bf16)
    peak = over_vars(scores, jnp.maximum)
    weights = jnp.exp(scores - peak)
    total = over_vars(weights, jnp.add)
    inner = over_vars(weights * grad_attn, jnp.add) / total
    packed = [group(peak + jnp.log(total), 0), group(inner, 0)]
    packed = jnp.concatenate(packed + [jnp.zeros((patches, LANES - 2 * H), f32)], axis=1)
    if patches < LANES:
        packed = jnp.concatenate([packed, jnp.zeros((LANES - patches, LANES), f32)], axis=0)
    stats_ref[...] = packed.T[: 2 * H, :]
    copies = [
        pltpu.make_async_copy(stats_ref, exch_ref.at[g, pl.ds(patches, 2 * H)], sems.at[g])
        for g in range(exch_ref.shape[0])
    ]
    for copy in copies:
        copy.start()
    for copy in copies:
        copy.wait()


def combine_stats(exch_ref, patches):
    groups = exch_ref.shape[0]
    logs, inners = [], []
    for g in range(groups):
        stats = exch_ref[g, patches : patches + 2 * H, :]
        rows = jnp.concatenate([stats, jnp.zeros((LANES - 2 * H, LANES), f32)], axis=0).T
        rows = rows[:patches]
        logs.append(rows[:, :H])
        inners.append(rows[:, H : 2 * H])
    peak = logs[0]
    for other in logs[1:]:
        peak = jnp.maximum(peak, other)
    factors = [jnp.exp(one - peak) for one in logs]
    total = sum(factors)
    shares = [factor / total for factor in factors]
    inner = sum(f * t for f, t in zip(shares, inners))
    return peak, total, inner, shares


def tokens_kernel(depth, slots, place_ref, column_ref, row_ref, exch_ref, out_ref):
    patches = column_ref.shape[0]
    groups, _, width = exch_ref.shape
    _, _, _, shares = combine_stats(exch_ref, patches)
    heads = width // DH
    first = place_ref[0] * heads
    pick = jnp.where(
        iota((3 * H, width), 0) % H == first + iota((3 * H, width), 1) // DH, 1.0, 0.0
    ).astype(bf16)
    mixture = jnp.zeros((patches, width), f32)
    for g in range(groups):
        scale = jnp.concatenate(split(shares[g], 3), axis=1)
        mixture = mixture + dot(scale, pick) * exch_ref[g, :patches, :]
    target = target_of(column_ref, row_ref, depth, True)
    place = jnp.where(iota((slots, patches), 0) == target, 1.0, 0.0).astype(bf16)
    out_ref[...] = dot(place, mixture.astype(bf16))


def merge_kernel(kept_ref, crossed_ref, tokens_ref, going_ref, query_ref):
    ring, rows = kept_ref.shape[0], kept_ref.shape[1]
    going_ref[:, rows:, :] = tokens_ref[...].reshape(ring, tokens_ref.shape[0] // ring, LANES)
    going_ref[:, :rows, :] = kept_ref[...] + crossed_ref[...]
    share = rows // CHUNK
    for t in range(TILES // 2):
        at = (t % share) * CHUNK + P_SIZE + 1
        query_ref[t : t + 1, :] = going_ref[t // share, at : at + 1, :]


def own_kernel(coming_ref, query_ref, out_ref):
    ring, rows = out_ref.shape[0], out_ref.shape[1]
    own = coming_ref[0, :rows, :]
    for r in range(1, ring):
        own = own + coming_ref[r, :rows, :]
    spare = jnp.concatenate(
        [query_ref[...], jnp.zeros((CHUNK - P_SIZE - 1 - TILES // 2, LANES), f32)], axis=0
    )
    rest = [own[CHUNK:]] if rows > CHUNK else []
    own = jnp.concatenate([own[: P_SIZE + 1], spare] + rest, axis=0)
    for r in range(ring):
        out_ref[r] = own


def final_kernel(core_ref, half_ref, other_ref, weight_ref, bias_ref, query_ref):
    ring, rows = half_ref.shape[0], half_ref.shape[1]
    share = rows // CHUNK
    low = core_ref[0] == 0
    for c in range(2):
        query = jnp.zeros((TILES // 2, LANES), f32)
        for r in range(ring):
            half, other = half_ref[r], other_ref[r]
            block = jnp.where(low, half, other) if c == 0 else jnp.where(low, other, half)
            for k in range(share):
                v, t = divmod((c * ring + r) * share + k, TILES)
                cut = slice(t * LANES, (t + 1) * LANES)
                weight_ref[v * P_SIZE : (v + 1) * P_SIZE, cut] = block[k * CHUNK : k * CHUNK + P_SIZE]
                bias_ref[v : v + 1, cut] = block[k * CHUNK + P_SIZE : k * CHUNK + P_SIZE + 1]
            query = query + block[P_SIZE + 1 : P_SIZE + 1 + TILES // 2]
        for t in range(TILES // 2):
            at = (c * (TILES // 2) + t) * 2
            query_ref[at : at + 1, :] = query[t : t + 1, :DH]
            query_ref[at + 1 : at + 2, :] = query[t : t + 1, DH:]


def backward_kernel(
    core_ref, exch_ref, both_ref, up_ref, xt_ref, embed_ref, bias_ref, query_ref, kept_ref, send_ref, gx_ref, wide_ref
):
    wide, patches = xt_ref.shape
    var_local = wide // P_SIZE
    peak, total, inner, _ = combine_stats(exch_ref, patches)
    peak, inner, inverse = (
        jnp.concatenate([one] * var_local, axis=1) for one in (peak, inner, 1.0 / total)
    )
    attention = jnp.exp(both_ref[0] - peak) * inverse
    grad_score = attention * (both_ref[1] - inner) * (1.0 / math.sqrt(DH))
    attention = split(attention, 2)
    high, low = split(grad_score, 2)
    turned = [part.astype(f32).T.astype(bf16) for part in (high, low)]
    expand = head_expand(2)
    query = query_ref[...]
    q_parts = split(query, 3)
    rows = [q_parts[0], q_parts[1], q_parts[2], q_parts[0], q_parts[1], q_parts[2]]
    query_rows = jnp.concatenate([jnp.broadcast_to(r.astype(f32), (H, D)) for r in rows], axis=0)
    on_head = iota((6 * H, D), 0) % H == iota((6 * H, D), 1) // DH
    query_rows = jnp.where(on_head, query_rows, 0.0).astype(bf16)
    upstream = up_ref[...].astype(f32)
    x_t = xt_ref[...]
    x_all = x_t.astype(f32).T.astype(bf16)
    embed_t = embed_ref[...].astype(f32).T.astype(bf16)
    lane_var = iota((patches, wide), 1) // P_SIZE
    grad_x = jnp.zeros((patches, wide), f32)
    query_sum = jnp.zeros((2 * H, D), f32)
    for v in range(var_local):
        attn = jnp.concatenate([group(part, v) for part in attention], axis=1)
        first, second = group(high, v), group(low, v)
        scored = jnp.concatenate([first, first, first, second, second, second], axis=1)
        grad = dot(attn, expand) * upstream + dot(scored, query_rows)
        low_grad = grad.astype(bf16)
        bias_row = jnp.sum(grad, axis=0, keepdims=True)
        weight_rows = dot(x_t[v * P_SIZE : (v + 1) * P_SIZE, :], low_grad)
        for t in range(TILES):
            cut = slice(t * LANES, (t + 1) * LANES)
            wide_ref[v * TILES + t, :P_SIZE, :] = weight_rows[:, cut]
            wide_ref[v * TILES + t, P_SIZE : P_SIZE + 1, :] = bias_row[:, cut]
        grad_x = jnp.where(lane_var == v, dot(low_grad, embed_t), grad_x)
        pair = jnp.concatenate([part[v * H : (v + 1) * H] for part in turned], axis=0)
        own = jnp.where(lane_var == v, x_all, jnp.zeros_like(x_all))
        embedded = (dot(own, embed_ref[...]) + bias_ref[v : v + 1, :].astype(f32)).astype(bf16)
        query_sum = query_sum + dot(pair, embedded)
    gx_ref[...] = grad_x.astype(bf16)
    diagonal = iota((2 * H, D), 0) % H == iota((2 * H, D), 1) // DH
    query_row = jnp.sum(jnp.where(diagonal, query_sum, 0.0), axis=0, keepdims=True)
    half = wide_ref.shape[0] // 2
    for t in range(TILES):
        at = (t // (TILES // 2)) * half + t % (TILES // 2)
        wide_ref[at, P_SIZE + 1 : P_SIZE + 2, :] = query_row[:, t * LANES : (t + 1) * LANES]
    core = core_ref[0]
    kept_ref[...] = wide_ref[pl.ds(core * half, half)].reshape(kept_ref.shape)
    send_ref[...] = wide_ref[pl.ds((1 - core) * half, half)].reshape(send_ref.shape)


def field_kernel(matrix_ref, gx_ref, out_ref):
    wide = gx_ref.shape[1]
    var_local = wide // P_SIZE
    blocks = gx_ref.shape[0] // PB
    gx_t = gx_ref[...].astype(f32).T.astype(bf16)
    fold = spread(var_local, wide, lambda r, c: c // P_SIZE == r)
    own_pixel = iota((wide, PIX_BLK), 0) % P_SIZE == iota((wide, PIX_BLK), 1) % P_SIZE
    copy = spread(PB, PIX_BLK, lambda r, c: r == c // P_SIZE)
    for block in range(blocks):
        wide_grad = dot(gx_t[:, block * PB : (block + 1) * PB], copy)
        wide_grad = jnp.where(own_pixel, wide_grad, 0.0).astype(bf16)
        grad = dot(fold, wide_grad).astype(bf16)
        out_ref[:, pl.ds(block * PTS_BLK, PTS_BLK)] = dot_t(grad, matrix_ref[block])


def local(
    fields, stencil, stencil_weight, owner_map, embed_weight, embed_bias, agg_query, out_grad
):
    by_rows = ("r", "c")
    ring = lax.axis_size("r")
    groups = lax.axis_size("z")
    row_devices = ring * 2
    var_local = fields.shape[0]
    patches = owner_map.shape[0]
    capacity = out_grad.shape[0]
    depth = capacity // row_devices
    width = D // groups
    wide = var_local * P_SIZE
    shape = jax.ShapeDtypeStruct

    inbox = lax.all_to_all(
        kernel_call(outbox_kernel, shape((row_devices, depth, D), bf16), mib=8)(out_grad),
        by_rows,
        split_axis=0,
        concat_axis=0,
        tiled=True,
    )

    index_t = stencil.T
    weight_t = stencil_weight.T
    embed_flat = embed_weight.reshape(wide, D)
    query = agg_query.reshape(1, D)
    row_map = owner_map.reshape(1, patches)
    x_all, embedded, scores, sums, matrix = kernel_call(
        forward_kernel,
        (
            shape((patches, wide), bf16),
            shape((var_local, patches, D), bf16),
            shape((patches, var_local * H), f32),
            shape((groups, patches + 2 * H, width), f32),
            shape((fields.shape[1] // PTS_BLK, PTS_BLK, PIX_BLK), bf16),
        ),
        mib=20,
        scratch=[pltpu.VMEM((patches, D), f32)],
    )(index_t, weight_t, fields, embed_flat, embed_bias, query)

    vmem = pl.BlockSpec(memory_space=pltpu.VMEM)
    anywhere = pl.BlockSpec(memory_space=pl.ANY)
    upstream, both, x_turned, exchange = kernel_call(
        lambda *refs: stats_kernel(depth, *refs),
        (
            shape((patches, D), bf16),
            shape((2, patches, var_local * H), f32),
            shape((wide, patches), bf16),
            shape(sums.shape, f32),
        ),
        mib=12,
        scratch=[pltpu.VMEM((2 * H, LANES), f32), pltpu.SemaphoreType.DMA((groups,))],
        in_specs=[vmem] * 6 + [anywhere],
        out_specs=(vmem, vmem, vmem, anywhere),
        aliases={6: 3},
    )(owner_map, row_map, inbox, embedded, scores, x_all, sums)
    exchange = lax.all_to_all(exchange, "z", 0, 0, tiled=True)

    core = lax.axis_index("c").astype(jnp.int32)
    place = lax.axis_index("z").astype(jnp.int32)
    smem = pl.BlockSpec(memory_space=pltpu.SMEM)
    swap = [(0, 1), (1, 0)]
    chunks = var_local * TILES
    rows = chunks // (2 * ring) * CHUNK
    pair = 2 * depth
    kept, sent, grad_x = kernel_call(
        backward_kernel,
        (
            shape((ring, rows, LANES), f32),
            shape((ring, rows, LANES), f32),
            shape((patches, wide), bf16),
        ),
        mib=16,
        scratch=[pltpu.VMEM((chunks, CHUNK, LANES), f32)],
        in_specs=[smem] + [vmem] * 7,
    )(core.reshape(1), exchange, both, upstream, x_turned, embed_flat, embed_bias, query)
    crossed = lax.ppermute(sent, "c", swap)
    outbox = kernel_call(
        lambda *refs: tokens_kernel(depth, capacity, *refs),
        shape((capacity, width), f32),
        mib=8,
        in_specs=[smem] + [vmem] * 3,
    )(place.reshape(1), owner_map, row_map, exchange)
    crossed, outbox = lax.optimization_barrier((crossed, outbox))
    going, query_half = kernel_call(
        merge_kernel,
        (shape((ring, rows + pair, LANES), f32), shape((TILES // 2, LANES), f32)),
        mib=8,
    )(kept, crossed, outbox)

    field_grad = kernel_call(field_kernel, shape((var_local, fields.shape[1]), f32), mib=16)(
        matrix, grad_x
    )

    coming = lax.all_to_all(going, "r", 0, 0, tiled=True)
    query_half = lax.psum(query_half, "z")
    own = kernel_call(own_kernel, shape((ring, rows, LANES), f32), mib=8)(coming, query_half)
    half = lax.all_to_all(own, "r", 0, 0, tiled=True)

    arrived = coming[:, rows:].astype(bf16).reshape(ring, 2, depth, width)
    crossed = lax.ppermute(jnp.where(core == 0, arrived[:, 1], arrived[:, 0]), "c", swap)
    kept = jnp.where(core == 0, arrived[:, 0], arrived[:, 1])
    tokens = jnp.where(
        core == 0, jnp.stack([kept, crossed], axis=1), jnp.stack([crossed, kept], axis=1)
    ).reshape(capacity, width)

    half, tokens, field_grad = lax.optimization_barrier((half, tokens, field_grad))
    other = lax.ppermute(half, "c", swap)
    weight_grad, bias_grad, query_grad = kernel_call(
        final_kernel,
        (shape((wide, D), f32), shape((var_local, D), f32), shape((H, DH), f32)),
        mib=8,
        in_specs=[smem, vmem, vmem],
    )(core.reshape(1), half, other)
    weight_grad = weight_grad.reshape(var_local, P_SIZE, D)
    return (tokens, field_grad, weight_grad, bias_grad, query_grad)


def solution(mesh):
    rows, groups = mesh.shape["rows"], mesh.shape["vars"]
    inner = Mesh(mesh.devices.reshape(rows // 2, 2, groups), ("r", "c", "z"))
    by_rows = ("r", "c")
    return jax.shard_map(
        local,
        mesh=inner,
        in_specs=(
            P("z", by_rows),
            P(by_rows, None),
            P(by_rows, None),
            P(by_rows, None),
            P("z", None, None),
            P("z", None),
            P(),
            P(by_rows, None),
        ),
        out_specs=(
            P(by_rows, "z"),
            P("z", by_rows),
            P("z", None, None),
            P("z", None),
            P(),
        ),
        check_vma=False,
    )
```

```python
import math

import jax
import jax.numpy as jnp
from jax import lax
from jax.experimental import pallas as pl
from jax.experimental.pallas import tpu as pltpu
from jax.sharding import Mesh
from jax.sharding import PartitionSpec as P

D = 1024
H = 16
DH = 64
P_SIZE = 16
K = 4
PTS_BLK = 1024
PB = 32
PIX_BLK = PB * P_SIZE
LANES = 128
TILES = D // LANES
CHUNK = 24
STATS = 80
STEPS = 128.0
FULL = 32600.0
i16 = jnp.int16
i32 = jnp.int32
INTERPRET = False

f32 = jnp.float32
bf16 = jnp.bfloat16


def iota(shape, axis):
    return lax.broadcasted_iota(jnp.int32, shape, axis)


def dot(first, second):
    return lax.dot_general(first, second, (((1,), (0,)), ((), ())), preferred_element_type=f32)


def dot_t(first, second):
    return lax.dot_general(first, second, (((1,), (1,)), ((), ())), preferred_element_type=f32)


def split(value, parts):
    pieces = []
    for _ in range(parts):
        piece = value.astype(bf16)
        pieces.append(piece)
        value = value - piece.astype(f32)
    return pieces


def over_vars(value, join):
    shift = value.shape[1] // 2
    while shift >= H:
        value = join(value, pltpu.roll(value, shift, axis=1))
        shift //= 2
    return value


def group(value, v):
    return value[:, v * H : (v + 1) * H]


def scale_code(value):
    most = jnp.max(jnp.abs(value), axis=1, keepdims=True)
    return jnp.floor(jnp.log(jnp.maximum(most, 1e-30)) * STEPS) + 1.0


def two_words(value):
    code = scale_code(value)
    fixed = jnp.round(value * (jnp.exp(code * (-1.0 / STEPS)) * 2.0**30)).astype(i32)
    low = (fixed & 0xFFFF) - 0x8000
    return (fixed >> 16).astype(f32), low.astype(f32), code


def from_words(high, low, code):
    return (high * 65536.0 + (low + 32768.0)) * (jnp.exp(code * (1.0 / STEPS)) * 2.0**-30)


def kernel_call(body, out_shape, mib, scratch=(), in_specs=None, out_specs=None, aliases=None):
    extra = {}
    if in_specs is not None:
        extra["in_specs"] = in_specs
    if out_specs is not None:
        extra["out_specs"] = out_specs
    return pl.pallas_call(
        body,
        out_shape=out_shape,
        scratch_shapes=list(scratch),
        input_output_aliases=aliases or {},
        interpret=INTERPRET,
        compiler_params=pltpu.CompilerParams(vmem_limit_bytes=mib << 20),
        **extra,
    )


def interp_transposed(index_ref, weight_ref, block):
    where = pl.ds(block * PIX_BLK, PIX_BLK)
    index = [index_ref[k : k + 1, where] for k in range(K)]
    weight = [weight_ref[k : k + 1, where] for k in range(K)]
    points = iota((PTS_BLK, PIX_BLK), 0)
    matrix = jnp.zeros((PTS_BLK, PIX_BLK), f32)
    for k in range(K):
        total = jnp.zeros((1, PIX_BLK), f32)
        for j in range(K):
            total = total + jnp.where(index[j] == index[k], weight[j], 0.0)
        matrix = jnp.where(points == index[k], total, matrix)
    return matrix.astype(bf16)


def spread(rows, cols, test):
    return jnp.where(test(iota((rows, cols), 0), iota((rows, cols), 1)), 1.0, 0.0).astype(bf16)


def pixel_masks(var_local):
    wide = var_local * P_SIZE
    copy_rows = spread(wide, var_local, lambda r, c: r // P_SIZE == c)
    own_pixel = iota((wide, PIX_BLK), 0) % P_SIZE == iota((wide, PIX_BLK), 1) % P_SIZE
    return copy_rows, own_pixel


def head_expand(copies):
    return spread(copies * H, D, lambda r, c: r % H == c // DH)


def forward_kernel(
    index_ref, weight_ref, fields_ref, embed_ref, bias_ref, query_ref, x_ref, e_ref, s_ref, exch_ref, code_ref, sum_ref
):
    var_local = fields_ref.shape[0]
    blocks = fields_ref.shape[1] // PTS_BLK
    wide = var_local * P_SIZE
    copy_rows, own_pixel = pixel_masks(var_local)
    gather = spread(PB, PIX_BLK, lambda r, c: r == c // P_SIZE)
    for block in range(blocks):
        matrix = interp_transposed(index_ref, weight_ref, block)
        pixels = dot(fields_ref[:, pl.ds(block * PTS_BLK, PTS_BLK)], matrix).astype(bf16)
        widened = jnp.where(own_pixel, dot(copy_rows, pixels), 0.0).astype(bf16)
        x_ref[pl.ds(block * PB, PB), :] = dot_t(gather, widened).astype(bf16)
    x_all = x_ref[...]
    patches = x_all.shape[0]
    var_of = iota((patches, wide), 1) // P_SIZE
    head_rows = iota((3 * H, D), 0) % H == iota((3 * H, D), 1) // DH
    parts = split(query_ref[...], 3)
    query_rows = jnp.concatenate(
        [jnp.broadcast_to(part.astype(f32), (H, D)) for part in parts], axis=0
    )
    query_rows = jnp.where(head_rows, query_rows, 0.0).astype(bf16)
    scores = []
    for v in range(var_local):
        own = jnp.where(var_of == v, x_all, jnp.zeros_like(x_all))
        embedded = (dot(own, embed_ref[...]) + bias_ref[v : v + 1, :].astype(f32)).astype(bf16)
        e_ref[v] = embedded
        three = dot_t(embedded, query_rows)
        scores.append(three[:, :H] + three[:, H : 2 * H] + three[:, 2 * H :])
    scores = jnp.concatenate(scores, axis=1) * (1.0 / math.sqrt(DH))
    s_ref[...] = scores
    weights = jnp.exp(scores - over_vars(scores, jnp.maximum))
    weights = split(weights / over_vars(weights, jnp.add), 2)
    expand = head_expand(2)
    for v in range(var_local):
        both = jnp.concatenate([group(part, v) for part in weights], axis=1)
        term = dot(both, expand) * e_ref[v].astype(f32)
        if v == 0:
            sum_ref[...] = term
        else:
            sum_ref[...] += term
    groups = exch_ref.shape[0]
    width = D // groups
    codes = []
    for g in range(groups):
        part = sum_ref[:, g * width : (g + 1) * width]
        code = scale_code(part)
        coded = jnp.round(part * (jnp.exp(code * (-1.0 / STEPS)) * FULL))
        exch_ref[g, :patches, :] = coded.astype(i32).astype(i16)
        codes.append(code)
    codes = jnp.concatenate(codes + [jnp.zeros((patches, LANES - groups), f32)], axis=1)
    if patches < LANES:
        codes = jnp.concatenate([codes, jnp.zeros((LANES - patches, LANES), f32)], axis=0)
    code_ref[...] = codes.T[:groups, :]


def target_of(column_ref, row_ref, depth, as_row):
    column = column_ref[...]
    row = row_ref[...]
    count = column.shape[0]
    same = column == row
    first, second = iota((count, count), 0), iota((count, count), 1)
    if as_row:
        rank = jnp.sum(jnp.where(same & (first < second), 1.0, 0.0), axis=0, keepdims=True)
        return row * depth + rank.astype(jnp.int32)
    rank = jnp.sum(jnp.where(same & (second < first), 1.0, 0.0), axis=1, keepdims=True)
    return column * depth + rank.astype(jnp.int32)


def outbox_kernel(grad_ref, out_ref):
    out_ref[...] = grad_ref[...].reshape(out_ref.shape)


def stats_kernel(
    depth,
    column_ref,
    row_ref,
    inbox_ref,
    e_ref,
    s_ref,
    x_ref,
    code_ref,
    old_ref,
    up_ref,
    both_ref,
    xt_ref,
    exch_ref,
    stats_ref,
    sems,
):
    patches = column_ref.shape[0]
    slots = inbox_ref.shape[0] * inbox_ref.shape[1]
    target = target_of(column_ref, row_ref, depth, False)
    pick = jnp.where(iota((patches, slots), 1) == target, 1.0, 0.0).astype(bf16)
    upstream = dot(pick, inbox_ref[...].reshape(slots, D))
    up_ref[...] = upstream.astype(bf16)
    reduce_heads = spread(D, H, lambda r, c: r // DH == c)
    var_local = e_ref.shape[0]
    grad_attn = []
    for v in range(var_local):
        high, low = split(upstream * e_ref[v].astype(f32), 2)
        grad_attn.append(dot(high, reduce_heads) + dot(low, reduce_heads))
    grad_attn = jnp.concatenate(grad_attn, axis=1)
    scores = s_ref[...]
    both_ref[0] = scores
    both_ref[1] = grad_attn
    xt_ref[...] = x_ref[...].astype(f32).T.astype(bf16)
    peak = over_vars(scores, jnp.maximum)
    weights = jnp.exp(scores - peak)
    total = over_vars(weights, jnp.add)
    inner = over_vars(weights * grad_attn, jnp.add) / total
    log_words = two_words(group(peak + jnp.log(total), 0))
    inner_words = two_words(group(inner, 0))
    packed = [*log_words[:2], *inner_words[:2], log_words[2], inner_words[2]]
    packed = jnp.concatenate(packed + [jnp.zeros((patches, LANES - 4 * H - 2), f32)], axis=1)
    if patches < LANES:
        packed = jnp.concatenate([packed, jnp.zeros((LANES - patches, LANES), f32)], axis=0)
    turned = packed.T[:STATS, :]
    row = iota((STATS, LANES), 0)
    copies = []
    for g in range(exch_ref.shape[0]):
        one = jnp.where(row == 4 * H + 2, code_ref[g : g + 1, :], turned)
        stats_ref[g] = one.astype(i32).astype(i16)
        copies.append(
            pltpu.make_async_copy(
                stats_ref.at[g], exch_ref.at[g, pl.ds(patches, STATS)], sems.at[g]
            )
        )
        copies[-1].start()
    for copy in copies:
        copy.wait()


def combine_stats(exch_ref, patches):
    groups = exch_ref.shape[0]
    logs, inners, scales = [], [], []
    for g in range(groups):
        stats = exch_ref[g, patches : patches + STATS, :].astype(i32).astype(f32)
        rows = jnp.concatenate([stats, jnp.zeros((LANES - STATS, LANES), f32)], axis=0).T
        rows = rows[:patches]
        at = 4 * H
        logs.append(from_words(rows[:, :H], rows[:, H : 2 * H], rows[:, at : at + 1]))
        inners.append(
            from_words(rows[:, 2 * H : 3 * H], rows[:, 3 * H : at], rows[:, at + 1 : at + 2])
        )
        scales.append(jnp.exp(rows[:, at + 2 : at + 3] * (1.0 / STEPS)) * (1.0 / FULL))
    peak = logs[0]
    for other in logs[1:]:
        peak = jnp.maximum(peak, other)
    factors = [jnp.exp(one - peak) for one in logs]
    total = sum(factors)
    shares = [factor / total for factor in factors]
    inner = sum(f * t for f, t in zip(shares, inners))
    return peak, total, inner, [share * scale for share, scale in zip(shares, scales)]


def tokens_kernel(depth, slots, place_ref, column_ref, row_ref, exch_ref, out_ref):
    patches = column_ref.shape[0]
    groups, _, width = exch_ref.shape
    _, _, _, shares = combine_stats(exch_ref, patches)
    heads = width // DH
    first = place_ref[0] * heads
    pick = jnp.where(
        iota((3 * H, width), 0) % H == first + iota((3 * H, width), 1) // DH, 1.0, 0.0
    ).astype(bf16)
    mixture = jnp.zeros((patches, width), f32)
    for g in range(groups):
        scale = jnp.concatenate(split(shares[g], 3), axis=1)
        mixture = mixture + dot(scale, pick) * exch_ref[g, :patches, :].astype(i32).astype(f32)
    target = target_of(column_ref, row_ref, depth, True)
    place = jnp.where(iota((slots, patches), 0) == target, 1.0, 0.0).astype(bf16)
    out_ref[...] = dot(place, mixture.astype(bf16))


def merge_kernel(kept_ref, crossed_ref, tokens_ref, going_ref, query_ref):
    ring, rows = kept_ref.shape[0], kept_ref.shape[1]
    going_ref[:, rows:, :] = tokens_ref[...].reshape(ring, tokens_ref.shape[0] // ring, LANES)
    going_ref[:, :rows, :] = kept_ref[...] + crossed_ref[...]
    share = rows // CHUNK
    for t in range(TILES // 2):
        at = (t % share) * CHUNK + P_SIZE + 1
        query_ref[t : t + 1, :] = going_ref[t // share, at : at + 1, :]


def own_kernel(coming_ref, query_ref, out_ref):
    ring, rows = out_ref.shape[0], out_ref.shape[1]
    own = coming_ref[0, :rows, :]
    for r in range(1, ring):
        own = own + coming_ref[r, :rows, :]
    spare = jnp.concatenate(
        [query_ref[...], jnp.zeros((CHUNK - P_SIZE - 1 - TILES // 2, LANES), f32)], axis=0
    )
    rest = [own[CHUNK:]] if rows > CHUNK else []
    own = jnp.concatenate([own[: P_SIZE + 1], spare] + rest, axis=0)
    for r in range(ring):
        out_ref[r] = own


def final_kernel(core_ref, half_ref, other_ref, weight_ref, bias_ref, query_ref):
    ring, rows = half_ref.shape[0], half_ref.shape[1]
    share = rows // CHUNK
    low = core_ref[0] == 0
    for c in range(2):
        query = jnp.zeros((TILES // 2, LANES), f32)
        for r in range(ring):
            half, other = half_ref[r], other_ref[r]
            block = jnp.where(low, half, other) if c == 0 else jnp.where(low, other, half)
            for k in range(share):
                v, t = divmod((c * ring + r) * share + k, TILES)
                cut = slice(t * LANES, (t + 1) * LANES)
                weight_ref[v * P_SIZE : (v + 1) * P_SIZE, cut] = block[k * CHUNK : k * CHUNK + P_SIZE]
                bias_ref[v : v + 1, cut] = block[k * CHUNK + P_SIZE : k * CHUNK + P_SIZE + 1]
            query = query + block[P_SIZE + 1 : P_SIZE + 1 + TILES // 2]
        for t in range(TILES // 2):
            at = (c * (TILES // 2) + t) * 2
            query_ref[at : at + 1, :] = query[t : t + 1, :DH]
            query_ref[at + 1 : at + 2, :] = query[t : t + 1, DH:]


def backward_kernel(
    core_ref, exch_ref, both_ref, up_ref, xt_ref, embed_ref, bias_ref, query_ref, kept_ref, send_ref, gx_ref, wide_ref
):
    wide, patches = xt_ref.shape
    var_local = wide // P_SIZE
    peak, total, inner, _ = combine_stats(exch_ref, patches)
    peak, inner, inverse = (
        jnp.concatenate([one] * var_local, axis=1) for one in (peak, inner, 1.0 / total)
    )
    attention = jnp.exp(both_ref[0] - peak) * inverse
    grad_score = attention * (both_ref[1] - inner) * (1.0 / math.sqrt(DH))
    attention = split(attention, 2)
    high, low = split(grad_score, 2)
    turned = [part.astype(f32).T.astype(bf16) for part in (high, low)]
    expand = head_expand(2)
    query = query_ref[...]
    q_parts = split(query, 3)
    rows = [q_parts[0], q_parts[1], q_parts[2], q_parts[0], q_parts[1], q_parts[2]]
    query_rows = jnp.concatenate([jnp.broadcast_to(r.astype(f32), (H, D)) for r in rows], axis=0)
    on_head = iota((6 * H, D), 0) % H == iota((6 * H, D), 1) // DH
    query_rows = jnp.where(on_head, query_rows, 0.0).astype(bf16)
    upstream = up_ref[...].astype(f32)
    x_t = xt_ref[...]
    x_all = x_t.astype(f32).T.astype(bf16)
    embed_t = embed_ref[...].astype(f32).T.astype(bf16)
    lane_var = iota((patches, wide), 1) // P_SIZE
    grad_x = jnp.zeros((patches, wide), f32)
    query_sum = jnp.zeros((2 * H, D), f32)
    for v in range(var_local):
        attn = jnp.concatenate([group(part, v) for part in attention], axis=1)
        first, second = group(high, v), group(low, v)
        scored = jnp.concatenate([first, first, first, second, second, second], axis=1)
        grad = dot(attn, expand) * upstream + dot(scored, query_rows)
        low_grad = grad.astype(bf16)
        bias_row = jnp.sum(grad, axis=0, keepdims=True)
        weight_rows = dot(x_t[v * P_SIZE : (v + 1) * P_SIZE, :], low_grad)
        for t in range(TILES):
            cut = slice(t * LANES, (t + 1) * LANES)
            wide_ref[v * TILES + t, :P_SIZE, :] = weight_rows[:, cut]
            wide_ref[v * TILES + t, P_SIZE : P_SIZE + 1, :] = bias_row[:, cut]
        grad_x = jnp.where(lane_var == v, dot(low_grad, embed_t), grad_x)
        pair = jnp.concatenate([part[v * H : (v + 1) * H] for part in turned], axis=0)
        own = jnp.where(lane_var == v, x_all, jnp.zeros_like(x_all))
        embedded = (dot(own, embed_ref[...]) + bias_ref[v : v + 1, :].astype(f32)).astype(bf16)
        query_sum = query_sum + dot(pair, embedded)
    gx_ref[...] = grad_x.astype(bf16)
    diagonal = iota((2 * H, D), 0) % H == iota((2 * H, D), 1) // DH
    query_row = jnp.sum(jnp.where(diagonal, query_sum, 0.0), axis=0, keepdims=True)
    half = wide_ref.shape[0] // 2
    for t in range(TILES):
        at = (t // (TILES // 2)) * half + t % (TILES // 2)
        wide_ref[at, P_SIZE + 1 : P_SIZE + 2, :] = query_row[:, t * LANES : (t + 1) * LANES]
    core = core_ref[0]
    kept_ref[...] = wide_ref[pl.ds(core * half, half)].reshape(kept_ref.shape)
    send_ref[...] = wide_ref[pl.ds((1 - core) * half, half)].reshape(send_ref.shape)


def field_kernel(index_ref, weight_ref, gx_ref, out_ref):
    wide = gx_ref.shape[1]
    var_local = wide // P_SIZE
    blocks = gx_ref.shape[0] // PB
    gx_t = gx_ref[...].astype(f32).T.astype(bf16)
    fold = spread(var_local, wide, lambda r, c: c // P_SIZE == r)
    own_pixel = iota((wide, PIX_BLK), 0) % P_SIZE == iota((wide, PIX_BLK), 1) % P_SIZE
    copy = spread(PB, PIX_BLK, lambda r, c: r == c // P_SIZE)
    for block in range(blocks):
        wide_grad = dot(gx_t[:, block * PB : (block + 1) * PB], copy)
        wide_grad = jnp.where(own_pixel, wide_grad, 0.0).astype(bf16)
        grad = dot(fold, wide_grad).astype(bf16)
        out_ref[:, pl.ds(block * PTS_BLK, PTS_BLK)] = dot_t(
            grad, interp_transposed(index_ref, weight_ref, block)
        )


def local(
    fields, stencil, stencil_weight, owner_map, embed_weight, embed_bias, agg_query, out_grad
):
    by_rows = ("r", "c")
    ring = lax.axis_size("r")
    groups = lax.axis_size("z")
    row_devices = ring * 2
    var_local = fields.shape[0]
    patches = owner_map.shape[0]
    capacity = out_grad.shape[0]
    depth = capacity // row_devices
    width = D // groups
    wide = var_local * P_SIZE
    shape = jax.ShapeDtypeStruct

    inbox = lax.all_to_all(
        kernel_call(outbox_kernel, shape((row_devices, depth, D), bf16), mib=8)(out_grad),
        by_rows,
        split_axis=0,
        concat_axis=0,
        tiled=True,
    )

    index_t = stencil.T
    weight_t = stencil_weight.T
    embed_flat = embed_weight.reshape(wide, D)
    query = agg_query.reshape(1, D)
    row_map = owner_map.reshape(1, patches)
    x_all, embedded, scores, sums, codes = kernel_call(
        forward_kernel,
        (
            shape((patches, wide), bf16),
            shape((var_local, patches, D), bf16),
            shape((patches, var_local * H), f32),
            shape((groups, patches + STATS, width), i16),
            shape((groups, LANES), f32),
        ),
        mib=20,
        scratch=[pltpu.VMEM((patches, D), f32)],
    )(index_t, weight_t, fields, embed_flat, embed_bias, query)

    vmem = pl.BlockSpec(memory_space=pltpu.VMEM)
    anywhere = pl.BlockSpec(memory_space=pl.ANY)
    upstream, both, x_turned, exchange = kernel_call(
        lambda *refs: stats_kernel(depth, *refs),
        (
            shape((patches, D), bf16),
            shape((2, patches, var_local * H), f32),
            shape((wide, patches), bf16),
            shape(sums.shape, i16),
        ),
        mib=12,
        scratch=[pltpu.VMEM((groups, STATS, LANES), i16), pltpu.SemaphoreType.DMA((groups,))],
        in_specs=[vmem] * 7 + [anywhere],
        out_specs=(vmem, vmem, vmem, anywhere),
        aliases={7: 3},
    )(owner_map, row_map, inbox, embedded, scores, x_all, codes, sums)
    exchange = lax.all_to_all(exchange, "z", 0, 0, tiled=True)

    core = lax.axis_index("c").astype(jnp.int32)
    place = lax.axis_index("z").astype(jnp.int32)
    smem = pl.BlockSpec(memory_space=pltpu.SMEM)
    swap = [(0, 1), (1, 0)]
    chunks = var_local * TILES
    rows = chunks // (2 * ring) * CHUNK
    pair = 2 * depth
    kept, sent, grad_x = kernel_call(
        backward_kernel,
        (
            shape((ring, rows, LANES), f32),
            shape((ring, rows, LANES), f32),
            shape((patches, wide), bf16),
        ),
        mib=16,
        scratch=[pltpu.VMEM((chunks, CHUNK, LANES), f32)],
        in_specs=[smem] + [vmem] * 7,
    )(core.reshape(1), exchange, both, upstream, x_turned, embed_flat, embed_bias, query)
    crossed = lax.ppermute(sent, "c", swap)
    outbox = kernel_call(
        lambda *refs: tokens_kernel(depth, capacity, *refs),
        shape((capacity, width), f32),
        mib=8,
        in_specs=[smem] + [vmem] * 3,
    )(place.reshape(1), owner_map, row_map, exchange)
    crossed, outbox = lax.optimization_barrier((crossed, outbox))
    going, query_half = kernel_call(
        merge_kernel,
        (shape((ring, rows + pair, LANES), f32), shape((TILES // 2, LANES), f32)),
        mib=8,
    )(kept, crossed, outbox)

    field_grad = kernel_call(field_kernel, shape((var_local, fields.shape[1]), f32), mib=16)(
        index_t, weight_t, grad_x
    )

    coming = lax.all_to_all(going, "r", 0, 0, tiled=True)
    query_half = lax.psum(query_half, "z")
    own = kernel_call(own_kernel, shape((ring, rows, LANES), f32), mib=8)(coming, query_half)
    half = lax.all_to_all(own, "r", 0, 0, tiled=True)

    arrived = coming[:, rows:].astype(bf16).reshape(ring, 2, depth, width)
    crossed = lax.ppermute(jnp.where(core == 0, arrived[:, 1], arrived[:, 0]), "c", swap)
    kept = jnp.where(core == 0, arrived[:, 0], arrived[:, 1])
    tokens = jnp.where(
        core == 0, jnp.stack([kept, crossed], axis=1), jnp.stack([crossed, kept], axis=1)
    ).reshape(capacity, width)

    half, tokens, field_grad = lax.optimization_barrier((half, tokens, field_grad))
    other = lax.ppermute(half, "c", swap)
    weight_grad, bias_grad, query_grad = kernel_call(
        final_kernel,
        (shape((wide, D), f32), shape((var_local, D), f32), shape((H, DH), f32)),
        mib=8,
        in_specs=[smem, vmem, vmem],
    )(core.reshape(1), half, other)
    weight_grad = weight_grad.reshape(var_local, P_SIZE, D)
    return (tokens, field_grad, weight_grad, bias_grad, query_grad)


def solution(mesh):
    rows, groups = mesh.shape["rows"], mesh.shape["vars"]
    inner = Mesh(mesh.devices.reshape(rows // 2, 2, groups), ("r", "c", "z"))
    by_rows = ("r", "c")
    return jax.shard_map(
        local,
        mesh=inner,
        in_specs=(
            P("z", by_rows),
            P(by_rows, None),
            P(by_rows, None),
            P(by_rows, None),
            P("z", None, None),
            P("z", None),
            P(),
            P(by_rows, None),
        ),
        out_specs=(
            P(by_rows, "z"),
            P("z", by_rows),
            P("z", None, None),
            P("z", None),
            P(),
        ),
        check_vma=False,
    )
```

```python
import math

import jax
import jax.numpy as jnp
from jax import lax
from jax.experimental import pallas as pl
from jax.experimental.pallas import tpu as pltpu
from jax.sharding import Mesh
from jax.sharding import PartitionSpec as P

D = 1024
H = 16
DH = 64
P_SIZE = 16
K = 4
PTS_BLK = 1024
PB = 32
PIX_BLK = PB * P_SIZE
LANES = 128
TILES = D // LANES
CHUNK = 24
SENT = CHUNK + TILES
STATS = 80
STEPS = 128.0
FULL = 32600.0
i16 = jnp.int16
i32 = jnp.int32
INTERPRET = False

f32 = jnp.float32
bf16 = jnp.bfloat16


def iota(shape, axis):
    return lax.broadcasted_iota(jnp.int32, shape, axis)


def dot(first, second):
    return lax.dot_general(first, second, (((1,), (0,)), ((), ())), preferred_element_type=f32)


def dot_t(first, second):
    return lax.dot_general(first, second, (((1,), (1,)), ((), ())), preferred_element_type=f32)


def split(value, parts):
    pieces = []
    for _ in range(parts):
        piece = value.astype(bf16)
        pieces.append(piece)
        value = value - piece.astype(f32)
    return pieces


def over_vars(value, join):
    shift = value.shape[1] // 2
    while shift >= H:
        value = join(value, pltpu.roll(value, shift, axis=1))
        shift //= 2
    return value


def group(value, v):
    return value[:, v * H : (v + 1) * H]


def scale_code(value):
    most = jnp.max(jnp.abs(value), axis=1, keepdims=True)
    return jnp.floor(jnp.log(jnp.maximum(most, 1e-30)) * STEPS) + 1.0


def two_words(value):
    code = scale_code(value)
    fixed = jnp.round(value * (jnp.exp(code * (-1.0 / STEPS)) * 2.0**30)).astype(i32)
    low = (fixed & 0xFFFF) - 0x8000
    return (fixed >> 16).astype(f32), low.astype(f32), code


def from_words(high, low, code):
    return (high * 65536.0 + (low + 32768.0)) * (jnp.exp(code * (1.0 / STEPS)) * 2.0**-30)


def block_code(value):
    most = jnp.max(jnp.max(jnp.abs(value), axis=2, keepdims=True), axis=1, keepdims=True)
    return jnp.floor(jnp.log(jnp.maximum(most, 1e-30)) * STEPS) + 1.0


def coded(value, code):
    return jnp.round(value * (jnp.exp(code * (-1.0 / STEPS)) * FULL))


def decoded(value, code):
    return value * (jnp.exp(code * (1.0 / STEPS)) * (1.0 / FULL))


def to_words(value):
    return value.astype(i32).astype(i16)


def kernel_call(body, out_shape, mib, scratch=(), in_specs=None, out_specs=None, aliases=None):
    extra = {}
    if in_specs is not None:
        extra["in_specs"] = in_specs
    if out_specs is not None:
        extra["out_specs"] = out_specs
    return pl.pallas_call(
        body,
        out_shape=out_shape,
        scratch_shapes=list(scratch),
        input_output_aliases=aliases or {},
        interpret=INTERPRET,
        compiler_params=pltpu.CompilerParams(vmem_limit_bytes=mib << 20),
        **extra,
    )


def interp_transposed(index_ref, weight_ref, block):
    where = pl.ds(block * PIX_BLK, PIX_BLK)
    index = [index_ref[k : k + 1, where] for k in range(K)]
    weight = [weight_ref[k : k + 1, where] for k in range(K)]
    points = iota((PTS_BLK, PIX_BLK), 0)
    matrix = jnp.zeros((PTS_BLK, PIX_BLK), f32)
    for k in range(K):
        total = jnp.zeros((1, PIX_BLK), f32)
        for j in range(K):
            total = total + jnp.where(index[j] == index[k], weight[j], 0.0)
        matrix = jnp.where(points == index[k], total, matrix)
    return matrix.astype(bf16)


def spread(rows, cols, test):
    return jnp.where(test(iota((rows, cols), 0), iota((rows, cols), 1)), 1.0, 0.0).astype(bf16)


def pixel_masks(var_local):
    wide = var_local * P_SIZE
    copy_rows = spread(wide, var_local, lambda r, c: r // P_SIZE == c)
    own_pixel = iota((wide, PIX_BLK), 0) % P_SIZE == iota((wide, PIX_BLK), 1) % P_SIZE
    return copy_rows, own_pixel


def head_expand(copies):
    return spread(copies * H, D, lambda r, c: r % H == c // DH)


def forward_kernel(
    index_ref, weight_ref, fields_ref, embed_ref, bias_ref, query_ref, x_ref, e_ref, s_ref, exch_ref, code_ref, sum_ref
):
    var_local = fields_ref.shape[0]
    blocks = fields_ref.shape[1] // PTS_BLK
    wide = var_local * P_SIZE
    copy_rows, own_pixel = pixel_masks(var_local)
    gather = spread(PB, PIX_BLK, lambda r, c: r == c // P_SIZE)
    for block in range(blocks):
        matrix = interp_transposed(index_ref, weight_ref, block)
        pixels = dot(fields_ref[:, pl.ds(block * PTS_BLK, PTS_BLK)], matrix).astype(bf16)
        widened = jnp.where(own_pixel, dot(copy_rows, pixels), 0.0).astype(bf16)
        x_ref[pl.ds(block * PB, PB), :] = dot_t(gather, widened).astype(bf16)
    x_all = x_ref[...]
    patches = x_all.shape[0]
    var_of = iota((patches, wide), 1) // P_SIZE
    head_rows = iota((3 * H, D), 0) % H == iota((3 * H, D), 1) // DH
    parts = split(query_ref[...], 3)
    query_rows = jnp.concatenate(
        [jnp.broadcast_to(part.astype(f32), (H, D)) for part in parts], axis=0
    )
    query_rows = jnp.where(head_rows, query_rows, 0.0).astype(bf16)
    scores = []
    for v in range(var_local):
        own = jnp.where(var_of == v, x_all, jnp.zeros_like(x_all))
        embedded = (dot(own, embed_ref[...]) + bias_ref[v : v + 1, :].astype(f32)).astype(bf16)
        e_ref[v] = embedded
        three = dot_t(embedded, query_rows)
        scores.append(three[:, :H] + three[:, H : 2 * H] + three[:, 2 * H :])
    scores = jnp.concatenate(scores, axis=1) * (1.0 / math.sqrt(DH))
    s_ref[...] = scores
    weights = jnp.exp(scores - over_vars(scores, jnp.maximum))
    weights = split(weights / over_vars(weights, jnp.add), 2)
    expand = head_expand(2)
    for v in range(var_local):
        both = jnp.concatenate([group(part, v) for part in weights], axis=1)
        term = dot(both, expand) * e_ref[v].astype(f32)
        if v == 0:
            sum_ref[...] = term
        else:
            sum_ref[...] += term
    groups = exch_ref.shape[0]
    width = D // groups
    codes = []
    for g in range(groups):
        part = sum_ref[:, g * width : (g + 1) * width]
        code = scale_code(part)
        coded = jnp.round(part * (jnp.exp(code * (-1.0 / STEPS)) * FULL))
        exch_ref[g, :patches, :] = coded.astype(i32).astype(i16)
        codes.append(code)
    codes = jnp.concatenate(codes + [jnp.zeros((patches, LANES - groups), f32)], axis=1)
    if patches < LANES:
        codes = jnp.concatenate([codes, jnp.zeros((LANES - patches, LANES), f32)], axis=0)
    code_ref[...] = codes.T[:groups, :]


def target_of(column_ref, row_ref, depth, as_row):
    column = column_ref[...]
    row = row_ref[...]
    count = column.shape[0]
    same = column == row
    first, second = iota((count, count), 0), iota((count, count), 1)
    if as_row:
        rank = jnp.sum(jnp.where(same & (first < second), 1.0, 0.0), axis=0, keepdims=True)
        return row * depth + rank.astype(jnp.int32)
    rank = jnp.sum(jnp.where(same & (second < first), 1.0, 0.0), axis=1, keepdims=True)
    return column * depth + rank.astype(jnp.int32)


def outbox_kernel(grad_ref, out_ref):
    out_ref[...] = grad_ref[...].reshape(out_ref.shape)


def stats_kernel(
    depth,
    column_ref,
    row_ref,
    inbox_ref,
    e_ref,
    s_ref,
    x_ref,
    code_ref,
    old_ref,
    up_ref,
    both_ref,
    xt_ref,
    exch_ref,
    stats_ref,
    sems,
):
    patches = column_ref.shape[0]
    slots = inbox_ref.shape[0] * inbox_ref.shape[1]
    target = target_of(column_ref, row_ref, depth, False)
    pick = jnp.where(iota((patches, slots), 1) == target, 1.0, 0.0).astype(bf16)
    upstream = dot(pick, inbox_ref[...].reshape(slots, D))
    up_ref[...] = upstream.astype(bf16)
    reduce_heads = spread(D, H, lambda r, c: r // DH == c)
    var_local = e_ref.shape[0]
    grad_attn = []
    for v in range(var_local):
        high, low = split(upstream * e_ref[v].astype(f32), 2)
        grad_attn.append(dot(high, reduce_heads) + dot(low, reduce_heads))
    grad_attn = jnp.concatenate(grad_attn, axis=1)
    scores = s_ref[...]
    both_ref[0] = scores
    both_ref[1] = grad_attn
    xt_ref[...] = x_ref[...].astype(f32).T.astype(bf16)
    peak = over_vars(scores, jnp.maximum)
    weights = jnp.exp(scores - peak)
    total = over_vars(weights, jnp.add)
    inner = over_vars(weights * grad_attn, jnp.add) / total
    log_words = two_words(group(peak + jnp.log(total), 0))
    inner_words = two_words(group(inner, 0))
    packed = [*log_words[:2], *inner_words[:2], log_words[2], inner_words[2]]
    packed = jnp.concatenate(packed + [jnp.zeros((patches, LANES - 4 * H - 2), f32)], axis=1)
    if patches < LANES:
        packed = jnp.concatenate([packed, jnp.zeros((LANES - patches, LANES), f32)], axis=0)
    turned = packed.T[:STATS, :]
    row = iota((STATS, LANES), 0)
    copies = []
    for g in range(exch_ref.shape[0]):
        one = jnp.where(row == 4 * H + 2, code_ref[g : g + 1, :], turned)
        stats_ref[g] = one.astype(i32).astype(i16)
        copies.append(
            pltpu.make_async_copy(
                stats_ref.at[g], exch_ref.at[g, pl.ds(patches, STATS)], sems.at[g]
            )
        )
        copies[-1].start()
    for copy in copies:
        copy.wait()


def combine_stats(exch_ref, patches):
    groups = exch_ref.shape[0]
    logs, inners, scales = [], [], []
    for g in range(groups):
        stats = exch_ref[g, patches : patches + STATS, :].astype(i32).astype(f32)
        rows = jnp.concatenate([stats, jnp.zeros((LANES - STATS, LANES), f32)], axis=0).T
        rows = rows[:patches]
        at = 4 * H
        logs.append(from_words(rows[:, :H], rows[:, H : 2 * H], rows[:, at : at + 1]))
        inners.append(
            from_words(rows[:, 2 * H : 3 * H], rows[:, 3 * H : at], rows[:, at + 1 : at + 2])
        )
        scales.append(jnp.exp(rows[:, at + 2 : at + 3] * (1.0 / STEPS)) * (1.0 / FULL))
    peak = logs[0]
    for other in logs[1:]:
        peak = jnp.maximum(peak, other)
    factors = [jnp.exp(one - peak) for one in logs]
    total = sum(factors)
    shares = [factor / total for factor in factors]
    inner = sum(f * t for f, t in zip(shares, inners))
    return peak, total, inner, [share * scale for share, scale in zip(shares, scales)]


def tokens_kernel(depth, slots, place_ref, column_ref, row_ref, exch_ref, out_ref):
    patches = column_ref.shape[0]
    groups, _, width = exch_ref.shape
    _, _, _, shares = combine_stats(exch_ref, patches)
    heads = width // DH
    first = place_ref[0] * heads
    pick = jnp.where(
        iota((3 * H, width), 0) % H == first + iota((3 * H, width), 1) // DH, 1.0, 0.0
    ).astype(bf16)
    mixture = jnp.zeros((patches, width), f32)
    for g in range(groups):
        scale = jnp.concatenate(split(shares[g], 3), axis=1)
        mixture = mixture + dot(scale, pick) * exch_ref[g, :patches, :].astype(i32).astype(f32)
    target = target_of(column_ref, row_ref, depth, True)
    place = jnp.where(iota((slots, patches), 0) == target, 1.0, 0.0).astype(bf16)
    out_ref[...] = dot(place, mixture.astype(bf16))


def code_chunks(weights, bias, extra):
    count = weights.shape[0]
    weight_code, bias_code = block_code(weights), block_code(bias)
    rows = [coded(weights, weight_code), coded(bias, bias_code)]
    rows += [jnp.broadcast_to(code, (count, 1, LANES)) for code in (weight_code, bias_code)]
    return jnp.concatenate(rows + [extra], axis=1)


def merge_kernel(kept_ref, crossed_ref, tokens_ref, going_ref, query_ref, sum_ref):
    ring, rows = kept_ref.shape[0], kept_ref.shape[1]
    share = rows // CHUNK
    sum_ref[...] = (kept_ref[...] + crossed_ref[...]).reshape(sum_ref.shape)
    for t in range(TILES // 2):
        query_ref[t : t + 1, :] = sum_ref[t, P_SIZE + 1 : P_SIZE + 2, :]
    chunks = sum_ref.shape[0]
    tokens = tokens_ref[...].reshape(ring, tokens_ref.shape[0] // ring, LANES)
    token_code = block_code(tokens)
    if share > 1:
        token_rows = jnp.concatenate([token_code] * share, axis=1).reshape(chunks, 1, 1)
    else:
        token_rows = token_code
    extra = jnp.broadcast_to(token_rows, (chunks, CHUNK - P_SIZE - 3, LANES))
    words = code_chunks(sum_ref[:, :P_SIZE, :], sum_ref[:, P_SIZE : P_SIZE + 1, :], extra)
    going_ref[...] = to_words(
        jnp.concatenate([words.reshape(ring, rows, LANES), coded(tokens, token_code)], axis=1)
    )


def own_kernel(coming_ref, query_ref, out_ref, arrived_ref):
    ring, whole = coming_ref.shape[0], coming_ref.shape[1]
    rows = whole - arrived_ref.shape[1]
    share = rows // CHUNK
    words = coming_ref[...].astype(i32).astype(f32)
    arrived_ref[...] = decoded(words[:, rows:, :], words[:, P_SIZE + 3 : P_SIZE + 4, :]).astype(bf16)
    high, low, code = two_words(query_ref[...])
    code = jnp.broadcast_to(code, high.shape)
    for k in range(share):
        at = k * CHUNK
        chunk = words[:, at : at + CHUNK, :]
        weights = decoded(chunk[:, :P_SIZE], chunk[:, P_SIZE + 1 : P_SIZE + 2])
        bias = decoded(chunk[:, P_SIZE : P_SIZE + 1], chunk[:, P_SIZE + 2 : P_SIZE + 3])
        weights, bias = (jnp.sum(part, axis=0, keepdims=True) for part in (weights, bias))
        extra = jnp.concatenate([jnp.zeros((1, LANES), f32), code], axis=0)
        block = code_chunks(weights, bias, extra[None])
        block = jnp.concatenate([block, jnp.concatenate([high, low], axis=0)[None]], axis=1)
        block = to_words(block)
        for r in range(ring):
            out_ref[r, k * SENT : (k + 1) * SENT, :] = block[0]


def final_kernel(core_ref, half_ref, other_ref, weight_ref, bias_ref, query_ref):
    ring, rows = half_ref.shape[0], half_ref.shape[1]
    share = rows // SENT
    low = core_ref[0] == 0
    quarter = TILES // 2
    for c in range(2):
        query = jnp.zeros((quarter, LANES), f32)
        for r in range(ring):
            half, other = (ref[r].astype(i32).astype(f32) for ref in (half_ref, other_ref))
            words = jnp.where(low, half, other) if c == 0 else jnp.where(low, other, half)
            for k in range(share):
                v, t = divmod((c * ring + r) * share + k, TILES)
                cut = slice(t * LANES, (t + 1) * LANES)
                block = words[k * SENT : (k + 1) * SENT]
                weight_ref[v * P_SIZE : (v + 1) * P_SIZE, cut] = decoded(
                    block[:P_SIZE], block[P_SIZE + 1 : P_SIZE + 2]
                )
                bias_ref[v : v + 1, cut] = decoded(
                    block[P_SIZE : P_SIZE + 1], block[P_SIZE + 2 : P_SIZE + 3]
                )
            query = query + from_words(
                words[CHUNK : CHUNK + quarter],
                words[CHUNK + quarter : CHUNK + 2 * quarter],
                words[CHUNK - quarter : CHUNK],
            )
        for t in range(quarter):
            at = (c * quarter + t) * 2
            query_ref[at : at + 1, :] = query[t : t + 1, :DH]
            query_ref[at + 1 : at + 2, :] = query[t : t + 1, DH:]


def backward_kernel(
    core_ref, exch_ref, both_ref, up_ref, xt_ref, embed_ref, bias_ref, query_ref, kept_ref, send_ref, gx_ref, wide_ref
):
    wide, patches = xt_ref.shape
    var_local = wide // P_SIZE
    peak, total, inner, _ = combine_stats(exch_ref, patches)
    peak, inner, inverse = (
        jnp.concatenate([one] * var_local, axis=1) for one in (peak, inner, 1.0 / total)
    )
    attention = jnp.exp(both_ref[0] - peak) * inverse
    grad_score = attention * (both_ref[1] - inner) * (1.0 / math.sqrt(DH))
    attention = split(attention, 2)
    high, low = split(grad_score, 2)
    turned = [part.astype(f32).T.astype(bf16) for part in (high, low)]
    expand = head_expand(2)
    query = query_ref[...]
    q_parts = split(query, 3)
    rows = [q_parts[0], q_parts[1], q_parts[2], q_parts[0], q_parts[1], q_parts[2]]
    query_rows = jnp.concatenate([jnp.broadcast_to(r.astype(f32), (H, D)) for r in rows], axis=0)
    on_head = iota((6 * H, D), 0) % H == iota((6 * H, D), 1) // DH
    query_rows = jnp.where(on_head, query_rows, 0.0).astype(bf16)
    upstream = up_ref[...].astype(f32)
    x_t = xt_ref[...]
    x_all = x_t.astype(f32).T.astype(bf16)
    embed_t = embed_ref[...].astype(f32).T.astype(bf16)
    lane_var = iota((patches, wide), 1) // P_SIZE
    grad_x = jnp.zeros((patches, wide), f32)
    query_sum = jnp.zeros((2 * H, D), f32)
    for v in range(var_local):
        attn = jnp.concatenate([group(part, v) for part in attention], axis=1)
        first, second = group(high, v), group(low, v)
        scored = jnp.concatenate([first, first, first, second, second, second], axis=1)
        grad = dot(attn, expand) * upstream + dot(scored, query_rows)
        low_grad = grad.astype(bf16)
        bias_row = jnp.sum(grad, axis=0, keepdims=True)
        weight_rows = dot(x_t[v * P_SIZE : (v + 1) * P_SIZE, :], low_grad)
        for t in range(TILES):
            cut = slice(t * LANES, (t + 1) * LANES)
            wide_ref[v * TILES + t, :P_SIZE, :] = weight_rows[:, cut]
            wide_ref[v * TILES + t, P_SIZE : P_SIZE + 1, :] = bias_row[:, cut]
        grad_x = jnp.where(lane_var == v, dot(low_grad, embed_t), grad_x)
        pair = jnp.concatenate([part[v * H : (v + 1) * H] for part in turned], axis=0)
        own = jnp.where(lane_var == v, x_all, jnp.zeros_like(x_all))
        embedded = (dot(own, embed_ref[...]) + bias_ref[v : v + 1, :].astype(f32)).astype(bf16)
        query_sum = query_sum + dot(pair, embedded)
    gx_ref[...] = grad_x.astype(bf16)
    diagonal = iota((2 * H, D), 0) % H == iota((2 * H, D), 1) // DH
    query_row = jnp.sum(jnp.where(diagonal, query_sum, 0.0), axis=0, keepdims=True)
    half = wide_ref.shape[0] // 2
    for t in range(TILES):
        at = (t // (TILES // 2)) * half + t % (TILES // 2)
        wide_ref[at, P_SIZE + 1 : P_SIZE + 2, :] = query_row[:, t * LANES : (t + 1) * LANES]
    core = core_ref[0]
    kept_ref[...] = wide_ref[pl.ds(core * half, half)].reshape(kept_ref.shape)
    send_ref[...] = wide_ref[pl.ds((1 - core) * half, half)].reshape(send_ref.shape)


def field_kernel(index_ref, weight_ref, gx_ref, out_ref):
    wide = gx_ref.shape[1]
    var_local = wide // P_SIZE
    blocks = gx_ref.shape[0] // PB
    gx_t = gx_ref[...].astype(f32).T.astype(bf16)
    fold = spread(var_local, wide, lambda r, c: c // P_SIZE == r)
    own_pixel = iota((wide, PIX_BLK), 0) % P_SIZE == iota((wide, PIX_BLK), 1) % P_SIZE
    copy = spread(PB, PIX_BLK, lambda r, c: r == c // P_SIZE)
    for block in range(blocks):
        wide_grad = dot(gx_t[:, block * PB : (block + 1) * PB], copy)
        wide_grad = jnp.where(own_pixel, wide_grad, 0.0).astype(bf16)
        grad = dot(fold, wide_grad).astype(bf16)
        out_ref[:, pl.ds(block * PTS_BLK, PTS_BLK)] = dot_t(
            grad, interp_transposed(index_ref, weight_ref, block)
        )


def local(
    fields, stencil, stencil_weight, owner_map, embed_weight, embed_bias, agg_query, out_grad
):
    by_rows = ("r", "c")
    ring = lax.axis_size("r")
    groups = lax.axis_size("z")
    row_devices = ring * 2
    var_local = fields.shape[0]
    patches = owner_map.shape[0]
    capacity = out_grad.shape[0]
    depth = capacity // row_devices
    width = D // groups
    wide = var_local * P_SIZE
    shape = jax.ShapeDtypeStruct

    inbox = lax.all_to_all(
        kernel_call(outbox_kernel, shape((row_devices, depth, D), bf16), mib=8)(out_grad),
        by_rows,
        split_axis=0,
        concat_axis=0,
        tiled=True,
    )

    index_t = stencil.T
    weight_t = stencil_weight.T
    embed_flat = embed_weight.reshape(wide, D)
    query = agg_query.reshape(1, D)
    row_map = owner_map.reshape(1, patches)
    x_all, embedded, scores, sums, codes = kernel_call(
        forward_kernel,
        (
            shape((patches, wide), bf16),
            shape((var_local, patches, D), bf16),
            shape((patches, var_local * H), f32),
            shape((groups, patches + STATS, width), i16),
            shape((groups, LANES), f32),
        ),
        mib=20,
        scratch=[pltpu.VMEM((patches, D), f32)],
    )(index_t, weight_t, fields, embed_flat, embed_bias, query)

    vmem = pl.BlockSpec(memory_space=pltpu.VMEM)
    anywhere = pl.BlockSpec(memory_space=pl.ANY)
    upstream, both, x_turned, exchange = kernel_call(
        lambda *refs: stats_kernel(depth, *refs),
        (
            shape((patches, D), bf16),
            shape((2, patches, var_local * H), f32),
            shape((wide, patches), bf16),
            shape(sums.shape, i16),
        ),
        mib=12,
        scratch=[pltpu.VMEM((groups, STATS, LANES), i16), pltpu.SemaphoreType.DMA((groups,))],
        in_specs=[vmem] * 7 + [anywhere],
        out_specs=(vmem, vmem, vmem, anywhere),
        aliases={7: 3},
    )(owner_map, row_map, inbox, embedded, scores, x_all, codes, sums)
    exchange = lax.all_to_all(exchange, "z", 0, 0, tiled=True)

    core = lax.axis_index("c").astype(jnp.int32)
    place = lax.axis_index("z").astype(jnp.int32)
    smem = pl.BlockSpec(memory_space=pltpu.SMEM)
    swap = [(0, 1), (1, 0)]
    chunks = var_local * TILES
    rows = chunks // (2 * ring) * CHUNK
    pair = 2 * depth
    kept, sent, grad_x = kernel_call(
        backward_kernel,
        (
            shape((ring, rows, LANES), f32),
            shape((ring, rows, LANES), f32),
            shape((patches, wide), bf16),
        ),
        mib=16,
        scratch=[pltpu.VMEM((chunks, CHUNK, LANES), f32)],
        in_specs=[smem] + [vmem] * 7,
    )(core.reshape(1), exchange, both, upstream, x_turned, embed_flat, embed_bias, query)
    crossed = lax.ppermute(sent, "c", swap)
    outbox = kernel_call(
        lambda *refs: tokens_kernel(depth, capacity, *refs),
        shape((capacity, width), f32),
        mib=8,
        in_specs=[smem] + [vmem] * 3,
    )(place.reshape(1), owner_map, row_map, exchange)
    crossed, outbox = lax.optimization_barrier((crossed, outbox))
    going, query_half = kernel_call(
        merge_kernel,
        (shape((ring, rows + pair, LANES), i16), shape((TILES // 2, LANES), f32)),
        mib=8,
        scratch=[pltpu.VMEM((chunks // 2, CHUNK, LANES), f32)],
    )(kept, crossed, outbox)

    field_grad = kernel_call(field_kernel, shape((var_local, fields.shape[1]), f32), mib=16)(
        index_t, weight_t, grad_x
    )

    coming = lax.all_to_all(going, "r", 0, 0, tiled=True)
    query_half = lax.psum(query_half, "z")
    own, arrived = kernel_call(
        own_kernel,
        (
            shape((ring, rows // CHUNK * SENT, LANES), i16),
            shape((ring, pair, width), bf16),
        ),
        mib=8,
    )(coming, query_half)
    half = lax.all_to_all(own, "r", 0, 0, tiled=True)

    arrived = arrived.reshape(ring, 2, depth, width)
    crossed = lax.ppermute(jnp.where(core == 0, arrived[:, 1], arrived[:, 0]), "c", swap)
    kept = jnp.where(core == 0, arrived[:, 0], arrived[:, 1])
    tokens = jnp.where(
        core == 0, jnp.stack([kept, crossed], axis=1), jnp.stack([crossed, kept], axis=1)
    ).reshape(capacity, width)

    half, tokens, field_grad = lax.optimization_barrier((half, tokens, field_grad))
    other = lax.ppermute(half, "c", swap)
    weight_grad, bias_grad, query_grad = kernel_call(
        final_kernel,
        (shape((wide, D), f32), shape((var_local, D), f32), shape((H, DH), f32)),
        mib=8,
        in_specs=[smem, vmem, vmem],
    )(core.reshape(1), half, other)
    weight_grad = weight_grad.reshape(var_local, P_SIZE, D)
    return (tokens, field_grad, weight_grad, bias_grad, query_grad)


def solution(mesh):
    rows, groups = mesh.shape["rows"], mesh.shape["vars"]
    inner = Mesh(mesh.devices.reshape(rows // 2, 2, groups), ("r", "c", "z"))
    by_rows = ("r", "c")
    return jax.shard_map(
        local,
        mesh=inner,
        in_specs=(
            P("z", by_rows),
            P(by_rows, None),
            P(by_rows, None),
            P(by_rows, None),
            P("z", None, None),
            P("z", None),
            P(),
            P(by_rows, None),
        ),
        out_specs=(
            P(by_rows, "z"),
            P("z", by_rows),
            P("z", None, None),
            P("z", None),
            P(),
        ),
        check_vma=False,
    )
```

```python
import math

import jax
import jax.numpy as jnp
from jax import lax
from jax.experimental import pallas as pl
from jax.experimental.pallas import tpu as pltpu
from jax.sharding import Mesh
from jax.sharding import PartitionSpec as P

D = 1024
H = 16
DH = 64
P_SIZE = 16
K = 4
PTS_BLK = 1024
PB = 32
PIX_BLK = PB * P_SIZE
LANES = 128
TILES = D // LANES
CHUNK = 24
SENT = CHUNK + TILES
STATS = 80
STEPS = 128.0
FULL = 32600.0
i16 = jnp.int16
i32 = jnp.int32
INTERPRET = False

f32 = jnp.float32
bf16 = jnp.bfloat16


def iota(shape, axis):
    return lax.broadcasted_iota(jnp.int32, shape, axis)


def dot(first, second):
    return lax.dot_general(first, second, (((1,), (0,)), ((), ())), preferred_element_type=f32)


def dot_t(first, second):
    return lax.dot_general(first, second, (((1,), (1,)), ((), ())), preferred_element_type=f32)


def split(value, parts):
    pieces = []
    for _ in range(parts):
        piece = value.astype(bf16)
        pieces.append(piece)
        value = value - piece.astype(f32)
    return pieces


def over_vars(value, join):
    shift = value.shape[1] // 2
    while shift >= H:
        value = join(value, pltpu.roll(value, shift, axis=1))
        shift //= 2
    return value


def group(value, v):
    return value[:, v * H : (v + 1) * H]


def scale_code(value):
    most = jnp.max(jnp.abs(value), axis=1, keepdims=True)
    return jnp.floor(jnp.log(jnp.maximum(most, 1e-30)) * STEPS) + 1.0


def two_words(value):
    code = scale_code(value)
    fixed = jnp.round(value * (jnp.exp(code * (-1.0 / STEPS)) * 2.0**30)).astype(i32)
    low = (fixed & 0xFFFF) - 0x8000
    return (fixed >> 16).astype(f32), low.astype(f32), code


def from_words(high, low, code):
    return (high * 65536.0 + (low + 32768.0)) * (jnp.exp(code * (1.0 / STEPS)) * 2.0**-30)


def block_code(value):
    most = jnp.max(jnp.max(jnp.abs(value), axis=2, keepdims=True), axis=1, keepdims=True)
    return jnp.floor(jnp.log(jnp.maximum(most, 1e-30)) * STEPS) + 1.0


def coded(value, code):
    return jnp.round(value * (jnp.exp(code * (-1.0 / STEPS)) * FULL))


def decoded(value, code):
    return value * (jnp.exp(code * (1.0 / STEPS)) * (1.0 / FULL))


def to_words(value):
    return value.astype(i32).astype(i16)


def kernel_call(body, out_shape, mib, scratch=(), in_specs=None, out_specs=None, aliases=None):
    extra = {}
    if in_specs is not None:
        extra["in_specs"] = in_specs
    if out_specs is not None:
        extra["out_specs"] = out_specs
    return pl.pallas_call(
        body,
        out_shape=out_shape,
        scratch_shapes=list(scratch),
        input_output_aliases=aliases or {},
        interpret=INTERPRET,
        compiler_params=pltpu.CompilerParams(vmem_limit_bytes=mib << 20),
        **extra,
    )


def interp_transposed(index_ref, weight_ref, block):
    where = pl.ds(block * PIX_BLK, PIX_BLK)
    index = [index_ref[k : k + 1, where] for k in range(K)]
    weight = [weight_ref[k : k + 1, where] for k in range(K)]
    points = iota((PTS_BLK, PIX_BLK), 0)
    matrix = jnp.zeros((PTS_BLK, PIX_BLK), f32)
    for k in range(K):
        total = jnp.zeros((1, PIX_BLK), f32)
        for j in range(K):
            total = total + jnp.where(index[j] == index[k], weight[j], 0.0)
        matrix = jnp.where(points == index[k], total, matrix)
    return matrix.astype(bf16)


def spread(rows, cols, test):
    return jnp.where(test(iota((rows, cols), 0), iota((rows, cols), 1)), 1.0, 0.0).astype(bf16)


def pixel_masks(var_local):
    wide = var_local * P_SIZE
    copy_rows = spread(wide, var_local, lambda r, c: r // P_SIZE == c)
    own_pixel = iota((wide, PIX_BLK), 0) % P_SIZE == iota((wide, PIX_BLK), 1) % P_SIZE
    return copy_rows, own_pixel


def head_expand(copies):
    return spread(copies * H, D, lambda r, c: r % H == c // DH)


def forward_kernel(
    index_ref, weight_ref, fields_ref, embed_ref, bias_ref, query_ref, e_ref, s_ref, exch_ref, code_ref, sum_ref, x_ref
):
    var_local = fields_ref.shape[0]
    blocks = fields_ref.shape[1] // PTS_BLK
    wide = var_local * P_SIZE
    copy_rows, own_pixel = pixel_masks(var_local)
    gather = spread(PB, PIX_BLK, lambda r, c: r == c // P_SIZE)
    for block in range(blocks):
        matrix = interp_transposed(index_ref, weight_ref, block)
        pixels = dot(fields_ref[:, pl.ds(block * PTS_BLK, PTS_BLK)], matrix).astype(bf16)
        widened = jnp.where(own_pixel, dot(copy_rows, pixels), 0.0).astype(bf16)
        x_ref[pl.ds(block * PB, PB), :] = dot_t(gather, widened).astype(bf16)
    x_all = x_ref[...]
    patches = x_all.shape[0]
    var_of = iota((patches, wide), 1) // P_SIZE
    head_rows = iota((3 * H, D), 0) % H == iota((3 * H, D), 1) // DH
    parts = split(query_ref[...], 3)
    query_rows = jnp.concatenate(
        [jnp.broadcast_to(part.astype(f32), (H, D)) for part in parts], axis=0
    )
    query_rows = jnp.where(head_rows, query_rows, 0.0).astype(bf16)
    scores = []
    for v in range(var_local):
        own = jnp.where(var_of == v, x_all, jnp.zeros_like(x_all))
        embedded = (dot(own, embed_ref[...]) + bias_ref[v : v + 1, :].astype(f32)).astype(bf16)
        e_ref[v] = embedded
        three = dot_t(embedded, query_rows)
        scores.append(three[:, :H] + three[:, H : 2 * H] + three[:, 2 * H :])
    scores = jnp.concatenate(scores, axis=1) * (1.0 / math.sqrt(DH))
    s_ref[0] = scores
    s_ref[1] = x_all.astype(f32)
    weights = jnp.exp(scores - over_vars(scores, jnp.maximum))
    weights = split(weights / over_vars(weights, jnp.add), 2)
    expand = head_expand(2)
    for v in range(var_local):
        both = jnp.concatenate([group(part, v) for part in weights], axis=1)
        term = dot(both, expand) * e_ref[v].astype(f32)
        if v == 0:
            sum_ref[...] = term
        else:
            sum_ref[...] += term
    groups = exch_ref.shape[0]
    width = D // groups
    codes = []
    for g in range(groups):
        part = sum_ref[:, g * width : (g + 1) * width]
        code = scale_code(part)
        coded = jnp.round(part * (jnp.exp(code * (-1.0 / STEPS)) * FULL))
        exch_ref[g, :patches, :] = coded.astype(i32).astype(i16)
        codes.append(code)
    codes = jnp.concatenate(codes + [jnp.zeros((patches, LANES - groups), f32)], axis=1)
    if patches < LANES:
        codes = jnp.concatenate([codes, jnp.zeros((LANES - patches, LANES), f32)], axis=0)
    code_ref[...] = codes.T[:groups, :]


def target_of(column_ref, row_ref, depth, as_row):
    column = column_ref[...]
    row = row_ref[...]
    count = column.shape[0]
    same = column == row
    first, second = iota((count, count), 0), iota((count, count), 1)
    if as_row:
        rank = jnp.sum(jnp.where(same & (first < second), 1.0, 0.0), axis=0, keepdims=True)
        return row * depth + rank.astype(jnp.int32)
    rank = jnp.sum(jnp.where(same & (second < first), 1.0, 0.0), axis=1, keepdims=True)
    return column * depth + rank.astype(jnp.int32)


def outbox_kernel(grad_ref, out_ref):
    out_ref[...] = grad_ref[...].reshape(out_ref.shape)


def stats_kernel(
    depth,
    column_ref,
    row_ref,
    inbox_ref,
    e_ref,
    s_ref,
    code_ref,
    old_ref,
    up_ref,
    both_ref,
    exch_ref,
    stats_ref,
    sems,
):
    patches = column_ref.shape[0]
    slots = inbox_ref.shape[0] * inbox_ref.shape[1]
    target = target_of(column_ref, row_ref, depth, False)
    pick = jnp.where(iota((patches, slots), 1) == target, 1.0, 0.0).astype(bf16)
    upstream = dot(pick, inbox_ref[...].reshape(slots, D))
    up_ref[:, :D] = upstream.astype(bf16)
    up_ref[:, D:] = s_ref[1].astype(bf16)
    reduce_heads = spread(D, H, lambda r, c: r // DH == c)
    var_local = e_ref.shape[0]
    grad_attn = []
    for v in range(var_local):
        high, low = split(upstream * e_ref[v].astype(f32), 2)
        grad_attn.append(dot(high, reduce_heads) + dot(low, reduce_heads))
    grad_attn = jnp.concatenate(grad_attn, axis=1)
    scores = s_ref[0]
    both_ref[0] = scores
    both_ref[1] = grad_attn
    peak = over_vars(scores, jnp.maximum)
    weights = jnp.exp(scores - peak)
    total = over_vars(weights, jnp.add)
    inner = over_vars(weights * grad_attn, jnp.add) / total
    log_words = two_words(group(peak + jnp.log(total), 0))
    inner_words = two_words(group(inner, 0))
    packed = [*log_words[:2], *inner_words[:2], log_words[2], inner_words[2]]
    packed = jnp.concatenate(packed + [jnp.zeros((patches, LANES - 4 * H - 2), f32)], axis=1)
    if patches < LANES:
        packed = jnp.concatenate([packed, jnp.zeros((LANES - patches, LANES), f32)], axis=0)
    turned = packed.T[:STATS, :]
    row = iota((STATS, LANES), 0)
    copies = []
    for g in range(exch_ref.shape[0]):
        one = jnp.where(row == 4 * H + 2, code_ref[g : g + 1, :], turned)
        stats_ref[g] = one.astype(i32).astype(i16)
        copies.append(
            pltpu.make_async_copy(
                stats_ref.at[g], exch_ref.at[g, pl.ds(patches, STATS)], sems.at[g]
            )
        )
        copies[-1].start()
    for copy in copies:
        copy.wait()


def combine_stats(exch_ref, patches):
    groups = exch_ref.shape[0]
    logs, inners, scales = [], [], []
    for g in range(groups):
        stats = exch_ref[g, patches : patches + STATS, :].astype(i32).astype(f32)
        rows = jnp.concatenate([stats, jnp.zeros((LANES - STATS, LANES), f32)], axis=0).T
        rows = rows[:patches]
        at = 4 * H
        logs.append(from_words(rows[:, :H], rows[:, H : 2 * H], rows[:, at : at + 1]))
        inners.append(
            from_words(rows[:, 2 * H : 3 * H], rows[:, 3 * H : at], rows[:, at + 1 : at + 2])
        )
        scales.append(jnp.exp(rows[:, at + 2 : at + 3] * (1.0 / STEPS)) * (1.0 / FULL))
    peak = logs[0]
    for other in logs[1:]:
        peak = jnp.maximum(peak, other)
    factors = [jnp.exp(one - peak) for one in logs]
    total = sum(factors)
    shares = [factor / total for factor in factors]
    inner = sum(f * t for f, t in zip(shares, inners))
    return peak, total, inner, [share * scale for share, scale in zip(shares, scales)]


def tokens_kernel(depth, slots, place_ref, column_ref, row_ref, exch_ref, out_ref):
    patches = column_ref.shape[0]
    groups, _, width = exch_ref.shape
    _, _, _, shares = combine_stats(exch_ref, patches)
    heads = width // DH
    first = place_ref[0] * heads
    pick = jnp.where(
        iota((3 * H, width), 0) % H == first + iota((3 * H, width), 1) // DH, 1.0, 0.0
    ).astype(bf16)
    mixture = jnp.zeros((patches, width), f32)
    for g in range(groups):
        scale = jnp.concatenate(split(shares[g], 3), axis=1)
        mixture = mixture + dot(scale, pick) * exch_ref[g, :patches, :].astype(i32).astype(f32)
    target = target_of(column_ref, row_ref, depth, True)
    place = jnp.where(iota((slots, patches), 0) == target, 1.0, 0.0).astype(bf16)
    out_ref[...] = dot(place, mixture.astype(bf16))


def code_chunks(weights, bias, extra):
    count = weights.shape[0]
    weight_code, bias_code = block_code(weights), block_code(bias)
    rows = [coded(weights, weight_code), coded(bias, bias_code)]
    rows += [jnp.broadcast_to(code, (count, 1, LANES)) for code in (weight_code, bias_code)]
    return jnp.concatenate(rows + [extra], axis=1)


def merge_kernel(kept_ref, crossed_ref, tokens_ref, going_ref, query_ref, sum_ref):
    ring, rows = kept_ref.shape[0], kept_ref.shape[1]
    share = rows // CHUNK
    sum_ref[...] = (kept_ref[...] + crossed_ref[...]).reshape(sum_ref.shape)
    for t in range(TILES // 2):
        query_ref[t : t + 1, :] = sum_ref[t, P_SIZE + 1 : P_SIZE + 2, :]
    chunks = sum_ref.shape[0]
    tokens = tokens_ref[...].reshape(ring, tokens_ref.shape[0] // ring, LANES)
    token_code = block_code(tokens)
    if share > 1:
        token_rows = jnp.concatenate([token_code] * share, axis=1).reshape(chunks, 1, 1)
    else:
        token_rows = token_code
    extra = jnp.broadcast_to(token_rows, (chunks, CHUNK - P_SIZE - 3, LANES))
    words = code_chunks(sum_ref[:, :P_SIZE, :], sum_ref[:, P_SIZE : P_SIZE + 1, :], extra)
    going_ref[...] = to_words(
        jnp.concatenate([words.reshape(ring, rows, LANES), coded(tokens, token_code)], axis=1)
    )


def own_kernel(coming_ref, query_ref, out_ref, arrived_ref):
    ring, whole = coming_ref.shape[0], coming_ref.shape[1]
    rows = whole - arrived_ref.shape[1]
    share = rows // CHUNK
    words = coming_ref[...].astype(i32).astype(f32)
    arrived_ref[...] = decoded(words[:, rows:, :], words[:, P_SIZE + 3 : P_SIZE + 4, :]).astype(bf16)
    high, low, code = two_words(query_ref[...])
    code = jnp.broadcast_to(code, high.shape)
    for k in range(share):
        at = k * CHUNK
        chunk = words[:, at : at + CHUNK, :]
        weights = decoded(chunk[:, :P_SIZE], chunk[:, P_SIZE + 1 : P_SIZE + 2])
        bias = decoded(chunk[:, P_SIZE : P_SIZE + 1], chunk[:, P_SIZE + 2 : P_SIZE + 3])
        weights, bias = (jnp.sum(part, axis=0, keepdims=True) for part in (weights, bias))
        extra = jnp.concatenate([jnp.zeros((1, LANES), f32), code], axis=0)
        block = code_chunks(weights, bias, extra[None])
        block = jnp.concatenate([block, jnp.concatenate([high, low], axis=0)[None]], axis=1)
        block = to_words(block)
        for r in range(ring):
            out_ref[r, k * SENT : (k + 1) * SENT, :] = block[0]


def final_kernel(core_ref, half_ref, other_ref, weight_ref, bias_ref, query_ref):
    ring, rows = half_ref.shape[0], half_ref.shape[1]
    share = rows // SENT
    low = core_ref[0] == 0
    quarter = TILES // 2
    for c in range(2):
        query = jnp.zeros((quarter, LANES), f32)
        for r in range(ring):
            half, other = (ref[r].astype(i32).astype(f32) for ref in (half_ref, other_ref))
            words = jnp.where(low, half, other) if c == 0 else jnp.where(low, other, half)
            for k in range(share):
                v, t = divmod((c * ring + r) * share + k, TILES)
                cut = slice(t * LANES, (t + 1) * LANES)
                block = words[k * SENT : (k + 1) * SENT]
                weight_ref[v * P_SIZE : (v + 1) * P_SIZE, cut] = decoded(
                    block[:P_SIZE], block[P_SIZE + 1 : P_SIZE + 2]
                )
                bias_ref[v : v + 1, cut] = decoded(
                    block[P_SIZE : P_SIZE + 1], block[P_SIZE + 2 : P_SIZE + 3]
                )
            query = query + from_words(
                words[CHUNK : CHUNK + quarter],
                words[CHUNK + quarter : CHUNK + 2 * quarter],
                words[CHUNK - quarter : CHUNK],
            )
        for t in range(quarter):
            at = (c * quarter + t) * 2
            query_ref[at : at + 1, :] = query[t : t + 1, :DH]
            query_ref[at + 1 : at + 2, :] = query[t : t + 1, DH:]


def backward_kernel(
    core_ref, exch_ref, both_ref, up_ref, embed_ref, bias_ref, query_ref, kept_ref, send_ref, gx_ref, wide_ref
):
    patches, wide = up_ref.shape[0], up_ref.shape[1] - D
    var_local = wide // P_SIZE
    peak, total, inner, _ = combine_stats(exch_ref, patches)
    peak, inner, inverse = (
        jnp.concatenate([one] * var_local, axis=1) for one in (peak, inner, 1.0 / total)
    )
    attention = jnp.exp(both_ref[0] - peak) * inverse
    grad_score = attention * (both_ref[1] - inner) * (1.0 / math.sqrt(DH))
    attention = split(attention, 2)
    high, low = split(grad_score, 2)
    turned = [part.astype(f32).T.astype(bf16) for part in (high, low)]
    expand = head_expand(2)
    query = query_ref[...]
    q_parts = split(query, 3)
    rows = [q_parts[0], q_parts[1], q_parts[2], q_parts[0], q_parts[1], q_parts[2]]
    query_rows = jnp.concatenate([jnp.broadcast_to(r.astype(f32), (H, D)) for r in rows], axis=0)
    on_head = iota((6 * H, D), 0) % H == iota((6 * H, D), 1) // DH
    query_rows = jnp.where(on_head, query_rows, 0.0).astype(bf16)
    upstream = up_ref[:, :D].astype(f32)
    x_all = up_ref[:, D:]
    x_t = x_all.astype(f32).T.astype(bf16)
    embed_t = embed_ref[...].astype(f32).T.astype(bf16)
    lane_var = iota((patches, wide), 1) // P_SIZE
    grad_x = jnp.zeros((patches, wide), f32)
    query_sum = jnp.zeros((2 * H, D), f32)
    for v in range(var_local):
        attn = jnp.concatenate([group(part, v) for part in attention], axis=1)
        first, second = group(high, v), group(low, v)
        scored = jnp.concatenate([first, first, first, second, second, second], axis=1)
        grad = dot(attn, expand) * upstream + dot(scored, query_rows)
        low_grad = grad.astype(bf16)
        bias_row = jnp.sum(grad, axis=0, keepdims=True)
        weight_rows = dot(x_t[v * P_SIZE : (v + 1) * P_SIZE, :], low_grad)
        for t in range(TILES):
            cut = slice(t * LANES, (t + 1) * LANES)
            wide_ref[v * TILES + t, :P_SIZE, :] = weight_rows[:, cut]
            wide_ref[v * TILES + t, P_SIZE : P_SIZE + 1, :] = bias_row[:, cut]
        grad_x = jnp.where(lane_var == v, dot(low_grad, embed_t), grad_x)
        pair = jnp.concatenate([part[v * H : (v + 1) * H] for part in turned], axis=0)
        own = jnp.where(lane_var == v, x_all, jnp.zeros_like(x_all))
        embedded = (dot(own, embed_ref[...]) + bias_ref[v : v + 1, :].astype(f32)).astype(bf16)
        query_sum = query_sum + dot(pair, embedded)
    gx_ref[...] = grad_x.astype(bf16)
    diagonal = iota((2 * H, D), 0) % H == iota((2 * H, D), 1) // DH
    query_row = jnp.sum(jnp.where(diagonal, query_sum, 0.0), axis=0, keepdims=True)
    half = wide_ref.shape[0] // 2
    for t in range(TILES):
        at = (t // (TILES // 2)) * half + t % (TILES // 2)
        wide_ref[at, P_SIZE + 1 : P_SIZE + 2, :] = query_row[:, t * LANES : (t + 1) * LANES]
    core = core_ref[0]
    kept_ref[...] = wide_ref[pl.ds(core * half, half)].reshape(kept_ref.shape)
    send_ref[...] = wide_ref[pl.ds((1 - core) * half, half)].reshape(send_ref.shape)


def field_kernel(index_ref, weight_ref, gx_ref, out_ref):
    wide = gx_ref.shape[1]
    var_local = wide // P_SIZE
    blocks = gx_ref.shape[0] // PB
    gx_t = gx_ref[...].astype(f32).T.astype(bf16)
    fold = spread(var_local, wide, lambda r, c: c // P_SIZE == r)
    own_pixel = iota((wide, PIX_BLK), 0) % P_SIZE == iota((wide, PIX_BLK), 1) % P_SIZE
    copy = spread(PB, PIX_BLK, lambda r, c: r == c // P_SIZE)
    for block in range(blocks):
        wide_grad = dot(gx_t[:, block * PB : (block + 1) * PB], copy)
        wide_grad = jnp.where(own_pixel, wide_grad, 0.0).astype(bf16)
        grad = dot(fold, wide_grad).astype(bf16)
        out_ref[:, pl.ds(block * PTS_BLK, PTS_BLK)] = dot_t(
            grad, interp_transposed(index_ref, weight_ref, block)
        )


def local(
    fields, stencil, stencil_weight, owner_map, embed_weight, embed_bias, agg_query, out_grad
):
    by_rows = ("r", "c")
    ring = lax.axis_size("r")
    groups = lax.axis_size("z")
    row_devices = ring * 2
    var_local = fields.shape[0]
    patches = owner_map.shape[0]
    capacity = out_grad.shape[0]
    depth = capacity // row_devices
    width = D // groups
    wide = var_local * P_SIZE
    shape = jax.ShapeDtypeStruct

    inbox = lax.all_to_all(
        kernel_call(outbox_kernel, shape((row_devices, depth, D), bf16), mib=8)(out_grad),
        by_rows,
        split_axis=0,
        concat_axis=0,
        tiled=True,
    )

    index_t = stencil.T
    weight_t = stencil_weight.T
    embed_flat = embed_weight.reshape(wide, D)
    query = agg_query.reshape(1, D)
    row_map = owner_map.reshape(1, patches)
    embedded, scores, sums, codes = kernel_call(
        forward_kernel,
        (
            shape((var_local, patches, D), bf16),
            shape((2, patches, wide), f32),
            shape((groups, patches + STATS, width), i16),
            shape((groups, LANES), f32),
        ),
        mib=20,
        scratch=[pltpu.VMEM((patches, D), f32), pltpu.VMEM((patches, wide), bf16)],
    )(index_t, weight_t, fields, embed_flat, embed_bias, query)

    vmem = pl.BlockSpec(memory_space=pltpu.VMEM)
    anywhere = pl.BlockSpec(memory_space=pl.ANY)
    upstream, both, exchange = kernel_call(
        lambda *refs: stats_kernel(depth, *refs),
        (
            shape((patches, D + wide), bf16),
            shape((2, patches, var_local * H), f32),
            shape(sums.shape, i16),
        ),
        mib=12,
        scratch=[pltpu.VMEM((groups, STATS, LANES), i16), pltpu.SemaphoreType.DMA((groups,))],
        in_specs=[vmem] * 6 + [anywhere],
        out_specs=(vmem, vmem, anywhere),
        aliases={6: 2},
    )(owner_map, row_map, inbox, embedded, scores, codes, sums)
    exchange = lax.all_to_all(exchange, "z", 0, 0, tiled=True)

    core = lax.axis_index("c").astype(jnp.int32)
    place = lax.axis_index("z").astype(jnp.int32)
    smem = pl.BlockSpec(memory_space=pltpu.SMEM)
    swap = [(0, 1), (1, 0)]
    chunks = var_local * TILES
    rows = chunks // (2 * ring) * CHUNK
    pair = 2 * depth
    kept, sent, grad_x = kernel_call(
        backward_kernel,
        (
            shape((ring, rows, LANES), f32),
            shape((ring, rows, LANES), f32),
            shape((patches, wide), bf16),
        ),
        mib=16,
        scratch=[pltpu.VMEM((chunks, CHUNK, LANES), f32)],
        in_specs=[smem] + [vmem] * 6,
    )(core.reshape(1), exchange, both, upstream, embed_flat, embed_bias, query)
    crossed = lax.ppermute(sent, "c", swap)
    outbox = kernel_call(
        lambda *refs: tokens_kernel(depth, capacity, *refs),
        shape((capacity, width), f32),
        mib=8,
        in_specs=[smem] + [vmem] * 3,
    )(place.reshape(1), owner_map, row_map, exchange)
    crossed, outbox = lax.optimization_barrier((crossed, outbox))
    going, query_half = kernel_call(
        merge_kernel,
        (shape((ring, rows + pair, LANES), i16), shape((TILES // 2, LANES), f32)),
        mib=8,
        scratch=[pltpu.VMEM((chunks // 2, CHUNK, LANES), f32)],
    )(kept, crossed, outbox)

    coming = lax.all_to_all(going, "r", 0, 0, tiled=True)
    query_half = lax.psum(query_half, "z")
    own, arrived = kernel_call(
        own_kernel,
        (
            shape((ring, rows // CHUNK * SENT, LANES), i16),
            shape((ring, pair, width), bf16),
        ),
        mib=8,
    )(coming, query_half)
    half = lax.all_to_all(own, "r", 0, 0, tiled=True)

    arrived, grad_x = lax.optimization_barrier((arrived, grad_x))
    field_grad = kernel_call(field_kernel, shape((var_local, fields.shape[1]), f32), mib=16)(
        index_t, weight_t, grad_x
    )

    arrived = arrived.reshape(ring, 2, depth, width)
    crossed = lax.ppermute(jnp.where(core == 0, arrived[:, 1], arrived[:, 0]), "c", swap)
    kept = jnp.where(core == 0, arrived[:, 0], arrived[:, 1])
    tokens = jnp.where(
        core == 0, jnp.stack([kept, crossed], axis=1), jnp.stack([crossed, kept], axis=1)
    ).reshape(capacity, width)

    half, tokens, field_grad = lax.optimization_barrier((half, tokens, field_grad))
    other = lax.ppermute(half, "c", swap)
    weight_grad, bias_grad, query_grad = kernel_call(
        final_kernel,
        (shape((wide, D), f32), shape((var_local, D), f32), shape((H, DH), f32)),
        mib=8,
        in_specs=[smem, vmem, vmem],
    )(core.reshape(1), half, other)
    weight_grad = weight_grad.reshape(var_local, P_SIZE, D)
    return (tokens, field_grad, weight_grad, bias_grad, query_grad)


def solution(mesh):
    rows, groups = mesh.shape["rows"], mesh.shape["vars"]
    inner = Mesh(mesh.devices.reshape(rows // 2, 2, groups), ("r", "c", "z"))
    by_rows = ("r", "c")
    return jax.shard_map(
        local,
        mesh=inner,
        in_specs=(
            P("z", by_rows),
            P(by_rows, None),
            P(by_rows, None),
            P(by_rows, None),
            P("z", None, None),
            P("z", None),
            P(),
            P(by_rows, None),
        ),
        out_specs=(
            P(by_rows, "z"),
            P("z", by_rows),
            P("z", None, None),
            P("z", None),
            P(),
        ),
        check_vma=False,
    )
```

```python
import math

import jax
import jax.numpy as jnp
from jax import lax
from jax.experimental import pallas as pl
from jax.experimental.pallas import tpu as pltpu
from jax.sharding import Mesh
from jax.sharding import PartitionSpec as P


D = 1024
H = 16
DH = 64
P_SIZE = 16
K = 4
PTS_BLK = 1024
PB = 32
PIX_BLK = PB * P_SIZE
LANES = 128
TILES = D // LANES
CHUNK = 24
SENT = CHUNK + TILES
STATS = 80
STEPS = 128.0
FULL = 32600.0
i16 = jnp.int16
i32 = jnp.int32
INTERPRET = False

f32 = jnp.float32
bf16 = jnp.bfloat16


def iota(shape, axis):
    return lax.broadcasted_iota(jnp.int32, shape, axis)


def dot(first, second):
    return lax.dot_general(first, second, (((1,), (0,)), ((), ())), preferred_element_type=f32)


def dot_t(first, second):
    return lax.dot_general(first, second, (((1,), (1,)), ((), ())), preferred_element_type=f32)


def split(value, parts):
    pieces = []
    for _ in range(parts):
        piece = value.astype(bf16)
        pieces.append(piece)
        value = value - piece.astype(f32)
    return pieces


def over_vars(value, join):
    shift = value.shape[1] // 2
    while shift >= H:
        value = join(value, pltpu.roll(value, shift, axis=1))
        shift //= 2
    return value


def group(value, v):
    return value[:, v * H : (v + 1) * H]


def scale_code(value):
    most = jnp.max(jnp.abs(value), axis=1, keepdims=True)
    return jnp.floor(jnp.log(jnp.maximum(most, 1e-30)) * STEPS) + 1.0


def two_words(value):
    code = scale_code(value)
    fixed = jnp.round(value * (jnp.exp(code * (-1.0 / STEPS)) * 2.0**30)).astype(i32)
    low = (fixed & 0xFFFF) - 0x8000
    return (fixed >> 16).astype(f32), low.astype(f32), code


def from_words(high, low, code):
    return (high * 65536.0 + (low + 32768.0)) * (jnp.exp(code * (1.0 / STEPS)) * 2.0**-30)


def block_code(value):
    most = jnp.max(jnp.max(jnp.abs(value), axis=2, keepdims=True), axis=1, keepdims=True)
    return jnp.floor(jnp.log(jnp.maximum(most, 1e-30)) * STEPS) + 1.0


def coded(value, code):
    return jnp.round(value * (jnp.exp(code * (-1.0 / STEPS)) * FULL))


def decoded(value, code):
    return value * (jnp.exp(code * (1.0 / STEPS)) * (1.0 / FULL))


def to_words(value):
    return value.astype(i32).astype(i16)


def kernel_call(body, out_shape, mib, scratch=(), in_specs=None, out_specs=None, aliases=None):
    extra = {}
    if in_specs is not None:
        extra["in_specs"] = in_specs
    if out_specs is not None:
        extra["out_specs"] = out_specs
    return pl.pallas_call(
        body,
        out_shape=out_shape,
        scratch_shapes=list(scratch),
        input_output_aliases=aliases or {},
        interpret=INTERPRET,
        compiler_params=pltpu.CompilerParams(vmem_limit_bytes=mib << 20),
        **extra,
    )


def interp_transposed(index_ref, weight_ref, block):
    where = pl.ds(block * PIX_BLK, PIX_BLK)
    index = [index_ref[k : k + 1, where] for k in range(K)]
    weight = [weight_ref[k : k + 1, where] for k in range(K)]
    points = iota((PTS_BLK, PIX_BLK), 0)
    matrix = jnp.zeros((PTS_BLK, PIX_BLK), f32)
    for k in range(K):
        total = jnp.zeros((1, PIX_BLK), f32)
        for j in range(K):
            total = total + jnp.where(index[j] == index[k], weight[j], 0.0)
        matrix = jnp.where(points == index[k], total, matrix)
    return matrix.astype(bf16)


def spread(rows, cols, test):
    return jnp.where(test(iota((rows, cols), 0), iota((rows, cols), 1)), 1.0, 0.0).astype(bf16)


def pixel_masks(var_local):
    wide = var_local * P_SIZE
    copy_rows = spread(wide, var_local, lambda r, c: r // P_SIZE == c)
    own_pixel = iota((wide, PIX_BLK), 0) % P_SIZE == iota((wide, PIX_BLK), 1) % P_SIZE
    return copy_rows, own_pixel


def head_expand(copies):
    return spread(copies * H, D, lambda r, c: r % H == c // DH)


def forward_kernel(
    index_ref, weight_ref, fields_ref, embed_ref, bias_ref, query_ref, e_ref, s_ref, exch_ref, code_ref, sum_ref, x_ref
):
    var_local = fields_ref.shape[0]
    blocks = fields_ref.shape[1] // PTS_BLK
    wide = var_local * P_SIZE
    copy_rows, own_pixel = pixel_masks(var_local)
    gather = spread(PB, PIX_BLK, lambda r, c: r == c // P_SIZE)
    for block in range(blocks):
        matrix = interp_transposed(index_ref, weight_ref, block)
        pixels = dot(fields_ref[:, pl.ds(block * PTS_BLK, PTS_BLK)], matrix).astype(bf16)
        widened = jnp.where(own_pixel, dot(copy_rows, pixels), 0.0).astype(bf16)
        x_ref[pl.ds(block * PB, PB), :] = dot_t(gather, widened).astype(bf16)
    x_all = x_ref[...]
    patches = x_all.shape[0]
    var_of = iota((patches, wide), 1) // P_SIZE
    head_rows = iota((3 * H, D), 0) % H == iota((3 * H, D), 1) // DH
    parts = split(query_ref[...], 3)
    query_rows = jnp.concatenate(
        [jnp.broadcast_to(part.astype(f32), (H, D)) for part in parts], axis=0
    )
    query_rows = jnp.where(head_rows, query_rows, 0.0).astype(bf16)
    scores = []
    for v in range(var_local):
        own = jnp.where(var_of == v, x_all, jnp.zeros_like(x_all))
        embedded = (dot(own, embed_ref[...]) + bias_ref[v : v + 1, :].astype(f32)).astype(bf16)
        e_ref[v] = embedded
        three = dot_t(embedded, query_rows)
        scores.append(three[:, :H] + three[:, H : 2 * H] + three[:, 2 * H :])
    scores = jnp.concatenate(scores, axis=1) * (1.0 / math.sqrt(DH))
    s_ref[0] = scores
    s_ref[1] = x_all.astype(f32)
    weights = jnp.exp(scores - over_vars(scores, jnp.maximum))
    weights = split(weights / over_vars(weights, jnp.add), 2)
    expand = head_expand(2)
    for v in range(var_local):
        both = jnp.concatenate([group(part, v) for part in weights], axis=1)
        term = dot(both, expand) * e_ref[v].astype(f32)
        if v == 0:
            sum_ref[...] = term
        else:
            sum_ref[...] += term
    groups = exch_ref.shape[0]
    width = D // groups
    codes = []
    for g in range(groups):
        part = sum_ref[:, g * width : (g + 1) * width]
        code = scale_code(part)
        coded = jnp.round(part * (jnp.exp(code * (-1.0 / STEPS)) * FULL))
        exch_ref[g, :patches, :] = coded.astype(i32).astype(i16)
        codes.append(code)
    codes = jnp.concatenate(codes + [jnp.zeros((patches, LANES - groups), f32)], axis=1)
    if patches < LANES:
        codes = jnp.concatenate([codes, jnp.zeros((LANES - patches, LANES), f32)], axis=0)
    code_ref[...] = codes.T[:groups, :]


def target_of(column_ref, row_ref, depth, as_row):
    column = column_ref[...]
    row = row_ref[...]
    count = column.shape[0]
    same = column == row
    first, second = iota((count, count), 0), iota((count, count), 1)
    if as_row:
        rank = jnp.sum(jnp.where(same & (first < second), 1.0, 0.0), axis=0, keepdims=True)
        return row * depth + rank.astype(jnp.int32)
    rank = jnp.sum(jnp.where(same & (second < first), 1.0, 0.0), axis=1, keepdims=True)
    return column * depth + rank.astype(jnp.int32)


def outbox_kernel(grad_ref, out_ref):
    out_ref[...] = grad_ref[...].reshape(out_ref.shape)


def stats_kernel(
    depth,
    column_ref,
    row_ref,
    inbox_ref,
    e_ref,
    s_ref,
    code_ref,
    old_ref,
    up_ref,
    both_ref,
    exch_ref,
    stats_ref,
    sems,
):
    patches = column_ref.shape[0]
    slots = inbox_ref.shape[0] * inbox_ref.shape[1]
    target = target_of(column_ref, row_ref, depth, False)
    pick = jnp.where(iota((patches, slots), 1) == target, 1.0, 0.0).astype(bf16)
    upstream = dot(pick, inbox_ref[...].reshape(slots, D))
    up_ref[:, :D] = upstream.astype(bf16)
    up_ref[:, D:] = s_ref[1].astype(bf16)
    reduce_heads = spread(D, H, lambda r, c: r // DH == c)
    var_local = e_ref.shape[0]
    grad_attn = []
    for v in range(var_local):
        high, low = split(upstream * e_ref[v].astype(f32), 2)
        grad_attn.append(dot(high, reduce_heads) + dot(low, reduce_heads))
    grad_attn = jnp.concatenate(grad_attn, axis=1)
    scores = s_ref[0]
    both_ref[0] = scores
    both_ref[1] = grad_attn
    peak = over_vars(scores, jnp.maximum)
    weights = jnp.exp(scores - peak)
    total = over_vars(weights, jnp.add)
    inner = over_vars(weights * grad_attn, jnp.add) / total
    log_words = two_words(group(peak + jnp.log(total), 0))
    inner_words = two_words(group(inner, 0))
    packed = [*log_words[:2], *inner_words[:2], log_words[2], inner_words[2]]
    packed = jnp.concatenate(packed + [jnp.zeros((patches, LANES - 4 * H - 2), f32)], axis=1)
    if patches < LANES:
        packed = jnp.concatenate([packed, jnp.zeros((LANES - patches, LANES), f32)], axis=0)
    turned = packed.T[:STATS, :]
    row = iota((STATS, LANES), 0)
    copies = []
    for g in range(exch_ref.shape[0]):
        one = jnp.where(row == 4 * H + 2, code_ref[g : g + 1, :], turned)
        stats_ref[g] = one.astype(i32).astype(i16)
        copies.append(
            pltpu.make_async_copy(
                stats_ref.at[g], exch_ref.at[g, pl.ds(patches, STATS)], sems.at[g]
            )
        )
        copies[-1].start()
    for copy in copies:
        copy.wait()


def combine_stats(exch_ref, patches):
    groups = exch_ref.shape[0]
    logs, inners, scales = [], [], []
    for g in range(groups):
        stats = exch_ref[g, patches : patches + STATS, :].astype(i32).astype(f32)
        rows = jnp.concatenate([stats, jnp.zeros((LANES - STATS, LANES), f32)], axis=0).T
        rows = rows[:patches]
        at = 4 * H
        logs.append(from_words(rows[:, :H], rows[:, H : 2 * H], rows[:, at : at + 1]))
        inners.append(
            from_words(rows[:, 2 * H : 3 * H], rows[:, 3 * H : at], rows[:, at + 1 : at + 2])
        )
        scales.append(jnp.exp(rows[:, at + 2 : at + 3] * (1.0 / STEPS)) * (1.0 / FULL))
    peak = logs[0]
    for other in logs[1:]:
        peak = jnp.maximum(peak, other)
    factors = [jnp.exp(one - peak) for one in logs]
    total = sum(factors)
    shares = [factor / total for factor in factors]
    inner = sum(f * t for f, t in zip(shares, inners))
    return peak, total, inner, [share * scale for share, scale in zip(shares, scales)]


def tokens_kernel(depth, slots, place_ref, column_ref, row_ref, exch_ref, out_ref):
    patches = column_ref.shape[0]
    groups, _, width = exch_ref.shape
    _, _, _, shares = combine_stats(exch_ref, patches)
    heads = width // DH
    first = place_ref[0] * heads
    pick = jnp.where(
        iota((3 * H, width), 0) % H == first + iota((3 * H, width), 1) // DH, 1.0, 0.0
    ).astype(bf16)
    mixture = jnp.zeros((patches, width), f32)
    for g in range(groups):
        scale = jnp.concatenate(split(shares[g], 3), axis=1)
        mixture = mixture + dot(scale, pick) * exch_ref[g, :patches, :].astype(i32).astype(f32)
    target = target_of(column_ref, row_ref, depth, True)
    place = jnp.where(iota((slots, patches), 0) == target, 1.0, 0.0).astype(bf16)
    out_ref[...] = dot(place, mixture.astype(bf16))


def code_chunks(weights, bias, extra):
    count = weights.shape[0]
    weight_code, bias_code = block_code(weights), block_code(bias)
    rows = [coded(weights, weight_code), coded(bias, bias_code)]
    rows += [jnp.broadcast_to(code, (count, 1, LANES)) for code in (weight_code, bias_code)]
    return jnp.concatenate(rows + [extra], axis=1)


def merge_kernel(kept_ref, crossed_ref, tokens_ref, going_ref, query_ref, sum_ref):
    ring, rows = kept_ref.shape[0], kept_ref.shape[1]
    share = rows // CHUNK
    sum_ref[...] = (kept_ref[...] + crossed_ref[...]).reshape(sum_ref.shape)
    for t in range(TILES // 2):
        query_ref[t : t + 1, :] = sum_ref[t, P_SIZE + 1 : P_SIZE + 2, :]
    chunks = sum_ref.shape[0]
    tokens = tokens_ref[...].reshape(ring, tokens_ref.shape[0] // ring, LANES)
    token_code = block_code(tokens)
    if share > 1:
        token_rows = jnp.concatenate([token_code] * share, axis=1).reshape(chunks, 1, 1)
    else:
        token_rows = token_code
    extra = jnp.broadcast_to(token_rows, (chunks, CHUNK - P_SIZE - 3, LANES))
    words = code_chunks(sum_ref[:, :P_SIZE, :], sum_ref[:, P_SIZE : P_SIZE + 1, :], extra)
    going_ref[...] = to_words(
        jnp.concatenate([words.reshape(ring, rows, LANES), coded(tokens, token_code)], axis=1)
    )


def own_kernel(coming_ref, query_ref, out_ref, arrived_ref):
    ring, whole = coming_ref.shape[0], coming_ref.shape[1]
    rows = whole - arrived_ref.shape[1]
    share = rows // CHUNK
    words = coming_ref[...].astype(i32).astype(f32)
    arrived_ref[...] = decoded(words[:, rows:, :], words[:, P_SIZE + 3 : P_SIZE + 4, :]).astype(bf16)
    high, low, code = two_words(query_ref[...])
    code = jnp.broadcast_to(code, high.shape)
    for k in range(share):
        at = k * CHUNK
        chunk = words[:, at : at + CHUNK, :]
        weights = decoded(chunk[:, :P_SIZE], chunk[:, P_SIZE + 1 : P_SIZE + 2])
        bias = decoded(chunk[:, P_SIZE : P_SIZE + 1], chunk[:, P_SIZE + 2 : P_SIZE + 3])
        weights, bias = (jnp.sum(part, axis=0, keepdims=True) for part in (weights, bias))
        extra = jnp.concatenate([jnp.zeros((1, LANES), f32), code], axis=0)
        block = code_chunks(weights, bias, extra[None])
        block = jnp.concatenate([block, jnp.concatenate([high, low], axis=0)[None]], axis=1)
        block = to_words(block)
        for r in range(ring):
            out_ref[r, k * SENT : (k + 1) * SENT, :] = block[0]


def final_kernel(core_ref, half_ref, other_ref, weight_ref, bias_ref, query_ref):
    ring, rows = half_ref.shape[0], half_ref.shape[1]
    share = rows // SENT
    low = core_ref[0] == 0
    quarter = TILES // 2
    for c in range(2):
        query = jnp.zeros((quarter, LANES), f32)
        for r in range(ring):
            half, other = (ref[r].astype(i32).astype(f32) for ref in (half_ref, other_ref))
            words = jnp.where(low, half, other) if c == 0 else jnp.where(low, other, half)
            for k in range(share):
                v, t = divmod((c * ring + r) * share + k, TILES)
                cut = slice(t * LANES, (t + 1) * LANES)
                block = words[k * SENT : (k + 1) * SENT]
                weight_ref[v * P_SIZE : (v + 1) * P_SIZE, cut] = decoded(
                    block[:P_SIZE], block[P_SIZE + 1 : P_SIZE + 2]
                )
                bias_ref[v : v + 1, cut] = decoded(
                    block[P_SIZE : P_SIZE + 1], block[P_SIZE + 2 : P_SIZE + 3]
                )
            query = query + from_words(
                words[CHUNK : CHUNK + quarter],
                words[CHUNK + quarter : CHUNK + 2 * quarter],
                words[CHUNK - quarter : CHUNK],
            )
        for t in range(quarter):
            at = (c * quarter + t) * 2
            query_ref[at : at + 1, :] = query[t : t + 1, :DH]
            query_ref[at + 1 : at + 2, :] = query[t : t + 1, DH:]


def backward_kernel(
    core_ref, exch_ref, both_ref, up_ref, embed_ref, bias_ref, query_ref, kept_ref, send_ref, gx_ref, wide_ref
):
    patches, wide = up_ref.shape[0], up_ref.shape[1] - D
    var_local = wide // P_SIZE
    peak, total, inner, _ = combine_stats(exch_ref, patches)
    peak, inner, inverse = (
        jnp.concatenate([one] * var_local, axis=1) for one in (peak, inner, 1.0 / total)
    )
    attention = jnp.exp(both_ref[0] - peak) * inverse
    grad_score = attention * (both_ref[1] - inner) * (1.0 / math.sqrt(DH))
    attention = split(attention, 2)
    high, low = split(grad_score, 2)
    turned = [part.astype(f32).T.astype(bf16) for part in (high, low)]
    expand = head_expand(2)
    query = query_ref[...]
    q_parts = split(query, 3)
    rows = [q_parts[0], q_parts[1], q_parts[2], q_parts[0], q_parts[1], q_parts[2]]
    query_rows = jnp.concatenate([jnp.broadcast_to(r.astype(f32), (H, D)) for r in rows], axis=0)
    on_head = iota((6 * H, D), 0) % H == iota((6 * H, D), 1) // DH
    query_rows = jnp.where(on_head, query_rows, 0.0).astype(bf16)
    upstream = up_ref[:, :D].astype(f32)
    x_all = up_ref[:, D:]
    x_t = x_all.astype(f32).T.astype(bf16)
    embed_t = embed_ref[...].astype(f32).T.astype(bf16)
    lane_var = iota((patches, wide), 1) // P_SIZE
    grad_x = jnp.zeros((patches, wide), f32)
    query_sum = jnp.zeros((2 * H, D), f32)
    for v in range(var_local):
        attn = jnp.concatenate([group(part, v) for part in attention], axis=1)
        first, second = group(high, v), group(low, v)
        scored = jnp.concatenate([first, first, first, second, second, second], axis=1)
        grad = dot(attn, expand) * upstream + dot(scored, query_rows)
        low_grad = grad.astype(bf16)
        bias_row = jnp.sum(grad, axis=0, keepdims=True)
        weight_rows = dot(x_t[v * P_SIZE : (v + 1) * P_SIZE, :], low_grad)
        for t in range(TILES):
            cut = slice(t * LANES, (t + 1) * LANES)
            wide_ref[v * TILES + t, :P_SIZE, :] = weight_rows[:, cut]
            wide_ref[v * TILES + t, P_SIZE : P_SIZE + 1, :] = bias_row[:, cut]
        grad_x = jnp.where(lane_var == v, dot(low_grad, embed_t), grad_x)
        pair = jnp.concatenate([part[v * H : (v + 1) * H] for part in turned], axis=0)
        own = jnp.where(lane_var == v, x_all, jnp.zeros_like(x_all))
        embedded = (dot(own, embed_ref[...]) + bias_ref[v : v + 1, :].astype(f32)).astype(bf16)
        query_sum = query_sum + dot(pair, embedded)
    gx_ref[...] = grad_x.astype(bf16)
    diagonal = iota((2 * H, D), 0) % H == iota((2 * H, D), 1) // DH
    query_row = jnp.sum(jnp.where(diagonal, query_sum, 0.0), axis=0, keepdims=True)
    half = wide_ref.shape[0] // 2
    for t in range(TILES):
        at = (t // (TILES // 2)) * half + t % (TILES // 2)
        wide_ref[at, P_SIZE + 1 : P_SIZE + 2, :] = query_row[:, t * LANES : (t + 1) * LANES]
    core = core_ref[0]
    kept_ref[...] = wide_ref[pl.ds(core * half, half)].reshape(kept_ref.shape)
    send_ref[...] = wide_ref[pl.ds((1 - core) * half, half)].reshape(send_ref.shape)


def field_kernel(index_ref, weight_ref, gx_ref, out_ref):
    wide = gx_ref.shape[1]
    var_local = wide // P_SIZE
    blocks = gx_ref.shape[0] // PB
    gx_t = gx_ref[...].astype(f32).T.astype(bf16)
    fold = spread(var_local, wide, lambda r, c: c // P_SIZE == r)
    own_pixel = iota((wide, PIX_BLK), 0) % P_SIZE == iota((wide, PIX_BLK), 1) % P_SIZE
    copy = spread(PB, PIX_BLK, lambda r, c: r == c // P_SIZE)
    for block in range(blocks):
        wide_grad = dot(gx_t[:, block * PB : (block + 1) * PB], copy)
        wide_grad = jnp.where(own_pixel, wide_grad, 0.0).astype(bf16)
        grad = dot(fold, wide_grad).astype(bf16)
        out_ref[:, pl.ds(block * PTS_BLK, PTS_BLK)] = dot_t(
            grad, interp_transposed(index_ref, weight_ref, block)
        )


def local(
    fields, stencil, stencil_weight, owner_map, embed_weight, embed_bias, agg_query, out_grad
):
    by_rows = ("r", "c")
    ring = lax.axis_size("r")
    by_vars = ("z1", "z2")
    groups = lax.axis_size(by_vars)
    row_devices = ring * 2
    var_local = fields.shape[0]
    patches = owner_map.shape[0]
    capacity = out_grad.shape[0]
    depth = capacity // row_devices
    width = D // groups
    wide = var_local * P_SIZE
    shape = jax.ShapeDtypeStruct

    inbox = lax.all_to_all(
        kernel_call(outbox_kernel, shape((row_devices, depth, D), bf16), mib=8)(out_grad),
        by_rows,
        split_axis=0,
        concat_axis=0,
        tiled=True,
    )

    index_t = stencil.T
    weight_t = stencil_weight.T
    embed_flat = embed_weight.reshape(wide, D)
    query = agg_query.reshape(1, D)
    row_map = owner_map.reshape(1, patches)
    embedded, scores, sums, codes = kernel_call(
        forward_kernel,
        (
            shape((var_local, patches, D), bf16),
            shape((2, patches, wide), f32),
            shape((groups, patches + STATS, width), i16),
            shape((groups, LANES), f32),
        ),
        mib=20,
        scratch=[pltpu.VMEM((patches, D), f32), pltpu.VMEM((patches, wide), bf16)],
    )(index_t, weight_t, fields, embed_flat, embed_bias, query)

    vmem = pl.BlockSpec(memory_space=pltpu.VMEM)
    anywhere = pl.BlockSpec(memory_space=pl.ANY)
    upstream, both, exchange = kernel_call(
        lambda *refs: stats_kernel(depth, *refs),
        (
            shape((patches, D + wide), bf16),
            shape((2, patches, var_local * H), f32),
            shape(sums.shape, i16),
        ),
        mib=12,
        scratch=[pltpu.VMEM((groups, STATS, LANES), i16), pltpu.SemaphoreType.DMA((groups,))],
        in_specs=[vmem] * 6 + [anywhere],
        out_specs=(vmem, vmem, anywhere),
        aliases={6: 2},
    )(owner_map, row_map, inbox, embedded, scores, codes, sums)
    exchange = lax.all_to_all(exchange, by_vars, 0, 0, tiled=True)

    core = lax.axis_index("c").astype(jnp.int32)
    place = lax.axis_index(by_vars).astype(jnp.int32)
    smem = pl.BlockSpec(memory_space=pltpu.SMEM)
    swap = [(0, 1), (1, 0)]
    chunks = var_local * TILES
    rows = chunks // (2 * ring) * CHUNK
    pair = 2 * depth
    kept, sent, grad_x = kernel_call(
        backward_kernel,
        (
            shape((ring, rows, LANES), f32),
            shape((ring, rows, LANES), f32),
            shape((patches, wide), bf16),
        ),
        mib=16,
        scratch=[pltpu.VMEM((chunks, CHUNK, LANES), f32)],
        in_specs=[smem] + [vmem] * 6,
    )(core.reshape(1), exchange, both, upstream, embed_flat, embed_bias, query)
    crossed = lax.ppermute(sent, "c", swap)
    outbox = kernel_call(
        lambda *refs: tokens_kernel(depth, capacity, *refs),
        shape((capacity, width), f32),
        mib=8,
        in_specs=[smem] + [vmem] * 3,
    )(place.reshape(1), owner_map, row_map, exchange)
    crossed, outbox = lax.optimization_barrier((crossed, outbox))
    going, query_half = kernel_call(
        merge_kernel,
        (shape((ring, rows + pair, LANES), i16), shape((TILES // 2, LANES), f32)),
        mib=8,
        scratch=[pltpu.VMEM((chunks // 2, CHUNK, LANES), f32)],
    )(kept, crossed, outbox)

    query_far = lax.ppermute(query_half, "z1", swap)
    coming = lax.all_to_all(going, "r", 0, 0, tiled=True)
    query_half = lax.psum(query_half + query_far, "z2")
    own, arrived = kernel_call(
        own_kernel,
        (
            shape((ring, rows // CHUNK * SENT, LANES), i16),
            shape((ring, pair, width), bf16),
        ),
        mib=8,
    )(coming, query_half)
    half = lax.all_to_all(own, "r", 0, 0, tiled=True)

    arrived, grad_x = lax.optimization_barrier((arrived, grad_x))
    field_grad = kernel_call(field_kernel, shape((var_local, fields.shape[1]), f32), mib=16)(
        index_t, weight_t, grad_x
    )

    arrived = arrived.reshape(ring, 2, depth, width)
    crossed = lax.ppermute(jnp.where(core == 0, arrived[:, 1], arrived[:, 0]), "c", swap)
    kept = jnp.where(core == 0, arrived[:, 0], arrived[:, 1])
    tokens = jnp.where(
        core == 0, jnp.stack([kept, crossed], axis=1), jnp.stack([crossed, kept], axis=1)
    ).reshape(capacity, width)

    half, tokens, field_grad = lax.optimization_barrier((half, tokens, field_grad))
    other = lax.ppermute(half, "c", swap)
    weight_grad, bias_grad, query_grad = kernel_call(
        final_kernel,
        (shape((wide, D), f32), shape((var_local, D), f32), shape((H, DH), f32)),
        mib=8,
        in_specs=[smem, vmem, vmem],
    )(core.reshape(1), half, other)
    weight_grad = weight_grad.reshape(var_local, P_SIZE, D)
    return (tokens, field_grad, weight_grad, bias_grad, query_grad)


def solution(mesh):
    rows, groups = mesh.shape["rows"], mesh.shape["vars"]
    inner = Mesh(mesh.devices.reshape(rows // 2, 2, 2, groups // 2), ("r", "c", "z1", "z2"))
    by_vars = ("z1", "z2")
    by_rows = ("r", "c")
    return jax.shard_map(
        local,
        mesh=inner,
        in_specs=(
            P(by_vars, by_rows),
            P(by_rows, None),
            P(by_rows, None),
            P(by_rows, None),
            P(by_vars, None, None),
            P(by_vars, None),
            P(),
            P(by_rows, None),
        ),
        out_specs=(
            P(by_rows, by_vars),
            P(by_vars, by_rows),
            P(by_vars, None, None),
            P(by_vars, None),
            P(),
        ),
        check_vma=False,
    )
```

```python
import math

import jax
import jax.numpy as jnp
from jax import lax
from jax.experimental import pallas as pl
from jax.experimental.pallas import tpu as pltpu
from jax.sharding import Mesh
from jax.sharding import PartitionSpec as P


D = 1024
H = 16
DH = 64
P_SIZE = 16
K = 4
PTS_BLK = 1024
PB = 32
PIX_BLK = PB * P_SIZE
LANES = 128
TILES = D // LANES
CHUNK = 24
SENT = CHUNK + TILES
STATS = 80
STEPS = 128.0
FULL = 32600.0
i16 = jnp.int16
i32 = jnp.int32
INTERPRET = False

f32 = jnp.float32
bf16 = jnp.bfloat16


def iota(shape, axis):
    return lax.broadcasted_iota(jnp.int32, shape, axis)


def dot(first, second):
    return lax.dot_general(first, second, (((1,), (0,)), ((), ())), preferred_element_type=f32)


def dot_t(first, second):
    return lax.dot_general(first, second, (((1,), (1,)), ((), ())), preferred_element_type=f32)


def split(value, parts):
    pieces = []
    for _ in range(parts):
        piece = value.astype(bf16)
        pieces.append(piece)
        value = value - piece.astype(f32)
    return pieces


def over_vars(value, join):
    shift = value.shape[1] // 2
    while shift >= H:
        value = join(value, pltpu.roll(value, shift, axis=1))
        shift //= 2
    return value


def group(value, v):
    return value[:, v * H : (v + 1) * H]


def scale_code(value):
    most = jnp.max(jnp.abs(value), axis=1, keepdims=True)
    return jnp.floor(jnp.log(jnp.maximum(most, 1e-30)) * STEPS) + 1.0


def two_words(value):
    code = scale_code(value)
    fixed = jnp.round(value * (jnp.exp(code * (-1.0 / STEPS)) * 2.0**30)).astype(i32)
    low = (fixed & 0xFFFF) - 0x8000
    return (fixed >> 16).astype(f32), low.astype(f32), code


def from_words(high, low, code):
    return (high * 65536.0 + (low + 32768.0)) * (jnp.exp(code * (1.0 / STEPS)) * 2.0**-30)


def block_code(value):
    most = jnp.max(jnp.max(jnp.abs(value), axis=2, keepdims=True), axis=1, keepdims=True)
    return jnp.floor(jnp.log(jnp.maximum(most, 1e-30)) * STEPS) + 1.0


def coded(value, code):
    return jnp.round(value * (jnp.exp(code * (-1.0 / STEPS)) * FULL))


def decoded(value, code):
    return value * (jnp.exp(code * (1.0 / STEPS)) * (1.0 / FULL))


def to_words(value):
    return value.astype(i32).astype(i16)


def kernel_call(body, out_shape, mib, scratch=(), in_specs=None, out_specs=None, aliases=None):
    extra = {}
    if in_specs is not None:
        extra["in_specs"] = in_specs
    if out_specs is not None:
        extra["out_specs"] = out_specs
    return pl.pallas_call(
        body,
        out_shape=out_shape,
        scratch_shapes=list(scratch),
        input_output_aliases=aliases or {},
        interpret=INTERPRET,
        compiler_params=pltpu.CompilerParams(vmem_limit_bytes=mib << 20),
        **extra,
    )


def interp_transposed(index_ref, weight_ref, block):
    where = pl.ds(block * PIX_BLK, PIX_BLK)
    index = [index_ref[k : k + 1, where] for k in range(K)]
    weight = [weight_ref[k : k + 1, where] for k in range(K)]
    points = iota((PTS_BLK, PIX_BLK), 0)
    matrix = jnp.zeros((PTS_BLK, PIX_BLK), f32)
    for k in range(K):
        total = jnp.zeros((1, PIX_BLK), f32)
        for j in range(K):
            total = total + jnp.where(index[j] == index[k], weight[j], 0.0)
        matrix = jnp.where(points == index[k], total, matrix)
    return matrix.astype(bf16)


def spread(rows, cols, test):
    return jnp.where(test(iota((rows, cols), 0), iota((rows, cols), 1)), 1.0, 0.0).astype(bf16)


def pixel_masks(var_local):
    wide = var_local * P_SIZE
    copy_rows = spread(wide, var_local, lambda r, c: r // P_SIZE == c)
    own_pixel = iota((wide, PIX_BLK), 0) % P_SIZE == iota((wide, PIX_BLK), 1) % P_SIZE
    return copy_rows, own_pixel


def head_expand(copies):
    return spread(copies * H, D, lambda r, c: r % H == c // DH)


def forward_kernel(
    index_ref, weight_ref, fields_ref, embed_ref, bias_ref, query_ref, e_ref, s_ref, exch_ref, code_ref, sum_ref, x_ref
):
    var_local = fields_ref.shape[0]
    blocks = fields_ref.shape[1] // PTS_BLK
    wide = var_local * P_SIZE
    copy_rows, own_pixel = pixel_masks(var_local)
    gather = spread(PB, PIX_BLK, lambda r, c: r == c // P_SIZE)
    for block in range(blocks):
        matrix = interp_transposed(index_ref, weight_ref, block)
        pixels = dot(fields_ref[:, pl.ds(block * PTS_BLK, PTS_BLK)], matrix).astype(bf16)
        widened = jnp.where(own_pixel, dot(copy_rows, pixels), 0.0).astype(bf16)
        x_ref[pl.ds(block * PB, PB), :] = dot_t(gather, widened).astype(bf16)
    x_all = x_ref[...]
    patches = x_all.shape[0]
    var_of = iota((patches, wide), 1) // P_SIZE
    head_rows = iota((3 * H, D), 0) % H == iota((3 * H, D), 1) // DH
    parts = split(query_ref[...], 3)
    query_rows = jnp.concatenate(
        [jnp.broadcast_to(part.astype(f32), (H, D)) for part in parts], axis=0
    )
    query_rows = jnp.where(head_rows, query_rows, 0.0).astype(bf16)
    scores = []
    for v in range(var_local):
        own = jnp.where(var_of == v, x_all, jnp.zeros_like(x_all))
        embedded = (dot(own, embed_ref[...]) + bias_ref[v : v + 1, :].astype(f32)).astype(bf16)
        e_ref[v] = embedded
        three = dot_t(embedded, query_rows)
        scores.append(three[:, :H] + three[:, H : 2 * H] + three[:, 2 * H :])
    scores = jnp.concatenate(scores, axis=1) * (1.0 / math.sqrt(DH))
    s_ref[0] = scores
    s_ref[1] = x_all.astype(f32)
    weights = jnp.exp(scores - over_vars(scores, jnp.maximum))
    weights = split(weights / over_vars(weights, jnp.add), 2)
    expand = head_expand(2)
    for v in range(var_local):
        both = jnp.concatenate([group(part, v) for part in weights], axis=1)
        term = dot(both, expand) * e_ref[v].astype(f32)
        if v == 0:
            sum_ref[...] = term
        else:
            sum_ref[...] += term
    groups = exch_ref.shape[0]
    width = D // groups
    codes = []
    for g in range(groups):
        part = sum_ref[:, g * width : (g + 1) * width]
        code = scale_code(part)
        coded = jnp.round(part * (jnp.exp(code * (-1.0 / STEPS)) * FULL))
        exch_ref[g, :patches, :] = coded.astype(i32).astype(i16)
        codes.append(code)
    codes = jnp.concatenate(codes + [jnp.zeros((patches, LANES - groups), f32)], axis=1)
    if patches < LANES:
        codes = jnp.concatenate([codes, jnp.zeros((LANES - patches, LANES), f32)], axis=0)
    code_ref[...] = codes.T[:groups, :]


def target_of(column_ref, row_ref, depth, as_row):
    column = column_ref[...]
    row = row_ref[...]
    count = column.shape[0]
    same = column == row
    first, second = iota((count, count), 0), iota((count, count), 1)
    if as_row:
        rank = jnp.sum(jnp.where(same & (first < second), 1.0, 0.0), axis=0, keepdims=True)
        return row * depth + rank.astype(jnp.int32)
    rank = jnp.sum(jnp.where(same & (second < first), 1.0, 0.0), axis=1, keepdims=True)
    return column * depth + rank.astype(jnp.int32)


def outbox_kernel(grad_ref, out_ref):
    out_ref[...] = grad_ref[...].reshape(out_ref.shape)


def outbox_call(row_devices, depth):
    steps = 4
    places = row_devices // steps
    return pl.pallas_call(
        outbox_kernel,
        out_shape=jax.ShapeDtypeStruct((row_devices, depth, D), bf16),
        grid=(steps,),
        in_specs=[pl.BlockSpec((places * depth, D), lambda i: (i, 0))],
        out_specs=pl.BlockSpec((places, depth, D), lambda i: (i, 0, 0)),
        interpret=INTERPRET,
        compiler_params=pltpu.CompilerParams(vmem_limit_bytes=4 << 20),
    )


def stats_kernel(
    depth,
    column_ref,
    row_ref,
    inbox_ref,
    e_ref,
    s_ref,
    code_ref,
    old_ref,
    up_ref,
    both_ref,
    exch_ref,
    stats_ref,
    sems,
):
    patches = column_ref.shape[0]
    slots = inbox_ref.shape[0] * inbox_ref.shape[1]
    target = target_of(column_ref, row_ref, depth, False)
    pick = jnp.where(iota((patches, slots), 1) == target, 1.0, 0.0).astype(bf16)
    upstream = dot(pick, inbox_ref[...].reshape(slots, D))
    up_ref[:, :D] = upstream.astype(bf16)
    up_ref[:, D:] = s_ref[1].astype(bf16)
    reduce_heads = spread(D, H, lambda r, c: r // DH == c)
    var_local = e_ref.shape[0]
    grad_attn = []
    for v in range(var_local):
        high, low = split(upstream * e_ref[v].astype(f32), 2)
        grad_attn.append(dot(high, reduce_heads) + dot(low, reduce_heads))
    grad_attn = jnp.concatenate(grad_attn, axis=1)
    scores = s_ref[0]
    both_ref[0] = scores
    both_ref[1] = grad_attn
    peak = over_vars(scores, jnp.maximum)
    weights = jnp.exp(scores - peak)
    total = over_vars(weights, jnp.add)
    inner = over_vars(weights * grad_attn, jnp.add) / total
    log_words = two_words(group(peak + jnp.log(total), 0))
    inner_words = two_words(group(inner, 0))
    packed = [*log_words[:2], *inner_words[:2], log_words[2], inner_words[2]]
    packed = jnp.concatenate(packed + [jnp.zeros((patches, LANES - 4 * H - 2), f32)], axis=1)
    if patches < LANES:
        packed = jnp.concatenate([packed, jnp.zeros((LANES - patches, LANES), f32)], axis=0)
    turned = packed.T[:STATS, :]
    row = iota((STATS, LANES), 0)
    copies = []
    for g in range(exch_ref.shape[0]):
        one = jnp.where(row == 4 * H + 2, code_ref[g : g + 1, :], turned)
        stats_ref[g] = one.astype(i32).astype(i16)
        copies.append(
            pltpu.make_async_copy(
                stats_ref.at[g], exch_ref.at[g, pl.ds(patches, STATS)], sems.at[g]
            )
        )
        copies[-1].start()
    for copy in copies:
        copy.wait()


def combine_stats(exch_ref, patches):
    groups = exch_ref.shape[0]
    logs, inners, scales = [], [], []
    for g in range(groups):
        stats = exch_ref[g, patches : patches + STATS, :].astype(i32).astype(f32)
        rows = jnp.concatenate([stats, jnp.zeros((LANES - STATS, LANES), f32)], axis=0).T
        rows = rows[:patches]
        at = 4 * H
        logs.append(from_words(rows[:, :H], rows[:, H : 2 * H], rows[:, at : at + 1]))
        inners.append(
            from_words(rows[:, 2 * H : 3 * H], rows[:, 3 * H : at], rows[:, at + 1 : at + 2])
        )
        scales.append(jnp.exp(rows[:, at + 2 : at + 3] * (1.0 / STEPS)) * (1.0 / FULL))
    peak = logs[0]
    for other in logs[1:]:
        peak = jnp.maximum(peak, other)
    factors = [jnp.exp(one - peak) for one in logs]
    total = sum(factors)
    shares = [factor / total for factor in factors]
    inner = sum(f * t for f, t in zip(shares, inners))
    return peak, total, inner, [share * scale for share, scale in zip(shares, scales)]


def tokens_kernel(depth, slots, place_ref, column_ref, row_ref, exch_ref, out_ref):
    patches = column_ref.shape[0]
    groups, _, width = exch_ref.shape
    _, _, _, shares = combine_stats(exch_ref, patches)
    heads = width // DH
    first = place_ref[0] * heads
    pick = jnp.where(
        iota((3 * H, width), 0) % H == first + iota((3 * H, width), 1) // DH, 1.0, 0.0
    ).astype(bf16)
    mixture = jnp.zeros((patches, width), f32)
    for g in range(groups):
        scale = jnp.concatenate(split(shares[g], 3), axis=1)
        mixture = mixture + dot(scale, pick) * exch_ref[g, :patches, :].astype(i32).astype(f32)
    target = target_of(column_ref, row_ref, depth, True)
    place = jnp.where(iota((slots, patches), 0) == target, 1.0, 0.0).astype(bf16)
    out_ref[...] = dot(place, mixture.astype(bf16))


def code_chunks(weights, bias, extra):
    count = weights.shape[0]
    weight_code, bias_code = block_code(weights), block_code(bias)
    rows = [coded(weights, weight_code), coded(bias, bias_code)]
    rows += [jnp.broadcast_to(code, (count, 1, LANES)) for code in (weight_code, bias_code)]
    return jnp.concatenate(rows + [extra], axis=1)


def merge_kernel(kept_ref, crossed_ref, tokens_ref, going_ref, query_ref, sum_ref):
    ring, rows = kept_ref.shape[0], kept_ref.shape[1]
    share = rows // CHUNK
    sum_ref[...] = (kept_ref[...] + crossed_ref[...]).reshape(sum_ref.shape)
    for t in range(TILES // 2):
        query_ref[t : t + 1, :] = sum_ref[t, P_SIZE + 1 : P_SIZE + 2, :]
    chunks = sum_ref.shape[0]
    tokens = tokens_ref[...].reshape(ring, tokens_ref.shape[0] // ring, LANES)
    token_code = block_code(tokens)
    if share > 1:
        token_rows = jnp.concatenate([token_code] * share, axis=1).reshape(chunks, 1, 1)
    else:
        token_rows = token_code
    extra = jnp.broadcast_to(token_rows, (chunks, CHUNK - P_SIZE - 3, LANES))
    words = code_chunks(sum_ref[:, :P_SIZE, :], sum_ref[:, P_SIZE : P_SIZE + 1, :], extra)
    going_ref[...] = to_words(
        jnp.concatenate([words.reshape(ring, rows, LANES), coded(tokens, token_code)], axis=1)
    )


def own_kernel(coming_ref, query_ref, out_ref, arrived_ref):
    ring, whole = coming_ref.shape[0], coming_ref.shape[1]
    rows = whole - arrived_ref.shape[1]
    share = rows // CHUNK
    words = coming_ref[...].astype(i32).astype(f32)
    arrived_ref[...] = decoded(words[:, rows:, :], words[:, P_SIZE + 3 : P_SIZE + 4, :]).astype(bf16)
    high, low, code = two_words(query_ref[...])
    code = jnp.broadcast_to(code, high.shape)
    for k in range(share):
        at = k * CHUNK
        chunk = words[:, at : at + CHUNK, :]
        weights = decoded(chunk[:, :P_SIZE], chunk[:, P_SIZE + 1 : P_SIZE + 2])
        bias = decoded(chunk[:, P_SIZE : P_SIZE + 1], chunk[:, P_SIZE + 2 : P_SIZE + 3])
        weights, bias = (jnp.sum(part, axis=0, keepdims=True) for part in (weights, bias))
        extra = jnp.concatenate([jnp.zeros((1, LANES), f32), code], axis=0)
        block = code_chunks(weights, bias, extra[None])
        block = jnp.concatenate([block, jnp.concatenate([high, low], axis=0)[None]], axis=1)
        block = to_words(block)
        for r in range(ring):
            out_ref[r, k * SENT : (k + 1) * SENT, :] = block[0]


def final_kernel(core_ref, half_ref, other_ref, weight_ref, bias_ref, query_ref):
    ring, rows = half_ref.shape[0], half_ref.shape[1]
    share = rows // SENT
    low = core_ref[0] == 0
    quarter = TILES // 2
    for c in range(2):
        query = jnp.zeros((quarter, LANES), f32)
        for r in range(ring):
            half, other = (ref[r].astype(i32).astype(f32) for ref in (half_ref, other_ref))
            words = jnp.where(low, half, other) if c == 0 else jnp.where(low, other, half)
            for k in range(share):
                v, t = divmod((c * ring + r) * share + k, TILES)
                cut = slice(t * LANES, (t + 1) * LANES)
                block = words[k * SENT : (k + 1) * SENT]
                weight_ref[v * P_SIZE : (v + 1) * P_SIZE, cut] = decoded(
                    block[:P_SIZE], block[P_SIZE + 1 : P_SIZE + 2]
                )
                bias_ref[v : v + 1, cut] = decoded(
                    block[P_SIZE : P_SIZE + 1], block[P_SIZE + 2 : P_SIZE + 3]
                )
            query = query + from_words(
                words[CHUNK : CHUNK + quarter],
                words[CHUNK + quarter : CHUNK + 2 * quarter],
                words[CHUNK - quarter : CHUNK],
            )
        for t in range(quarter):
            at = (c * quarter + t) * 2
            query_ref[at : at + 1, :] = query[t : t + 1, :DH]
            query_ref[at + 1 : at + 2, :] = query[t : t + 1, DH:]


def backward_kernel(
    core_ref, exch_ref, both_ref, up_ref, embed_ref, bias_ref, query_ref, kept_ref, send_ref, gx_ref, wide_ref
):
    patches, wide = up_ref.shape[0], up_ref.shape[1] - D
    var_local = wide // P_SIZE
    peak, total, inner, _ = combine_stats(exch_ref, patches)
    peak, inner, inverse = (
        jnp.concatenate([one] * var_local, axis=1) for one in (peak, inner, 1.0 / total)
    )
    attention = jnp.exp(both_ref[0] - peak) * inverse
    grad_score = attention * (both_ref[1] - inner) * (1.0 / math.sqrt(DH))
    attention = split(attention, 2)
    high, low = split(grad_score, 2)
    turned = [part.astype(f32).T.astype(bf16) for part in (high, low)]
    expand = head_expand(2)
    query = query_ref[...]
    q_parts = split(query, 3)
    rows = [q_parts[0], q_parts[1], q_parts[2], q_parts[0], q_parts[1], q_parts[2]]
    query_rows = jnp.concatenate([jnp.broadcast_to(r.astype(f32), (H, D)) for r in rows], axis=0)
    on_head = iota((6 * H, D), 0) % H == iota((6 * H, D), 1) // DH
    query_rows = jnp.where(on_head, query_rows, 0.0).astype(bf16)
    upstream = up_ref[:, :D].astype(f32)
    x_all = up_ref[:, D:]
    x_t = x_all.astype(f32).T.astype(bf16)
    embed_t = embed_ref[...].astype(f32).T.astype(bf16)
    lane_var = iota((patches, wide), 1) // P_SIZE
    grad_x = jnp.zeros((patches, wide), f32)
    query_sum = jnp.zeros((2 * H, D), f32)
    for v in range(var_local):
        attn = jnp.concatenate([group(part, v) for part in attention], axis=1)
        first, second = group(high, v), group(low, v)
        scored = jnp.concatenate([first, first, first, second, second, second], axis=1)
        grad = dot(attn, expand) * upstream + dot(scored, query_rows)
        low_grad = grad.astype(bf16)
        bias_row = jnp.sum(grad, axis=0, keepdims=True)
        weight_rows = dot(x_t[v * P_SIZE : (v + 1) * P_SIZE, :], low_grad)
        for t in range(TILES):
            cut = slice(t * LANES, (t + 1) * LANES)
            wide_ref[v * TILES + t, :P_SIZE, :] = weight_rows[:, cut]
            wide_ref[v * TILES + t, P_SIZE : P_SIZE + 1, :] = bias_row[:, cut]
        grad_x = jnp.where(lane_var == v, dot(low_grad, embed_t), grad_x)
        pair = jnp.concatenate([part[v * H : (v + 1) * H] for part in turned], axis=0)
        own = jnp.where(lane_var == v, x_all, jnp.zeros_like(x_all))
        embedded = (dot(own, embed_ref[...]) + bias_ref[v : v + 1, :].astype(f32)).astype(bf16)
        query_sum = query_sum + dot(pair, embedded)
    gx_ref[...] = grad_x.astype(bf16)
    diagonal = iota((2 * H, D), 0) % H == iota((2 * H, D), 1) // DH
    query_row = jnp.sum(jnp.where(diagonal, query_sum, 0.0), axis=0, keepdims=True)
    half = wide_ref.shape[0] // 2
    for t in range(TILES):
        at = (t // (TILES // 2)) * half + t % (TILES // 2)
        wide_ref[at, P_SIZE + 1 : P_SIZE + 2, :] = query_row[:, t * LANES : (t + 1) * LANES]
    core = core_ref[0]
    kept_ref[...] = wide_ref[pl.ds(core * half, half)].reshape(kept_ref.shape)
    send_ref[...] = wide_ref[pl.ds((1 - core) * half, half)].reshape(send_ref.shape)


def field_kernel(index_ref, weight_ref, gx_ref, out_ref):
    wide = gx_ref.shape[1]
    var_local = wide // P_SIZE
    blocks = gx_ref.shape[0] // PB
    gx_t = gx_ref[...].astype(f32).T.astype(bf16)
    fold = spread(var_local, wide, lambda r, c: c // P_SIZE == r)
    own_pixel = iota((wide, PIX_BLK), 0) % P_SIZE == iota((wide, PIX_BLK), 1) % P_SIZE
    copy = spread(PB, PIX_BLK, lambda r, c: r == c // P_SIZE)
    for block in range(blocks):
        wide_grad = dot(gx_t[:, block * PB : (block + 1) * PB], copy)
        wide_grad = jnp.where(own_pixel, wide_grad, 0.0).astype(bf16)
        grad = dot(fold, wide_grad).astype(bf16)
        out_ref[:, pl.ds(block * PTS_BLK, PTS_BLK)] = dot_t(
            grad, interp_transposed(index_ref, weight_ref, block)
        )


def local(
    fields, stencil, stencil_weight, owner_map, embed_weight, embed_bias, agg_query, out_grad
):
    by_rows = ("r", "c")
    ring = lax.axis_size("r")
    by_vars = ("z1", "z2")
    groups = lax.axis_size(by_vars)
    row_devices = ring * 2
    var_local = fields.shape[0]
    patches = owner_map.shape[0]
    capacity = out_grad.shape[0]
    depth = capacity // row_devices
    width = D // groups
    wide = var_local * P_SIZE
    shape = jax.ShapeDtypeStruct

    inbox = lax.all_to_all(
        outbox_call(row_devices, depth)(out_grad),
        by_rows,
        split_axis=0,
        concat_axis=0,
        tiled=True,
    )

    index_t = stencil.T
    weight_t = stencil_weight.T
    embed_flat = embed_weight.reshape(wide, D)
    query = agg_query.reshape(1, D)
    row_map = owner_map.reshape(1, patches)
    embedded, scores, sums, codes = kernel_call(
        forward_kernel,
        (
            shape((var_local, patches, D), bf16),
            shape((2, patches, wide), f32),
            shape((groups, patches + STATS, width), i16),
            shape((groups, LANES), f32),
        ),
        mib=20,
        scratch=[pltpu.VMEM((patches, D), f32), pltpu.VMEM((patches, wide), bf16)],
    )(index_t, weight_t, fields, embed_flat, embed_bias, query)

    vmem = pl.BlockSpec(memory_space=pltpu.VMEM)
    anywhere = pl.BlockSpec(memory_space=pl.ANY)
    upstream, both, exchange = kernel_call(
        lambda *refs: stats_kernel(depth, *refs),
        (
            shape((patches, D + wide), bf16),
            shape((2, patches, var_local * H), f32),
            shape(sums.shape, i16),
        ),
        mib=12,
        scratch=[pltpu.VMEM((groups, STATS, LANES), i16), pltpu.SemaphoreType.DMA((groups,))],
        in_specs=[vmem] * 6 + [anywhere],
        out_specs=(vmem, vmem, anywhere),
        aliases={6: 2},
    )(owner_map, row_map, inbox, embedded, scores, codes, sums)
    exchange = lax.all_to_all(exchange, by_vars, 0, 0, tiled=True)

    core = lax.axis_index("c").astype(jnp.int32)
    place = lax.axis_index(by_vars).astype(jnp.int32)
    smem = pl.BlockSpec(memory_space=pltpu.SMEM)
    swap = [(0, 1), (1, 0)]
    chunks = var_local * TILES
    rows = chunks // (2 * ring) * CHUNK
    pair = 2 * depth
    kept, sent, grad_x = kernel_call(
        backward_kernel,
        (
            shape((ring, rows, LANES), f32),
            shape((ring, rows, LANES), f32),
            shape((patches, wide), bf16),
        ),
        mib=16,
        scratch=[pltpu.VMEM((chunks, CHUNK, LANES), f32)],
        in_specs=[smem] + [vmem] * 6,
    )(core.reshape(1), exchange, both, upstream, embed_flat, embed_bias, query)
    crossed = lax.ppermute(sent, "c", swap)
    outbox = kernel_call(
        lambda *refs: tokens_kernel(depth, capacity, *refs),
        shape((capacity, width), f32),
        mib=8,
        in_specs=[smem] + [vmem] * 3,
    )(place.reshape(1), owner_map, row_map, exchange)
    crossed, outbox = lax.optimization_barrier((crossed, outbox))
    going, query_half = kernel_call(
        merge_kernel,
        (shape((ring, rows + pair, LANES), i16), shape((TILES // 2, LANES), f32)),
        mib=8,
        scratch=[pltpu.VMEM((chunks // 2, CHUNK, LANES), f32)],
    )(kept, crossed, outbox)

    query_far = lax.ppermute(query_half, "z1", swap)
    coming = lax.all_to_all(going, "r", 0, 0, tiled=True)
    query_half = lax.psum(query_half + query_far, "z2")
    own, arrived = kernel_call(
        own_kernel,
        (
            shape((ring, rows // CHUNK * SENT, LANES), i16),
            shape((ring, pair, width), bf16),
        ),
        mib=8,
    )(coming, query_half)
    half = lax.all_to_all(own, "r", 0, 0, tiled=True)

    arrived, grad_x = lax.optimization_barrier((arrived, grad_x))
    field_grad = kernel_call(field_kernel, shape((var_local, fields.shape[1]), f32), mib=16)(
        index_t, weight_t, grad_x
    )

    arrived = arrived.reshape(ring, 2, depth, width)
    crossed = lax.ppermute(jnp.where(core == 0, arrived[:, 1], arrived[:, 0]), "c", swap)
    kept = jnp.where(core == 0, arrived[:, 0], arrived[:, 1])
    tokens = jnp.where(
        core == 0, jnp.stack([kept, crossed], axis=1), jnp.stack([crossed, kept], axis=1)
    ).reshape(capacity, width)

    half, tokens, field_grad = lax.optimization_barrier((half, tokens, field_grad))
    other = lax.ppermute(half, "c", swap)
    weight_grad, bias_grad, query_grad = kernel_call(
        final_kernel,
        (shape((wide, D), f32), shape((var_local, D), f32), shape((H, DH), f32)),
        mib=8,
        in_specs=[smem, vmem, vmem],
    )(core.reshape(1), half, other)
    weight_grad = weight_grad.reshape(var_local, P_SIZE, D)
    return (tokens, field_grad, weight_grad, bias_grad, query_grad)


def solution(mesh):
    rows, groups = mesh.shape["rows"], mesh.shape["vars"]
    inner = Mesh(mesh.devices.reshape(rows // 2, 2, 2, groups // 2), ("r", "c", "z1", "z2"))
    by_vars = ("z1", "z2")
    by_rows = ("r", "c")
    return jax.shard_map(
        local,
        mesh=inner,
        in_specs=(
            P(by_vars, by_rows),
            P(by_rows, None),
            P(by_rows, None),
            P(by_rows, None),
            P(by_vars, None, None),
            P(by_vars, None),
            P(),
            P(by_rows, None),
        ),
        out_specs=(
            P(by_rows, by_vars),
            P(by_vars, by_rows),
            P(by_vars, None, None),
            P(by_vars, None),
            P(),
        ),
        check_vma=False,
    )
```
